32 devices in a mesh: res: 8 (over y, x, core), hid: 4 (over z).
Axes of the slice: x: 2, y: 2, z: 4, core: 2. Of those that a mesh axis runs over, the one named last changes fastest.
Arguments:
- node_state: bfloat16 [1024, 512], P('res', 'hid'), may hold values from -6 to 6
- edge_state: bfloat16 [1024, 64, 192], P('res', 'hid'), may hold values from -6 to 6
- node_gain: float32 [512], replicated, may hold values from 0.25 to 1.75
- edge_gain: float32 [192], replicated, may hold values from 0.25 to 1.75
- ffn_gain: float32 [512], replicated, may hold values from 0.25 to 1.75
- w_self: bfloat16 [512, 2048], P(None, 'hid'), may hold values from -0.15625 to 0.15625
- w_neigh: bfloat16 [512, 2048], P(None, 'hid'), may hold values from -0.15625 to 0.15625
- w_edge: bfloat16 [192, 2048], P(None, 'hid'), may hold values from -0.15625 to 0.15625
- w_message: bfloat16 [2048, 512], P('hid'), may hold values from -0.375 to 0.375
- w_update: bfloat16 [2048, 192], P('hid'), may hold values from -0.125 to 0.125
- w_expand: bfloat16 [512, 2048], P(None, 'hid'), may hold values from -0.25 to 0.25
- w_contract: bfloat16 [2048, 512], P('hid'), may hold values from -0.1875 to 0.1875
- neighbours: int32 [1024, 64], P('res'), may hold values from 0 to 639, as said below
- requests: int32 [8, 8, 64], P('res'), may hold values from 0 to 127, as said below
- counts: int32 [1024], P('res'), may hold values from 30 to 60
- node_cotangent: bfloat16 [1024, 512], P('res', 'hid'), may hold values from -6 to 6
- edge_cotangent: bfloat16 [1024, 64, 192], P('res', 'hid'), may hold values from -6 to 6
Outputs:
- next_node: bfloat16 [1024, 512], P('res', 'hid')
- next_edge: bfloat16 [1024, 64, 192], P('res', 'hid')
- grad_node_state: float32 [1024, 512], P('res', 'hid')
- grad_edge_state: float32 [1024, 64, 192], P('res', 'hid')
- grad_node_gain: float32 [512], P('res')
- grad_edge_gain: float32 [192], P('res')
- grad_ffn_gain: float32 [512], P('res')
- grad_w_self: float32 [512, 2048], P('res', 'hid')
- grad_w_neigh: float32 [512, 2048], P('res', 'hid')
- grad_w_edge: float32 [192, 2048], P('res', 'hid')
- grad_w_message: float32 [2048, 512], P('hid', 'res')
- grad_w_update: float32 [2048, 192], P('hid', 'res')
- grad_w_expand: float32 [512, 2048], P('res', 'hid')
- grad_w_contract: float32 [2048, 512], P('hid', 'res')
The draws below stay inside these ranges and needn't reach their ends.
Inputs may be any that keep to these rules, and one draw needn't show every extreme that they name: `neighbours`: entry v of a residue in block p names row v of block p if v < 128, else row requests[p, q, c] of block q with q = (v - 128) // 64 and c = (v - 128) % 64; the share of such entries varies from residue to residue. requests[p, q] holds 64 distinct rows of block q.
All inputs are finite; a program needn't handle non-finite values.
Results may differ from the reference program's by a relative error of at most 0.028.
Values may be sent and summed in bfloat16 or wider, within the bound.
A program may use at most 128 MiB of HBM per device.

```python
import jax
import jax.numpy as jnp
from jax import lax

D = 512
C = 192
MH = 2048
FF = 2048
K = 64
NB_MOST = 60
NB_LEAST = 30
RES_DEV = 128
RESIDUES = 1024
CAP = 64
N_RES = 8


def draw_neighbours(key, part):
    key_share, key_roll, key_near, key_far = jax.random.split(key, 4)
    local_row = jnp.arange(RESIDUES, dtype=jnp.int32) % RES_DEV
    far_share = jax.random.randint(key_share, (RESIDUES, 1), 0, 61)
    roll_value = jax.random.randint(key_roll, (RESIDUES, K), 0, 100)
    near_entry = (local_row[:, None] + jax.random.randint(key_near, (RESIDUES, K), -16, 17)) % RES_DEV
    far_entry = RES_DEV + jax.random.randint(key_far, (RESIDUES, K), 0, 4 * RES_DEV)
    entries = jnp.where(roll_value < far_share, far_entry, near_entry).astype(jnp.int32)
    return entries.at[0, 0].set(5 * RES_DEV - 1).at[0, 1].set(0)


def draw_requests(key, part):
    pair_keys = jax.random.split(key, N_RES * N_RES)

    def one_pair(pair_key):
        chosen = jax.random.permutation(pair_key, RES_DEV)[:CAP].astype(jnp.int32)
        has_last = jnp.any(chosen == RES_DEV - 1)
        return jnp.where(has_last, chosen, chosen.at[0].set(RES_DEV - 1))
    return jax.vmap(one_pair)(pair_keys).reshape(N_RES, N_RES, CAP).astype(jnp.int32)


def draw_counts(key, part):
    drawn = jax.random.randint(key, (RESIDUES,), NB_LEAST, NB_MOST + 1).astype(jnp.int32)
    return drawn.at[0].set(NB_MOST).at[1].set(NB_LEAST)


def block_scale(stream_key, shape, cuts, smallest, top_value):
    level, own = 1.0, jax.random.fold_in(stream_key, 6)
    for axis_at, blocks in cuts:
        draws = jnp.exp(jax.random.uniform(jax.random.fold_in(own, axis_at), (blocks,), jnp.float32, smallest / len(cuts), top_value / len(cuts)))
        level = level * jnp.repeat(draws, shape[axis_at] // blocks).reshape([-1 if axis == axis_at else 1 for axis in range(len(shape))])
    return level


def bell_draw(stream_key, shape, scale, limit, cuts=(), kind=jnp.bfloat16):
    gain = block_scale(stream_key, shape, cuts, -0.22, 0.18) if cuts else 1.0
    result = jax.random.normal(stream_key, shape, jnp.float32) * scale * gain
    return jnp.minimum(jnp.maximum(result, -limit), limit).astype(kind)


def setup_inputs(seed: int = 0) -> dict:
    key_of = jax.random.split(jax.random.key(seed), 18)
    return {
        "node_state": bell_draw(key_of[0], (RESIDUES, D), 1.0, 6.0, ((0, 8), (1, 4))),
        "edge_state": bell_draw(key_of[1], (RESIDUES, K, C), 1.0, 6.0, ((0, 8), (1, 4))),
        "node_gain": jnp.clip(1.0 + 0.15 * jax.random.normal(key_of[2], (D,), jnp.float32), 0.25, 1.75),
        "edge_gain": jnp.clip(1.0 + 0.15 * jax.random.normal(key_of[3], (C,), jnp.float32), 0.25, 1.75),
        "ffn_gain": jnp.clip(1.0 + 0.15 * jax.random.normal(key_of[4], (D,), jnp.float32), 0.25, 1.75),
        "w_self": bell_draw(key_of[5], (D, MH), (2 * D + C) ** -0.5, 0.15625, ((1, 4),)),
        "w_neigh": bell_draw(key_of[6], (D, MH), (2 * D + C) ** -0.5, 0.15625, ((1, 4),)),
        "w_edge": bell_draw(key_of[7], (C, MH), (2 * D + C) ** -0.5, 0.15625, ((1, 4),)),
        "w_message": bell_draw(key_of[8], (MH, D), (MH // 8) ** -0.5, 0.375, ((0, 4),)),
        "w_update": bell_draw(key_of[9], (MH, C), MH ** -0.5, 0.125, ((0, 4),)),
        "w_expand": bell_draw(key_of[10], (D, FF), D ** -0.5, 0.25, ((1, 4),)),
        "w_contract": bell_draw(key_of[11], (FF, D), (FF // 2) ** -0.5, 0.1875, ((0, 4),)),
        "neighbours": draw_neighbours(jax.random.fold_in(key_of[17], 71), 0),
        "requests": draw_requests(jax.random.fold_in(key_of[17], 71), 0),
        "counts": draw_counts(jax.random.fold_in(key_of[17], 71), 0),
        "node_cotangent": bell_draw(key_of[15], (RESIDUES, D), 1.0, 6.0, ((0, 8), (1, 4))),
        "edge_cotangent": bell_draw(key_of[16], (RESIDUES, K, C), 1.0, 6.0, ((0, 8), (1, 4))),
    }


EPSILON = 1e-05
HIGHEST = lax.Precision.HIGHEST

@jax.custom_vjp
def low(v):
    return lax.optimization_barrier(v.astype(jnp.bfloat16)).astype(jnp.float32)

@jax.custom_vjp
def low_back(v):
    return v

def low_keep(v):
    return (low(v), None)

def low_pass(kept, grad):
    return (grad,)

def back_keep(v):
    return (v, None)

def back_low(kept, grad):
    return (low(grad),)
low.defvjp(low_keep, low_pass)
low_back.defvjp(back_keep, back_low)

def layer_norm(values, gain_value):
    centred = values - lax.optimization_barrier(jnp.mean(values, -1, keepdims=True))
    return centred * lax.rsqrt(lax.optimization_barrier(jnp.mean(centred * centred, -1, keepdims=True)) + EPSILON) * gain_value

def matmul(left_side, right_side):
    return jnp.dot(left_side, right_side, precision=HIGHEST)

def reference(node_state, edge_state, node_gain, edge_gain, ffn_gain, w_self, w_neigh, w_edge, w_message, w_update, w_expand, w_contract, neighbours, requests, counts, node_cotangent, edge_cotangent):
    residues = neighbours.shape[0]
    blocks = residues // RES_DEV
    block_of = (jnp.arange(residues) // RES_DEV).astype(jnp.int32)[:, None]
    remote = jnp.maximum(neighbours - RES_DEV, 0).astype(jnp.int32)
    source = (remote // CAP).astype(jnp.int32)
    fetched = requests[block_of, source, (remote % CAP).astype(jnp.int32)]
    global_index = jnp.where(neighbours < RES_DEV, block_of * RES_DEV + neighbours, source * RES_DEV + fetched).astype(jnp.int32)
    live_slots = (jnp.arange(K)[None, :] < counts[:, None]).astype(jnp.float32)
    mean_share = live_slots / counts[:, None].astype(jnp.float32)

    def graph_layer(node_in, edge_in, gain_node, gain_edge, gain_ffn, self_proj, neigh_proj, edge_proj, message_proj, update_proj, expand_proj, contract_proj):
        normed = low(layer_norm(node_in, gain_node))
        edge_normed = low(layer_norm(edge_in, gain_edge))
        own_term = matmul(normed, self_proj)
        neigh_term = matmul(normed, neigh_proj)

        def run_block(block_item):
            own_block, index_block, edge_block, share_block, live_block = block_item
            before = own_block[:, None, :] + neigh_term[index_block] + jnp.einsum('bkc,cm->bkm', edge_block, edge_proj, precision=HIGHEST)
            before = low_back(before)
            hidden = low(jax.nn.gelu(before))
            mean_hidden = low(lax.optimization_barrier(jnp.sum(hidden * share_block[:, :, None], 1)))
            update = low_back(jnp.einsum('bkm,mc->bkc', hidden, update_proj, precision=HIGHEST) * live_block[:, :, None])
            return (mean_hidden, update)
        mean_hidden, update = lax.map(jax.checkpoint(run_block), (own_term.reshape(blocks, RES_DEV, -1), global_index.reshape(blocks, RES_DEV, K), edge_normed.reshape(blocks, RES_DEV, K, -1), mean_share.reshape(blocks, RES_DEV, K), live_slots.reshape(blocks, RES_DEV, K)))
        mean_hidden = mean_hidden.reshape(residues, -1)
        update = update.reshape(residues, K, -1)
        middle = node_in + low_back(matmul(mean_hidden, message_proj))
        ffn_input = low(layer_norm(middle, gain_ffn))
        expand = low_back(matmul(ffn_input, expand_proj))
        active = low(jax.nn.gelu(expand))
        return (middle + low_back(matmul(active, contract_proj)), edge_in + update)
    params = (node_gain, edge_gain, ffn_gain) + tuple((matrix.astype(jnp.float32) for matrix in (w_self, w_neigh, w_edge, w_message, w_update, w_expand, w_contract)))
    first_node, first_edge = graph_layer(node_state.astype(jnp.float32), edge_state.astype(jnp.float32), *params)
    outputs, pullback = jax.vjp(graph_layer, low(first_node), low(first_edge), *params)
    gradients = pullback((node_cotangent.astype(jnp.float32), edge_cotangent.astype(jnp.float32)))
    return (outputs[0].astype(jnp.bfloat16), outputs[1].astype(jnp.bfloat16), gradients[0], gradients[1], gradients[2], gradients[3], gradients[4], gradients[5], gradients[6], gradients[7], gradients[8], gradients[9], gradients[10], gradients[11])
```

```python
import functools
import jax, jax.numpy as jnp
from jax import lax
from jax.experimental import pallas as pl
from jax.experimental.pallas import tpu as pltpu
from jax.sharding import PartitionSpec as P
F32=jnp.float32; BF=jnp.bfloat16
EPS=1e-5
GC=0.7978845608028654; GA=0.044715
def nt(a,b): return lax.dot_general(a,b,(((1,),(1,)),((),())),preferred_element_type=F32)
def tn(a,b): return lax.dot_general(a,b,(((0,),(0,)),((),())),preferred_element_type=F32)
def norm_back(dy,u,s,g):
    d=dy*g
    return s*(d-jnp.mean(d,-1,keepdims=True)-u*jnp.mean(d*u,-1,keepdims=True))
def nn(a,b): return jnp.dot(a,b,preferred_element_type=F32)
def unit(v):
    c=v-jnp.mean(v,-1,keepdims=True)
    s=lax.rsqrt(jnp.mean(c*c,-1,keepdims=True)+EPS)
    return c*s,s

def efwd_kernel(second,nres,TR,unroll,e_ref,v_ref,tab_ref,eg_ref,cnt_ref,wn_ref,ws_ref,weu_ref,wm_ref,*rest):
    if second:
        gt_ref,en_ref,msg_ref,dg_ref,mean_ref,gwu_ref,A,B,upd,macc,mean,L,gacc=rest
    else:
        en_ref,msg_ref,A,B,upd,macc,mean,L=rest
    c=pl.program_id(0); nc=pl.num_programs(0)
    rows,cw=e_ref.shape
    tabn,dn=tab_ref.shape
    U=wn_ref.shape[-1]
    sl=rows//nres
    nt_=rows//TR
    rt=TR//sl
    KA=A.shape[1]
    @pl.when(c==0)
    def _():
        i128=lax.broadcasted_iota(jnp.int32,(TR,128),1)
        r128=lax.broadcasted_iota(jnp.int32,(TR,128),0)
        def init(t,_):
            rs=pl.ds(pl.multiple_of(t*TR,TR),TR)
            v=v_ref[rs,:]
            for q in range(tabn//128):
                A[rs,q*128:(q+1)*128]=jnp.where(v==i128+q*128,1.0,0.0).astype(BF)
            own=(r128//sl+t*rt)==i128
            A[rs,tabn:tabn+nres]=jnp.where(own,1.0,0.0).astype(BF)
            u,_s=unit(e_ref[rs,:].astype(F32))
            A[rs,tabn+nres:tabn+nres+cw]=(u*eg_ref[...]).astype(BF)
            A[rs,tabn+nres+cw:]=jnp.zeros((TR,KA-tabn-nres-cw),BF)
            upd[rs,:]=jnp.zeros((TR,cw),F32)
            return 0
        lax.fori_loop(0,nt_,init,0)
        macc[...]=jnp.zeros_like(macc)
        ri=lax.broadcasted_iota(jnp.int32,(rt,TR),0); ci=lax.broadcasted_iota(jnp.int32,(rt,TR),1)
        S=jnp.where(ci//sl==ri,1.0,0.0).astype(BF)
        for t in range(nt_ if second else 1):
            L[t,:rt,:]=S
            if second:
                lv=v_ref[t*TR:(t+1)*TR,:]>=0
                lm=jnp.concatenate([lv,lv],axis=1)[:,:cw]
                L[t,rt:,:]=jnp.where(lm,gt_ref[t*TR:(t+1)*TR,:].astype(F32),0.0).astype(BF).T
    B[:tabn,:]=nn(tab_ref[...],wn_ref[0]).astype(BF)
    B[tabn:tabn+nres,:]=nn(tab_ref[:nres,:],ws_ref[0]).astype(BF)
    B[tabn+nres:,:]=weu_ref[0,:256,:]
    if second: gacc[...]=jnp.zeros_like(gacc)
    def step(t,_):
        rs=pl.ds(pl.multiple_of(t*TR,TR),TR)
        x=nn(A[rs,:],B[...])
        x2=x*x
        th=jnp.tanh(x*(GC+(GC*GA)*x2))
        hx=0.5*x
        hid=hx+hx*th
        live=v_ref[rs,:]>=0
        lm=jnp.concatenate([live]*(U//128),axis=1)
        hb=jnp.where(lm,hid,0.0).astype(BF)
        if second:
            dg_ref[rs,:]=(0.5+0.5*th+hx*(1.0-th*th)*(GC+(3*GC*GA)*x2)).astype(BF)
        upd[rs,:]+=nt(hb,weu_ref[0,256:256+cw,:])
        if second:
            m=nn(L[t],hb)
            gacc[...]+=m[rt:,:]
            mean[pl.ds(pl.multiple_of(t*rt,rt),rt),:]=m[:rt,:]
        else:
            mean[pl.ds(pl.multiple_of(t*rt,rt),rt),:]=nn(L[0],hb)
        return 0
    lax.fori_loop(0,nt_,step,0,unroll=unroll)
    mb=(mean[...]*(1.0/cnt_ref[...])).astype(BF)
    if second:
        mean_ref[0]=mb
        gwu_ref[0]=gacc[...].astype(BF)
    macc[...]+=nn(mb,wm_ref[0])
    @pl.when(c==nc-1)
    def _():
        msg_ref[...]=macc[...].astype(BF)
        def fin(t,_):
            rs=pl.ds(pl.multiple_of(t*TR,TR),TR)
            en_ref[rs,:]=(e_ref[rs,:].astype(F32)+upd[rs,:]).astype(BF)
            return 0
        lax.fori_loop(0,nt_,fin,0)

def efwd(second,e,v,tab,eg,cnt,wn,ws,weu,wm,gt=None,TR=1024,unroll=1):
    rows,cw=e.shape; tabn,dn=tab.shape; H,_,U=wn.shape; nres=cnt.shape[0]
    sl=rows//nres; rt=TR//sl; ntl=rows//TR
    KA=tabn+nres+256
    full=lambda a: pl.BlockSpec(a.shape,lambda c:(0,)*a.ndim,pipeline_mode=pl.Buffered(1))
    wsp=lambda a: pl.BlockSpec((1,)+a.shape[1:],lambda c:(c,0,0))
    ins=[e,v,tab,eg,cnt,wn,ws,weu,wm]+([gt] if second else [])
    specs=[full(a) for a in (e,v,tab,eg,cnt)]+[wsp(a) for a in (wn,ws,weu,wm)]+([full(gt)] if second else [])
    osh=[jax.ShapeDtypeStruct((rows,cw),BF),jax.ShapeDtypeStruct((nres,dn),BF)]
    osp=[pl.BlockSpec((rows,cw),lambda c:(0,0)),pl.BlockSpec((nres,dn),lambda c:(0,0))]
    lrows=rt+(cw if second else 0)
    scr=[pltpu.VMEM((rows,KA),BF),pltpu.VMEM((KA,U),BF),pltpu.VMEM((rows,cw),F32),pltpu.VMEM((nres,dn),F32),pltpu.VMEM((nres,U),F32),pltpu.VMEM((ntl if second else 1,lrows,TR),BF)]
    if second:
        osh+=[jax.ShapeDtypeStruct((rows,H*U),BF),jax.ShapeDtypeStruct((H,nres,U),BF),jax.ShapeDtypeStruct((H,cw,U),BF)]
        osp+=[pl.BlockSpec((rows,U),lambda c:(0,c)),pl.BlockSpec((1,nres,U),lambda c:(c,0,0)),pl.BlockSpec((1,cw,U),lambda c:(c,0,0))]
        scr+=[pltpu.VMEM((cw,U),F32)]
    fl=2*rows*KA*H*U+2*rows*H*U*cw*(2 if second else 1)
    return pl.pallas_call(functools.partial(efwd_kernel,second,nres,TR,unroll),grid=(H,),in_specs=specs,out_specs=osp,out_shape=osh,scratch_shapes=scr,
        compiler_params=pltpu.CompilerParams(vmem_limit_bytes=60<<20,dimension_semantics=("arbitrary",)),
        cost_estimate=pl.CostEstimate(flops=fl,bytes_accessed=16<<20,transcendentals=rows*H*U),name="edges_second" if second else "edges_first")(*ins)

def ebwd_kernel(nres,TR,e_ref,v_ref,vr_ref,tab_ref,eg_ref,cnt_ref,gm_ref,cot_ref,dg_ref,wn_ref,ws_ref,weu_ref,wm_ref,ge_ref,gtab_ref,gown_ref,gwn_ref,gwe_ref,gg_ref,L2,L3,tabT,R2,gb,gen,gta):
    c=pl.program_id(0); nc=pl.num_programs(0)
    rows,cw=e_ref.shape
    tabn,dn=tab_ref.shape
    U=wn_ref.shape[-1]
    sl=rows//nres
    nt_=rows//TR
    rt=TR//sl
    K2=L2.shape[1]
    @pl.when(c==0)
    def _():
        i128=lax.broadcasted_iota(jnp.int32,(TR,nres),1)
        r128=lax.broadcasted_iota(jnp.int32,(TR,nres),0)
        tabT[...]=tab_ref[...].T
        for t in range(nt_):
            rs=pl.ds(t*TR,TR)
            live=v_ref[rs,:]>=0
            own=((r128//sl+t*rt)==i128)&live
            L2[rs,:nres]=jnp.where(own,1.0,0.0).astype(BF)
            lm=jnp.concatenate([live,live],axis=1)[:,:cw]
            L2[rs,nres:nres+cw]=jnp.where(lm,cot_ref[rs,:].astype(F32),0.0).astype(BF)
            L2[rs,nres+cw:]=jnp.zeros((TR,K2-nres-cw),BF)
            u,_s=unit(e_ref[rs,:].astype(F32))
            L3[tabn+nres:tabn+nres+cw,t*TR:(t+1)*TR]=(u*eg_ref[...]).astype(BF).T
            vr=vr_ref[:,t*TR:(t+1)*TR]
            si=lax.broadcasted_iota(jnp.int32,(128,TR),0)
            for q in range(tabn//128):
                L3[q*128:(q+1)*128,t*TR:(t+1)*TR]=jnp.where(vr==si+q*128,1.0,0.0).astype(BF)
            li=lax.broadcasted_iota(jnp.int32,(nres,TR),1); s2=lax.broadcasted_iota(jnp.int32,(nres,TR),0)
            L3[tabn:tabn+nres,t*TR:(t+1)*TR]=jnp.where((li//sl+t*rt)==s2,1.0,0.0).astype(BF)
        gen[...]=jnp.zeros_like(gen)
        gta[...]=jnp.zeros_like(gta)
    R2[:nres,:]=(nt(gm_ref[...],wm_ref[0])*(1.0/cnt_ref[...])).astype(BF)
    R2[nres:,:]=weu_ref[0,256:,:]
    def step(t,_):
        rs=pl.ds(pl.multiple_of(t*TR,TR),TR)
        g=(nn(L2[rs,:],R2[...])*dg_ref[rs,:].astype(F32)).astype(BF)
        gb[rs,:]=g
        gen[rs,:]+=nt(g,weu_ref[0,:cw,:])
        return 0
    lax.fori_loop(0,nt_,step,0)
    acc=nn(L3[...],gb[...])
    gp=acc[:tabn].astype(BF)
    go=acc[tabn:tabn+nres].astype(BF)
    gown_ref[0]=go
    gwe_ref[0]=acc[tabn+nres:].astype(BF)
    gwn_ref[0]=nn(tabT[...],gp).astype(BF)
    gta[...]+=nt(gp,wn_ref[0])
    gta[:nres,:]+=nt(go,ws_ref[0])
    @pl.when(c==nc-1)
    def _():
        gtab_ref[...]=gta[...].astype(BF)
        gg_ref[...]=jnp.zeros_like(gg_ref)
        for t in range(nt_):
            rs=pl.ds(t*TR,TR)
            u,s=unit(e_ref[rs,:].astype(F32))
            dy=gen[rs,:]
            gg_ref[...]+=jnp.sum(dy*u,0,keepdims=True)
            dyg=dy*eg_ref[...]
            dv=s*(dyg-jnp.mean(dyg,-1,keepdims=True)-u*jnp.mean(dyg*u,-1,keepdims=True))
            ge_ref[rs,:]=cot_ref[rs,:].astype(F32)+dv

def ebwd(e,v,vr,tab,eg,cnt,gm,cot,dg,wn,ws,weu,wm,TR=1024):
    rows,cw=e.shape; tabn,dn=tab.shape; H,_,U=wn.shape; nres=cnt.shape[0]
    K2=nres+256
    full=lambda a: pl.BlockSpec(a.shape,lambda c:(0,)*a.ndim,pipeline_mode=pl.Buffered(1))
    wsp=lambda a: pl.BlockSpec((1,)+a.shape[1:],lambda c:(c,0,0))
    ins=[e,v,vr,tab,eg,cnt,gm,cot,dg,wn,ws,weu,wm]
    specs=[full(a) for a in ins[:8]]+[pl.BlockSpec((rows,U),lambda c:(0,c))]+[wsp(a) for a in ins[9:]]
    S=jax.ShapeDtypeStruct
    osh=[S((rows,cw),F32),S((tabn,dn),BF),S((H,nres,U),BF),S((H,dn,U),BF),S((H,cw,U),BF),S((1,cw),F32)]
    c3=lambda c:(c,0,0); c0=lambda c:(0,0)
    osp=[pl.BlockSpec((rows,cw),c0,pipeline_mode=pl.Buffered(1)),pl.BlockSpec((tabn,dn),c0),pl.BlockSpec((1,nres,U),c3),pl.BlockSpec((1,dn,U),c3),pl.BlockSpec((1,cw,U),c3),pl.BlockSpec((1,cw),c0)]
    scr=[pltpu.VMEM((rows,K2),BF),pltpu.VMEM((tabn+nres+cw,rows),BF),pltpu.VMEM((dn,tabn),BF),pltpu.VMEM((K2,U),BF),pltpu.VMEM((rows,U),BF),pltpu.VMEM((rows,cw),F32),pltpu.VMEM((tabn,dn),F32)]
    fl=2*rows*H*U*(K2+256+960)
    return pl.pallas_call(functools.partial(ebwd_kernel,nres,TR),grid=(H,),in_specs=specs,out_specs=osp,out_shape=osh,scratch_shapes=scr,
        compiler_params=pltpu.CompilerParams(vmem_limit_bytes=60<<20,dimension_semantics=("arbitrary",)),
        cost_estimate=pl.CostEstimate(flops=fl,bytes_accessed=24<<20,transcendentals=0),name="edges_back")(*ins)


class Net:
    def __init__(self, send_sems, recv_sems):
        self.send_sems, self.recv_sems, self.count, self.sent = send_sems, recv_sems, 0, []

    def push(self, src, dst, device):
        k = self.count
        self.count += 1
        copy = pltpu.make_async_remote_copy(
            src_ref=src,
            dst_ref=dst,
            send_sem=self.send_sems.at[k],
            recv_sem=self.recv_sems.at[k],
            device_id=device,
            device_id_type=pl.DeviceIdType.MESH,
        )
        copy.start()
        self.sent.append(copy)
        return copy

    def finish(self):
        for copy in self.sent:
            copy.wait_send()


def flip_bit(index, bit):
    step = 1 << bit
    return index + step - 2 * step * ((index // step) % 2)


def greet(devices):
    barrier = pltpu.get_barrier_semaphore()
    for device in devices:
        pl.semaphore_signal(
            barrier, inc=1, device_id=device, device_id_type=pl.DeviceIdType.MESH
        )
    pl.semaphore_wait(barrier, len(devices))


def place(groups, parts):
    p, h = lax.axis_index("res"), lax.axis_index("hid")
    line = [None] + [(p, lax.rem(h + i, parts)) for i in range(1, parts)]
    plane = [None] + [(lax.rem(p + i, groups), h) for i in range(1, groups)]
    return p, h, line, plane


def send_rows(net, p, groups, plane, nres, cap, normed, sid_ref, tab_ref, rows_buf):
    copies = []
    ids = lax.broadcasted_iota(jnp.int32, (nres, cap), 0)
    mine = pl.ds(pl.multiple_of(nres + p * cap, 16), cap)
    for i in range(groups):
        q = lax.rem(p + i, groups)
        chosen = jnp.where(ids == sid_ref[q], 1.0, 0.0).astype(BF)
        rows = tn(chosen, normed).astype(BF)
        if i == 0:
            tab_ref[mine, :] = rows
        else:
            rows_buf[i] = rows
            copies.append(net.push(rows_buf.at[i], tab_ref.at[mine, :], plane[i]))
    return copies


def prologue_kernel(groups, parts, nw, *refs):
    node_ref, cot_ref, req_ref, gain_ref = refs[:4]
    w_refs = refs[4 : 4 + nw]
    tab_ref, xr_ref, cf_ref, sid_ref = refs[4 + nw : 8 + nw]
    full_refs = refs[8 + nw : 8 + 2 * nw]
    nbuf, cbuf, nfull, rows_buf, ss, rs, ls = refs[8 + 2 * nw :]
    p, h, line, plane = place(groups, parts)
    nres, part = node_ref.shape
    cap = req_ref.shape[2]
    rp = nres // parts
    greet(line[1:] + plane[1:])
    net = Net(ss, rs)
    node_copies = [net.push(node_ref, nbuf.at[h], line[i]) for i in range(1, parts)]
    req_copies = [
        net.push(req_ref.at[lax.rem(p + i, groups)], sid_ref.at[p], plane[i])
        for i in range(1, groups)
    ]
    cot_copies = [net.push(cot_ref, cbuf.at[h], line[i]) for i in range(1, parts)]
    nbuf[h] = node_ref[...]
    cbuf[h] = cot_ref[...]
    sid_ref[p] = req_ref[p]
    levels = groups.bit_length() - 1
    low, half = p % 2, p // 2
    turned = sum(((half // (1 << b)) % 2) * (1 << (levels - 2 - b)) for b in range(levels - 1))
    starts = (low * (groups // 2) + half, low * (groups // 2) + turned)
    slice_rows = w_refs[0].shape[0] // groups
    gathered = []
    local = []
    for w in range(nw):
        rows = pl.ds(pl.multiple_of(starts[w % 2] * slice_rows, slice_rows), slice_rows)
        gathered.append(
            [
                net.push(
                    w_refs[w].at[rows, :], full_refs[w].at[parts - i, rows, :], line[i]
                )
                for i in range(1, parts)
            ]
        )
        keep = pltpu.make_async_copy(w_refs[w], full_refs[w].at[0], ls.at[w])
        keep.start()
        local.append(keep)
    for copy in node_copies:
        copy.wait_recv()
    for c in range(parts):
        nfull[:, c * part : (c + 1) * part] = nbuf[c]
    unit_node, scale = unit(nfull[...].astype(F32))
    normed = (unit_node * gain_ref[...]).astype(BF)
    tab_ref[:nres, :] = normed
    xr_ref[...] = nfull[pl.ds(pl.multiple_of(h * rp, rp), rp), :]
    for copy in req_copies:
        copy.wait_recv()
    row_copies = send_rows(net, p, groups, plane, nres, cap, normed, sid_ref, tab_ref, rows_buf)
    last = [None] * nw
    for t in range(nw + levels - 1):
        for level in range(levels - 1, -1, -1):
            w = t - level
            if not 0 <= w < nw:
                continue
            for copy in gathered[w] if level == 0 else [last[w]]:
                copy.wait_recv()
            if level == levels - 1:
                bit = 0
            else:
                bit = 1 + (level if w % 2 == 0 else levels - 2 - level)
            span = slice_rows << level
            held = (starts[w % 2] // (1 << level)) * span
            view = full_refs[w].at[1:parts, pl.ds(pl.multiple_of(held, span), span), :]
            last[w] = net.push(view, view, (flip_bit(p, bit), h))
    for copy in cot_copies:
        copy.wait_recv()
    for c in range(parts):
        cf_ref[:, c * part : (c + 1) * part] = cbuf[c]
    for copy in row_copies + last:
        copy.wait_recv()
    for keep in local:
        keep.wait()
    net.finish()


def prologue(groups, parts, node, cot, req, gain, weights):
    nres, part = node.shape
    cap = req.shape[2]
    dn = part * parts
    nw = len(weights)
    levels = groups.bit_length() - 1
    copies = 2 * (parts - 1) + 2 * (groups - 1) + nw * (parts - 1 + levels)
    S = jax.ShapeDtypeStruct
    vm, anyspace = pl.BlockSpec(memory_space=pltpu.VMEM), pl.BlockSpec(memory_space=pl.ANY)
    return pl.pallas_call(
        functools.partial(prologue_kernel, groups, parts, nw),
        in_specs=[vm] * 4 + [anyspace] * nw,
        out_specs=[vm] * 4 + [anyspace] * nw,
        out_shape=[
            S((nres + groups * cap, dn), BF),
            S((nres // parts, dn), BF),
            S((nres, dn), BF),
            S(req.shape, jnp.int32),
        ]
        + [S((parts,) + w.shape, BF) for w in weights],
        scratch_shapes=[
            pltpu.VMEM((parts, nres, part), BF),
            pltpu.VMEM((parts, nres, part), BF),
            pltpu.VMEM((nres, dn), BF),
            pltpu.VMEM((groups, cap, dn), BF),
            pltpu.SemaphoreType.DMA((copies,)),
            pltpu.SemaphoreType.DMA((copies,)),
            pltpu.SemaphoreType.DMA((nw,)),
        ],
        compiler_params=pltpu.CompilerParams(
            collective_id=0, has_side_effects=True, vmem_limit_bytes=24 << 20
        ),
        name="gather_start",
    )(node, cot, req, gain, *weights)


def gelu_parts(x):
    x2 = x * x
    th = jnp.tanh(x * (GC + (GC * GA) * x2))
    hx = 0.5 * x
    return hx + hx * th, 0.5 + 0.5 * th + hx * (1.0 - th * th) * (GC + (3 * GC * GA) * x2)


def node_kernel(groups, parts, second, *refs):
    if second:
        (msg_ref, xr_ref, gain_ref, wx_ref, wc_ref, cf_ref) = refs[:6]
        (nn_ref, gm_ref, gmid_ref, act_ref, gex_ref, fi_ref, fg_ref) = refs[6:13]
        (rbuf, wxv, wcv, dgs, nsp, ss, rs, ls) = refs[13:]
    else:
        (msg_ref, xr_ref, gain_ref, wx_ref, wc_ref, ngain_ref, sid_ref) = refs[:7]
        (tab_ref, x1_ref) = refs[7:9]
        (rbuf, wxv, wcv, nfull, rows_buf, ss, rs, ls) = refs[9:]
    p, h, line, plane = place(groups, parts)
    nres, dn = msg_ref.shape
    rp = nres // parts
    mine = pl.ds(pl.multiple_of(h * rp, rp), rp)
    load_x = pltpu.make_async_copy(wx_ref, wxv, ls.at[0])
    load_c = pltpu.make_async_copy(wc_ref, wcv, ls.at[1])
    load_x.start()
    load_c.start()
    greet(line[1:] if second else line[1:] + plane[1:])
    net = Net(ss, rs)
    copies = [
        net.push(
            msg_ref.at[pl.ds(pl.multiple_of(lax.rem(h + i, parts) * rp, rp), rp), :],
            rbuf.at[i],
            line[i],
        )
        for i in range(1, parts)
    ]
    middle = xr_ref[...].astype(F32) + msg_ref[mine, :].astype(F32)
    for i, copy in enumerate(copies):
        copy.wait_recv()
        middle = middle + rbuf[i + 1].astype(F32)
    unit_ffn, scale = unit(middle)
    ffn_input = (unit_ffn * gain_ref[...]).astype(BF)
    load_x.wait()
    load_c.wait()
    out = middle
    for c in range(parts):
        act, dg = gelu_parts(nn(ffn_input, wxv[c]))
        act = act.astype(BF)
        out = out + nn(act, wcv[c])
        if second:
            act_ref[c] = act
            dgs[c] = dg
    result = out.astype(BF)
    if not second:
        x1_ref[...] = result
        nfull[mine, :] = result
        copies = [net.push(x1_ref, nfull.at[mine, :], line[i]) for i in range(1, parts)]
        for copy in copies:
            copy.wait_recv()
        unit_node, scale = unit(nfull[...].astype(F32))
        normed = (unit_node * ngain_ref[...]).astype(BF)
        tab_ref[:nres, :] = normed
        cap = sid_ref.shape[2]
        copies = send_rows(net, p, groups, plane, nres, cap, normed, sid_ref, tab_ref, rows_buf)
        for copy in copies:
            copy.wait_recv()
        net.finish()
        return
    part = dn // parts
    fi_ref[...] = ffn_input
    cot = cf_ref[mine, :]
    g_input = jnp.zeros((rp, dn), F32)
    for c in range(parts):
        g_expand = (nt(cot, wcv[c]) * dgs[c]).astype(BF)
        gex_ref[c] = g_expand
        g_input = g_input + nt(g_expand, wxv[c])
    fg_ref[...] = jnp.sum(g_input * unit_ffn, 0, keepdims=True)
    g_middle = cot.astype(F32) + norm_back(g_input, unit_ffn, scale, gain_ref[...])
    gmid_ref[...] = g_middle
    gm_ref[mine, :] = g_middle.astype(BF)
    copies = [net.push(gm_ref.at[mine, :], gm_ref.at[mine, :], line[i]) for i in range(1, parts)]
    for c in range(parts):
        nsp[c] = result[:, c * part : (c + 1) * part]
    copies += [
        net.push(nsp.at[lax.rem(h + i, parts)], nn_ref.at[mine, :], line[i])
        for i in range(1, parts)
    ]
    nn_ref[mine, :] = nsp[h]
    for copy in copies:
        copy.wait_recv()
    net.finish()


def node_step(groups, parts, second, msg, xr, gain, wx, wc, *more):
    nres, dn = msg.shape
    rp = nres // parts
    part = dn // parts
    units = wx.shape[2]
    S = jax.ShapeDtypeStruct
    vm, anyspace = pl.BlockSpec(memory_space=pltpu.VMEM), pl.BlockSpec(memory_space=pl.ANY)
    if second:
        out_shape = [
            S((nres, part), BF),
            S((nres, dn), BF),
            S((rp, dn), F32),
            S((parts, rp, units), BF),
            S((parts, rp, units), BF),
            S((rp, dn), BF),
            S((1, dn), F32),
        ]
        extra = [pltpu.VMEM((parts, rp, units), F32), pltpu.VMEM((parts, rp, part), BF)]
        copies = 3 * (parts - 1)
    else:
        cap = more[1].shape[2]
        out_shape = [S((nres + groups * cap, dn), BF), S((rp, dn), BF)]
        extra = [pltpu.VMEM((nres, dn), BF), pltpu.VMEM((groups, cap, dn), BF)]
        copies = 2 * (parts - 1) + groups - 1
    return pl.pallas_call(
        functools.partial(node_kernel, groups, parts, second),
        in_specs=[vm] * 3 + [anyspace] * 2 + [vm] * len(more),
        out_specs=[vm] * len(out_shape),
        out_shape=out_shape,
        scratch_shapes=[
            pltpu.VMEM((parts, rp, dn), BF),
            pltpu.VMEM(wx.shape, BF),
            pltpu.VMEM(wc.shape, BF),
            *extra,
            pltpu.SemaphoreType.DMA((copies,)),
            pltpu.SemaphoreType.DMA((copies,)),
            pltpu.SemaphoreType.DMA((2,)),
        ],
        compiler_params=pltpu.CompilerParams(
            collective_id=2 if second else 1, has_side_effects=True, vmem_limit_bytes=32 << 20
        ),
        name="node_second" if second else "node_first",
    )(msg, xr, gain, wx, wc, *more)


class PlaneSum:
    def __init__(self, net, p, h, groups, order, first, recv, acc):
        self.net, self.p, self.h, self.groups = net, p, h, groups
        self.order, self.held, self.recv, self.acc = order, first, recv, acc
        self.level, self.copy, self.count = 0, None, groups

    def bit(self):
        levels = self.groups.bit_length() - 1
        if self.level == 0:
            return 0
        return self.level if self.order == 0 else levels - self.level

    def pick(self, value):
        low = self.level == 0 or self.order == 0
        return self.held.at[:, :, value] if low else self.held.at[:, value]

    def send(self):
        bit = self.bit()
        own = (self.p // (1 << bit)) % 2
        self.own = own
        self.copy = self.net.push(
            self.pick(1 - own), self.recv[self.level], (flip_bit(self.p, bit), self.h)
        )

    def add(self):
        self.copy.wait_recv()
        count = self.count // 2
        got, out, kept = self.recv[self.level], self.acc[self.level], self.pick(self.own)
        for i in range(count):
            total = kept[:, i].astype(F32) + got[:, i].astype(F32)
            if count == 1:
                out[...] = total.astype(out.dtype)
            elif self.order == 0:
                out[:, i // 2, i % 2] = total.astype(out.dtype)
            else:
                out[:, i // (count // 2), i % (count // 2)] = total.astype(out.dtype)
        self.held, self.count = out, count
        self.level += 1


def plane_scratch(groups, lead, rows, units, order):
    recv, acc = [], []
    count = groups
    while count > 1:
        count //= 2
        recv.append(pltpu.VMEM((lead, count, rows, units), BF))
        if count == 1:
            acc.append(pltpu.VMEM((lead, rows, units), F32 if lead == 1 else BF))
        elif order == 0:
            acc.append(pltpu.VMEM((lead, count // 2, 2, rows, units), BF))
        else:
            acc.append(pltpu.VMEM((lead, 2, count // 2, rows, units), BF))
    return recv + acc


def finish_kernel(groups, parts, *refs):
    (gtab_ref, gown_ref, mean_ref, act_ref, gex_ref, fi_ref, gm_ref, cf_ref, tab_ref, sid_ref) = refs[:10]
    (x1_ref, gmid_ref, ngain_ref, gwn_ref, gwe_ref, gwu_ref, vec_ref) = refs[10:17]
    (gnode_ref, ows_ref, own_ref, owe_ref, owm_ref, owu_ref, owx_ref, owc_ref, ovec_ref) = refs[17:26]
    (ret, gnp, gbuf, gnr, gnf, zown, zmean, actf, gexf, fif, vec, vz, vp) = refs[26:39]
    rest = list(refs[39:-2])
    ss, rs = refs[-2:]
    p, h, line, plane = place(groups, parts)
    nres = gm_ref.shape[0]
    dn = gm_ref.shape[1]
    cap = sid_ref.shape[2]
    rp = nres // parts
    part = dn // parts
    levels = groups.bit_length() - 1
    mine = pl.ds(pl.multiple_of(h * rp, rp), rp)

    def take(count):
        taken = rest[:count]
        del rest[:count]
        return taken

    greet(line[1:] + plane[1:])
    net = Net(ss, rs)

    def plane_sum(order, first=None):
        got = take(2 * levels + (1 if first is None else 0))
        source = got.pop(0) if first is None else first
        return PlaneSum(net, p, h, groups, order, source, got[:levels], got[levels:])

    sums = {
        "neigh": plane_sum(0, gwn_ref),
        "edge": plane_sum(1, gwe_ref),
        "update": plane_sum(1, gwu_ref),
        "self": plane_sum(0),
        "message": plane_sum(1),
        "expand": plane_sum(0),
        "contract": plane_sum(1),
    }
    zsum = dict(zip(("neigh", "edge", "update"), take(3)))

    def fill(name, value):
        rows = value.shape[0] // groups
        value = value.astype(BF)
        for s in range(groups):
            sums[name].held[0, s // 2, s % 2] = value[s * rows : (s + 1) * rows, :]

    ret_copies = [
        net.push(
            gtab_ref.at[
                pl.ds(pl.multiple_of(nres + lax.rem(p + i, groups) * cap, 16), cap), :
            ],
            ret.at[i],
            plane[i],
        )
        for i in range(1, groups)
    ]
    own_copies = [net.push(gown_ref.at[i], zown.at[i], line[i]) for i in range(1, parts)]
    for name in ("neigh", "edge", "update"):
        sums[name].send()
    mean_copies = [net.push(mean_ref.at[i], zmean.at[i], line[i]) for i in range(1, parts)]
    ffn_copies = []
    for i in range(1, parts):
        ffn_copies.append(net.push(act_ref.at[i], actf.at[mine, :], line[i]))
        ffn_copies.append(net.push(gex_ref.at[i], gexf.at[mine, :], line[i]))
        ffn_copies.append(net.push(fi_ref, fif.at[mine, :], line[i]))
    actf[mine, :] = act_ref[0]
    gexf[mine, :] = gex_ref[0]
    fif[mine, :] = fi_ref[...]
    ids = lax.broadcasted_iota(jnp.int32, (nres, cap), 0)
    total = gtab_ref[:nres, :].astype(F32)
    for i in range(groups):
        if i:
            ret_copies[i - 1].wait_recv()
            rows = ret[i]
        else:
            rows = gtab_ref[pl.ds(pl.multiple_of(nres + p * cap, 16), cap), :]
        chosen = jnp.where(ids == sid_ref[lax.rem(p + groups - i, groups)], 1.0, 0.0).astype(BF)
        total = total + nn(chosen, rows)
    gnp[...] = total.astype(BF)
    row_copies = [
        net.push(
            gnp.at[pl.ds(pl.multiple_of(lax.rem(h + i, parts) * rp, rp), rp), :],
            gbuf.at[i],
            line[i],
        )
        for i in range(1, parts)
    ]
    for name in ("neigh", "edge", "update"):
        sums[name].add()
        sums[name].send()
    value = gown_ref[0].astype(F32)
    for i in range(1, parts):
        own_copies[i - 1].wait_recv()
        value = value + zown[i].astype(F32)
    fill("self", tn(tab_ref[:nres, :], value.astype(BF)))
    sums["self"].send()
    g_normed = gnp[mine, :].astype(F32)
    for i in range(1, parts):
        row_copies[i - 1].wait_recv()
        g_normed = g_normed + gbuf[i].astype(F32)
    unit_node, scale = unit(x1_ref[...].astype(F32))
    rows = gmid_ref[...] + norm_back(g_normed, unit_node, scale, ngain_ref[...])
    for c in range(parts):
        gnr[c] = rows[:, c * part : (c + 1) * part]
    node_copies = [
        net.push(gnr.at[lax.rem(h + i, parts)], gnf.at[mine, :], line[i]) for i in range(1, parts)
    ]
    gnf[mine, :] = gnr[h]
    vec[:, :dn] = jnp.sum(g_normed * unit_node, 0, keepdims=True)
    vec[:, dn:] = vec_ref[...]
    vec_copies = [net.push(vec, vz.at[i], line[i]) for i in range(1, parts)]
    value = mean_ref[0].astype(F32)
    for i in range(1, parts):
        mean_copies[i - 1].wait_recv()
        value = value + zmean[i].astype(F32)
    fill("message", tn(gm_ref[...], value.astype(BF)))
    sums["message"].send()
    for copy in ffn_copies:
        copy.wait_recv()
    fill("expand", tn(fif[...], gexf[...]))
    sums["expand"].send()
    fill("contract", tn(cf_ref[...], actf[...]))
    sums["contract"].send()
    value = vec[...]
    for i in range(1, parts):
        vec_copies[i - 1].wait_recv()
        value = value + vz[i]
    vp[0] = value
    vec_copies = [net.push(vp.at[0], vp.at[i], plane[i]) for i in range(1, groups)]
    for level in range(1, levels):
        for name in ("self", "neigh", "edge", "update", "message", "expand", "contract"):
            sums[name].add() if name in zsum or level > 0 else None
            if sums[name].level < levels:
                sums[name].send()
    line_copies = {}
    for name in ("neigh", "edge", "update"):
        done = sums[name].held
        line_copies[name] = [
            net.push(done.at[i], zsum[name].at[i], line[i]) for i in range(1, parts)
        ]
    for name, out in (
        ("self", ows_ref),
        ("message", owm_ref),
        ("expand", owx_ref),
        ("contract", owc_ref),
    ):
        while sums[name].level < levels:
            sums[name].add()
            if sums[name].level < levels:
                sums[name].send()
        out[...] = sums[name].held[0]
    value = vp[0]
    for i in range(1, groups):
        vec_copies[i - 1].wait_recv()
        value = value + vp[i]
    ovec_ref[...] = value
    for copy in node_copies:
        copy.wait_recv()
    gnode_ref[...] = gnf[...]
    for name, out in (("neigh", own_ref), ("edge", owe_ref), ("update", owu_ref)):
        value = sums[name].held[0].astype(F32)
        for i in range(1, parts):
            line_copies[name][i - 1].wait_recv()
            value = value + zsum[name][i].astype(F32)
        out[...] = value
    net.finish()


def finish(groups, parts, gtab, gown, mean, act, gex, fi, gm, cf, tab, sid, x1, gmid, ngain, gwn, gwe, gwu, vec):
    nres, dn = gm.shape
    cap = sid.shape[2]
    units = gown.shape[2]
    rp = nres // parts
    part = dn // parts
    levels = groups.bit_length() - 1
    cw = gwe.shape[1]
    wide = dn // groups
    narrow = cw // groups
    split = lambda g: g.reshape(parts, groups // 2, 2, g.shape[1] // groups, units)
    S = jax.ShapeDtypeStruct
    V = pltpu.VMEM
    total = dn + vec.shape[1]
    scratch = [
        V((groups, cap, dn), BF),
        V((nres, dn), BF),
        V((parts, rp, dn), BF),
        V((parts, rp, part), F32),
        V((nres, part), F32),
        V((parts, nres, units), BF),
        V((parts, nres, units), BF),
        V((nres, units), BF),
        V((nres, units), BF),
        V((nres, dn), BF),
        V((1, total), F32),
        V((parts, 1, total), F32),
        V((groups, 1, total), F32),
    ]
    scratch += plane_scratch(groups, parts, wide, units, 0)
    scratch += plane_scratch(groups, parts, narrow, units, 1)
    scratch += plane_scratch(groups, parts, narrow, units, 1)
    for order in (0, 1, 0, 1):
        scratch += [V((1, groups // 2, 2, wide, units), BF)]
        scratch += plane_scratch(groups, 1, wide, units, order)
    scratch += [V((parts, wide, units), BF), V((parts, narrow, units), BF), V((parts, narrow, units), BF)]
    copies = (groups - 1) * 2 + (parts - 1) * (1 + 1 + 3 + 1 + 1 + 1 + 3) + 7 * levels
    scratch += [pltpu.SemaphoreType.DMA((copies,)), pltpu.SemaphoreType.DMA((copies,))]
    vm = pl.BlockSpec(memory_space=pltpu.VMEM)
    return pl.pallas_call(
        functools.partial(finish_kernel, groups, parts),
        in_specs=[vm] * 17,
        out_specs=[vm] * 9,
        out_shape=[
            S((nres, part), F32),
            S((wide, units), F32),
            S((wide, units), F32),
            S((narrow, units), F32),
            S((wide, units), F32),
            S((narrow, units), F32),
            S((wide, units), F32),
            S((wide, units), F32),
            S((1, total), F32),
        ],
        scratch_shapes=scratch,
        compiler_params=pltpu.CompilerParams(
            collective_id=3, has_side_effects=True, vmem_limit_bytes=56 << 20
        ),
        name="finish",
    )(gtab, gown, mean, act, gex, fi, gm, cf, tab, sid, x1, gmid, ngain, split(gwn), split(gwe), split(gwu), vec)


def per_device(
    node_state,
    edge_state,
    node_gain,
    edge_gain,
    ffn_gain,
    w_self,
    w_neigh,
    w_edge,
    w_message,
    w_update,
    w_expand,
    w_contract,
    neighbours,
    requests,
    counts,
    node_cotangent,
    edge_cotangent,
):
    groups, parts = lax.axis_size("res"), lax.axis_size("hid")
    nres, slots = neighbours.shape
    slot_part, cw = edge_state.shape[1:]
    units = w_self.shape[1]
    rows = nres * slot_part
    h, p = lax.axis_index("hid"), lax.axis_index("res")
    count_col = counts.astype(F32)[:, None]
    live = lax.broadcasted_iota(jnp.int32, (nres, slots), 1) < counts[:, None]
    entry = jnp.where(live, neighbours, -1)
    entry = lax.dynamic_slice_in_dim(entry, h * slot_part, slot_part, 1).reshape(rows)
    entry_col = jnp.broadcast_to(entry[:, None], (rows, 128))
    entry_row = entry[None, :]
    gap = jnp.zeros((256 - cw, units), BF)
    w_pair = jnp.concatenate([w_edge, gap, w_update.T, gap], 0)
    ngain, egain, fgain = node_gain[None], edge_gain[None], ffn_gain[None]
    edges = edge_state.reshape(rows, cw)
    cot = edge_cotangent.reshape(rows, cw)
    tab, xr, cf, sid, wn, ws, wp, wm, wx, wc = prologue(
        groups,
        parts,
        node_state,
        node_cotangent,
        requests[0][:, None, :],
        ngain,
        [w_neigh, w_self, w_pair, w_message, w_expand, w_contract],
    )
    edge_one, msg = efwd(False, edges, entry_col, tab, egain, count_col, wn, ws, wp, wm)
    tab, x1 = node_step(groups, parts, False, msg, xr, fgain, wx, wc, ngain, sid)
    edge_two, msg, dg, mean, gwu = efwd(
        True, edge_one, entry_col, tab, egain, count_col, wn, ws, wp, wm, cot
    )
    node_two, gm, gmid, act, gex, fi, fg = node_step(
        groups, parts, True, msg, x1, fgain, wx, wc, cf
    )
    grad_edge, gtab, gown, gwn, gwe, eg = ebwd(
        edge_one, entry_col, entry_row, tab, egain, count_col, gm, cot, dg, wn, ws, wp, wm
    )
    vec = jnp.concatenate([fg, eg], 1)
    gnode, gws, gwn, gwe, gwm, gwu, gwx, gwc, vec = finish(
        groups, parts, gtab, gown, mean, act, gex, fi, gm, cf, tab, sid, x1, gmid, ngain, gwn, gwe, gwu, vec
    )
    dn = ngain.shape[1]
    cut = lambda start, size: lax.dynamic_slice_in_dim(
        vec[0, start : start + size], p * (size // groups), size // groups, 0
    )
    return (
        node_two,
        edge_two.reshape(nres, slot_part, cw),
        gnode,
        grad_edge.reshape(nres, slot_part, cw),
        cut(0, dn),
        cut(2 * dn, cw),
        cut(dn, dn),
        gws,
        gwn,
        gwe,
        gwm.T,
        gwu.T,
        gwx,
        gwc.T,
    )


def solution(mesh):
    return jax.shard_map(
        per_device,
        mesh=mesh,
        in_specs=(
            P("res", "hid"),
            P("res", "hid", None),
            P(),
            P(),
            P(),
            P(None, "hid"),
            P(None, "hid"),
            P(None, "hid"),
            P("hid", None),
            P("hid", None),
            P(None, "hid"),
            P("hid", None),
            P("res", None),
            P("res", None, None),
            P("res"),
            P("res", "hid"),
            P("res", "hid", None),
        ),
        out_specs=(
            P("res", "hid"),
            P("res", "hid", None),
            P("res", "hid"),
            P("res", "hid", None),
            P("res"),
            P("res"),
            P("res"),
            P("res", "hid"),
            P("res", "hid"),
            P("res", "hid"),
            P("hid", "res"),
            P("hid", "res"),
            P("res", "hid"),
            P("hid", "res"),
        ),
        check_vma=False,
    )
```

```python
import functools

import jax
import jax.numpy as jnp
from jax import lax
from jax.experimental import pallas as pl
from jax.experimental.pallas import tpu as pltpu
from jax.sharding import PartitionSpec as P

F32, BF = jnp.float32, jnp.bfloat16
EPSILON = 1e-05
TANH_SCALE = 0.7978845608028654
TANH_CUBE = 0.044715
MESH = pl.DeviceIdType.MESH
NEIGH, PAIR, SELF, MESSAGE = range(4)
EXPAND, CONTRACT = range(2)


def contract(a, b, dim_a, dim_b):
    return lax.dot_general(
        a, b, (((dim_a,), (dim_b,)), ((), ())), preferred_element_type=F32
    )


def nn(a, b):
    return contract(a, b, 1, 0)


def nt(a, b):
    return contract(a, b, 1, 1)


def tn(a, b):
    return contract(a, b, 0, 0)


def normalize(values, axis):
    centred = values - jnp.mean(values, axis, keepdims=True)
    scaling = lax.rsqrt(jnp.mean(centred * centred, axis, keepdims=True) + EPSILON)
    return centred * scaling, scaling


def norm_back(grad, unit, scaling, gain, axis):
    scaled = grad * gain
    return scaling * (
        scaled
        - jnp.mean(scaled, axis, keepdims=True)
        - unit * jnp.mean(scaled * unit, axis, keepdims=True)
    )


def gelu(x):
    return (0.5 * x) * (1.0 + jnp.tanh(x * (TANH_SCALE + TANH_SCALE * TANH_CUBE * (x * x))))


def gelu_pair(x):
    square = x * x
    bent = jnp.tanh(x * (TANH_SCALE + TANH_SCALE * TANH_CUBE * square))
    half = 0.5 * x
    slope = 0.5 + 0.5 * bent + half * (1.0 - bent * bent) * (
        TANH_SCALE + 3 * TANH_SCALE * TANH_CUBE * square
    )
    return half + half * bent, slope


class Net:
    def __init__(self, send_sems, recv_sems):
        self.send_sems, self.recv_sems, self.count, self.sent = send_sems, recv_sems, 0, []

    def make(self, src, dst, device):
        k = self.count
        self.count += 1
        copy = pltpu.make_async_remote_copy(
            src_ref=src,
            dst_ref=dst,
            send_sem=self.send_sems.at[k],
            recv_sem=self.recv_sems.at[k],
            device_id=device,
            device_id_type=MESH,
        )
        self.sent.append(copy)
        return copy

    def push(self, src, dst, device):
        copy = self.make(src, dst, device)
        copy.start()
        return copy

    def finish(self):
        for copy in self.sent:
            copy.wait_send()


def start(copies):
    for copy in copies:
        copy.start()


def arrived(copies):
    for copy in copies:
        copy.wait_recv()


def flip_bit(index, bit):
    step = 1 << bit
    return index + step - 2 * step * ((index // step) % 2)


def greet(devices):
    barrier = pltpu.get_barrier_semaphore()
    for device in devices:
        pl.semaphore_signal(barrier, inc=1, device_id=device, device_id_type=MESH)
    pl.semaphore_wait(barrier, len(devices))


def place(groups, parts):
    p, h = lax.axis_index("res"), lax.axis_index("hid")
    line = [None] + [(p, lax.rem(h + i, parts)) for i in range(1, parts)]
    plane = [None] + [(lax.rem(p + i, groups), h) for i in range(1, groups)]
    return p, h, line, plane


class Rows:
    def __init__(self, net, p, groups, plane, nres, cap, tab_ref, rows_buf):
        self.mine = pl.ds(pl.multiple_of(nres + p * cap, 16), cap)
        self.asked = [lax.rem(p + i, groups) for i in range(groups)]
        self.nres, self.cap, self.tab, self.buf = nres, cap, tab_ref, rows_buf
        self.copies = [
            net.make(rows_buf.at[i], tab_ref.at[self.mine, :], plane[i]) for i in range(1, groups)
        ]

    def send(self, normed, sid_ref):
        ids = lax.broadcasted_iota(jnp.int32, (self.nres, self.cap), 0)
        self.tab[: self.nres, :] = normed
        for i, q in enumerate(self.asked):
            chosen = jnp.where(ids == sid_ref[q], 1.0, 0.0).astype(BF)
            rows = tn(chosen, normed).astype(BF)
            if i == 0:
                self.tab[self.mine, :] = rows
            else:
                self.buf[i] = rows
                self.copies[i - 1].start()


class Gather:
    def __init__(self, net, p, h, groups, parts, edge_full, node_full, depth):
        self.levels = groups.bit_length() - 1
        low, half = p % 2, p // 2
        turned = sum(
            ((half // (1 << b)) % 2) * (1 << (self.levels - 2 - b)) for b in range(self.levels - 1)
        )
        starts = [low * (groups // 2) + half, low * (groups // 2) + turned]
        rows = depth // groups
        back = [(p, lax.rem(h + parts - i, parts)) for i in range(parts)]
        self.batches = []

        def batch(full, pieces):
            line, steps = [], [[] for _ in range(self.levels)]
            for lead, weights, turn in pieces:
                begin = starts[turn]
                own = pl.ds(pl.multiple_of(begin * rows, rows), rows)
                for r in range(lead[0], lead[1]):
                    line.append(
                        net.make(
                            full.at[0, weights[0] : weights[1], own, :],
                            full.at[r, weights[0] : weights[1], own, :],
                            back[r],
                        )
                    )
                for level in range(self.levels):
                    if level == self.levels - 1:
                        bit = 0
                    else:
                        bit = 1 + (level if turn == 0 else self.levels - 2 - level)
                    span = rows << level
                    held = (begin // (1 << level)) * span
                    view = full.at[
                        lead[0] : lead[1],
                        weights[0] : weights[1],
                        pl.ds(pl.multiple_of(held, span), span),
                        :,
                    ]
                    steps[level].append(net.make(view, view, (flip_bit(p, bit), h)))
            self.batches.append([line] + steps)

        for r in range(1, parts):
            batch(edge_full, [((r, r + 1), (NEIGH, SELF), 0), ((r, r + 1), (SELF, MESSAGE), 1)])
        for turn, full, w in (
            (0, edge_full, MESSAGE),
            (1, node_full, EXPAND),
            (0, node_full, CONTRACT),
        ):
            batch(full, [((1, parts), (w, w + 1), turn)])
        self.slots = len(self.batches) + self.levels + 1

    def turn(self, slot):
        for stage in range(self.levels + 1, -1, -1):
            b = slot - stage
            if 0 <= b < len(self.batches):
                if stage:
                    arrived(self.batches[b][stage - 1])
                if stage <= self.levels:
                    start(self.batches[b][stage])


def build_inputs(a_ref, edges, v_ref, egain, tabn):
    slots, cw, nres = edges.shape
    index = lax.broadcasted_iota(jnp.int32, (tabn, nres), 0)
    own = lax.broadcasted_iota(jnp.int32, (nres, nres), 0) == lax.broadcasted_iota(
        jnp.int32, (nres, nres), 1
    )
    own = jnp.where(own, 1.0, 0.0).astype(BF)
    height = a_ref.shape[0]

    def one(k, _):
        cs = pl.ds(pl.multiple_of(k * nres, nres), nres)
        a_ref[:tabn, cs] = jnp.where(index == v_ref[k], 1.0, 0.0).astype(BF)
        a_ref[tabn : tabn + nres, cs] = own
        unit, _scale = normalize(edges[k].astype(F32), 0)
        a_ref[tabn + nres : tabn + nres + cw, cs] = (unit * egain).astype(BF)
        a_ref[tabn + nres + cw :, cs] = jnp.zeros((height - tabn - nres - cw, nres), BF)
        return 0

    lax.fori_loop(0, slots, one, 0)


def edge_chunk(c, w_ref, tab, a_ref, bt, wut, v_ref, upd, mean, cw, second=None):
    tabn, nres = tab.shape[0], mean.shape[-1]
    slots = a_ref.shape[1] // nres
    bt[:, :tabn] = nt(w_ref[c, NEIGH], tab[...]).astype(BF)
    bt[:, tabn : tabn + nres] = nt(w_ref[c, SELF], tab[:nres, :]).astype(BF)
    bt[:, tabn + nres :] = w_ref[c, PAIR, :, :256]
    wut[...] = w_ref[c, PAIR, :, 256:].T[:cw]
    before = nn(bt[...], a_ref[...])
    if second is None:
        hidden = gelu(before)
    else:
        dg, gup, gwu = second
        hidden, slope = gelu_pair(before)
    total, kept = None, []
    for k in range(slots):
        cs = slice(k * nres, (k + 1) * nres)
        live = (v_ref[k] >= 0).astype(F32)
        part = hidden[:, cs] * live
        total = part if total is None else total + part
        kept.append(part.astype(BF))
        if second is not None:
            dg[:, cs] = (slope[:, cs] * live).astype(BF)
    mean[c] = total
    kept = jnp.concatenate(kept, axis=1)
    upd[...] += nn(wut[...], kept)
    if second is not None:
        gwu[c] = nt(gup[...], kept).astype(BF)


def message_part(w_ref, mean, inverse, parts, mean_out=None):
    total = None
    for c in range(parts):
        scaled = (mean[c] * inverse).astype(BF)
        if mean_out is not None:
            mean_out[c] = scaled
        term = tn(scaled, w_ref[c, MESSAGE])
        total = term if total is None else total + term
    return total.astype(BF)


def add_update(edges, upd, out):
    slots, _, nres = edges.shape
    for k in range(slots):
        out[k] = (edges[k].astype(F32) + upd[:, k * nres : (k + 1) * nres]).astype(BF)


def first_kernel(groups, parts, *refs):
    (node_ref, cot_ref, req_ref, v_ref, egain_ref, inv_ref, ngain_ref, fgain_ref) = refs[:8]
    (edges_hbm, wn_hbm, ws_hbm, we_hbm, wu_hbm, wm_hbm, wx_hbm, wc_hbm) = refs[8:16]
    (w_ref, wf_ref, tab_ref, x1_ref, xf_ref, e1_ref, cf_ref, sid_ref) = refs[16:24]
    (nbuf, cbuf, nfull, xrows, rows0, rows1, tab0, edges, lw, le, a_ref, bt, wut, upd, mean) = refs[24:39]
    (msg, mbuf, ss, rs, ls) = refs[39:]
    p, h, line, plane = place(groups, parts)
    nres, part = node_ref.shape
    cap = req_ref.shape[2]
    cw = edges.shape[1]
    rp = nres // parts
    tabn = tab0.shape[0]
    mine = pl.ds(pl.multiple_of(h * rp, rp), rp)
    loads = [
        pltpu.make_async_copy(src, dst, ls.at[k])
        for k, (src, dst) in enumerate(
            (
                (wn_hbm, lw.at[0]),
                (we_hbm, le.at[0]),
                (wu_hbm, le.at[1]),
                (ws_hbm, lw.at[1]),
                (edges_hbm, edges),
                (wm_hbm, w_ref.at[0, MESSAGE]),
                (wx_hbm, lw.at[2]),
                (wc_hbm, wf_ref.at[0, CONTRACT]),
            )
        )
    ]
    start(loads)
    net = Net(ss, rs)
    node_copies = [net.make(node_ref, nbuf.at[h], line[i]) for i in range(1, parts)]
    req_copies = [
        net.make(req_ref.at[lax.rem(p + i, groups)], sid_ref.at[p], plane[i])
        for i in range(1, groups)
    ]
    cot_copies = [net.make(cot_ref, cbuf.at[h], line[i]) for i in range(1, parts)]
    rows_first = Rows(net, p, groups, plane, nres, cap, tab0, rows0)
    rows_next = Rows(net, p, groups, plane, nres, cap, tab_ref, rows1)
    message_copies = [
        net.make(
            msg.at[pl.ds(pl.multiple_of(lax.rem(h + i, parts) * rp, rp), rp), :],
            mbuf.at[i],
            line[i],
        )
        for i in range(1, parts)
    ]
    x1_copies = [net.make(x1_ref, xf_ref.at[mine, :], line[i]) for i in range(1, parts)]
    gather = Gather(net, p, h, groups, parts, w_ref, wf_ref, w_ref.shape[2])
    greet(line[1:] + plane[1:])
    start(node_copies)
    start(req_copies)
    start(cot_copies)
    nbuf[h] = node_ref[...]
    cbuf[h] = cot_ref[...]
    sid_ref[p] = req_ref[p]
    loads[0].wait()
    w_ref[0, NEIGH] = lw[0].T
    loads[1].wait()
    loads[2].wait()
    units = w_ref.shape[2]
    w_ref[0, PAIR, :, :cw] = le[0].T
    w_ref[0, PAIR, :, cw:256] = jnp.zeros((units, 256 - cw), BF)
    w_ref[0, PAIR, :, 256 : 256 + cw] = le[1].T
    w_ref[0, PAIR, :, 256 + cw :] = jnp.zeros((units, 256 - cw), BF)
    loads[3].wait()
    w_ref[0, SELF] = lw[1].T
    gather.turn(0)
    arrived(node_copies)
    for c in range(parts):
        nfull[:, c * part : (c + 1) * part] = nbuf[c]
    unit_node, _scale = normalize(nfull[...].astype(F32), 1)
    normed = (unit_node * ngain_ref[...]).astype(BF)
    xrows[...] = nfull[mine, :]
    arrived(req_copies)
    rows_first.send(normed, sid_ref)
    loads[4].wait()
    build_inputs(a_ref, edges, v_ref, egain_ref[...], tabn)
    loads[5].wait()
    loads[6].wait()
    wf_ref[0, EXPAND] = lw[2].T
    loads[7].wait()
    gather.turn(1)
    arrived(cot_copies)
    for c in range(parts):
        cf_ref[:, c * part : (c + 1) * part] = cbuf[c]
    upd[...] = jnp.zeros_like(upd)
    arrived(rows_first.copies)
    ready = gather.levels + 1
    ahead = 2

    def chunk(c, _):
        for k in range(1, parts):

            @pl.when(c == k)
            def _():
                for slot in range(ahead if k == 1 else ready + k - 1, ready + k):
                    gather.turn(slot)

        edge_chunk(c, w_ref, tab0, a_ref, bt, wut, v_ref, upd, mean, cw)
        return 0

    lax.fori_loop(0, parts, chunk, 0)
    gather.turn(ready + parts - 1)
    add_update(edges, upd, e1_ref)
    msg[...] = message_part(w_ref, mean, inv_ref[...], parts)
    start(message_copies)
    middle = xrows[...].astype(F32) + msg[mine, :].astype(F32)
    gather.turn(ready + parts)
    for i, copy in enumerate(message_copies):
        copy.wait_recv()
        middle = middle + mbuf[i + 1].astype(F32)
    unit_ffn, _scale = normalize(middle, 1)
    ffn_input = (unit_ffn * fgain_ref[...]).astype(BF)
    active = [gelu(nt(ffn_input, wf_ref[c, EXPAND])).astype(BF) for c in range(parts)]
    for slot in range(ready + parts + 1, gather.slots):
        gather.turn(slot)
    out = middle
    for c in range(parts):
        out = out + nn(active[c], wf_ref[c, CONTRACT])
    out = out.astype(BF)
    x1_ref[...] = out
    xf_ref[mine, :] = out
    start(x1_copies)
    arrived(x1_copies)
    unit_node, _scale = normalize(xf_ref[...].astype(F32), 1)
    rows_next.send((unit_node * ngain_ref[...]).astype(BF), sid_ref)
    arrived(rows_next.copies)
    net.finish()


def first(groups, parts, node, cot, req, v, egain, inv, ngain, fgain, edges, weights):
    nres, part = node.shape
    cap = req.shape[2]
    dn = part * parts
    slots, cw, _ = edges.shape
    units = weights[0].shape[1]
    rows = slots * nres
    tabn = nres + groups * cap
    rp = nres // parts
    levels = groups.bit_length() - 1
    copies = 4 * (parts - 1) + 3 * (groups - 1) + (parts - 1) * (2 + 2 * levels + 3) + 3 * levels
    S, V = jax.ShapeDtypeStruct, pltpu.VMEM
    vm, anyspace = pl.BlockSpec(memory_space=pltpu.VMEM), pl.BlockSpec(memory_space=pltpu.MemorySpace.HBM)
    return pl.pallas_call(
        functools.partial(first_kernel, groups, parts),
        in_specs=[vm] * 8 + [anyspace] * 8,
        out_specs=[vm] * 8,
        out_shape=[
            S((parts, 4, units, dn), BF),
            S((parts, 2, units, dn), BF),
            S((tabn, dn), BF),
            S((rp, dn), BF),
            S((nres, dn), BF),
            S(edges.shape, BF),
            S((nres, dn), BF),
            S(req.shape, jnp.int32),
        ],
        scratch_shapes=[
            V((parts, nres, part), BF),
            V((parts, nres, part), BF),
            V((nres, dn), BF),
            V((rp, dn), BF),
            V((groups, cap, dn), BF),
            V((groups, cap, dn), BF),
            V((tabn, dn), BF),
            V(edges.shape, BF),
            V((3, dn, units), BF),
            V((2, cw, units), BF),
            V((tabn + nres + 256, rows), BF),
            V((units, tabn + nres + 256), BF),
            V((cw, units), BF),
            V((cw, rows), F32),
            V((parts, units, nres), F32),
            V((nres, dn), BF),
            V((parts, rp, dn), BF),
            pltpu.SemaphoreType.DMA((copies,)),
            pltpu.SemaphoreType.DMA((copies,)),
            pltpu.SemaphoreType.DMA((8,)),
        ],
        compiler_params=pltpu.CompilerParams(
            collective_id=0, has_side_effects=True, vmem_limit_bytes=38 << 20
        ),
        name="first_pass",
    )(node, cot, req, v, egain, inv, ngain, fgain, edges, *weights)


def second_kernel(groups, parts, *refs):
    (w_ref, wf_ref, tab_ref, x1_ref, e1_ref, v_ref, egain_ref, inv_ref, fgain_ref, cf_ref) = refs[:10]
    cot_hbm, refs = refs[10], refs[1:]
    (a_ref, gup, dg_hbm, mean_ref, gwu_ref, e2_ref) = refs[10:16]
    (nn_ref, gm_ref, gmid_ref, act_ref, gex_ref, fi_ref, fg_ref) = refs[16:23]
    (cot, bt, wut, upd, mean, dgbuf, msg, mbuf, slopes, nsp, ss, rs, ls, ds) = refs[23:]
    p, h, line, plane = place(groups, parts)
    slots, cw, nres = e1_ref.shape
    tabn, dn = tab_ref.shape
    rp = nres // parts
    part = dn // parts
    mine = pl.ds(pl.multiple_of(h * rp, rp), rp)
    load = pltpu.make_async_copy(cot_hbm, cot, ls.at[0])
    load.start()
    net = Net(ss, rs)
    message_copies = [
        net.make(
            msg.at[pl.ds(pl.multiple_of(lax.rem(h + i, parts) * rp, rp), rp), :],
            mbuf.at[i],
            line[i],
        )
        for i in range(1, parts)
    ]
    gm_copies = [
        net.make(gm_ref.at[mine, :], gm_ref.at[mine, :], line[i]) for i in range(1, parts)
    ]
    out_copies = [
        net.make(nsp.at[lax.rem(h + i, parts)], nn_ref.at[mine, :], line[i])
        for i in range(1, parts)
    ]
    greet(line[1:])
    build_inputs(a_ref, e1_ref, v_ref, egain_ref[...], tabn)
    upd[...] = jnp.zeros_like(upd)
    load.wait()
    for k in range(slots):
        live = (v_ref[k] >= 0).astype(F32)
        gup[:, k * nres : (k + 1) * nres] = (cot[k].astype(F32) * live).astype(BF)

    def save(c):
        return pltpu.make_async_copy(dgbuf.at[c % 2], dg_hbm.at[c], ds.at[c % 2])

    def chunk(c, _):
        @pl.when(c >= 2)
        def _():
            save(c - 2).wait()

        edge_chunk(
            c, w_ref, tab_ref, a_ref, bt, wut, v_ref, upd, mean, cw, (dgbuf.at[c % 2], gup, gwu_ref)
        )
        save(c).start()
        return 0

    lax.fori_loop(0, parts, chunk, 0)
    msg[...] = message_part(w_ref, mean, inv_ref[...], parts, mean_ref)
    start(message_copies)
    add_update(e1_ref, upd, e2_ref)
    middle = x1_ref[...].astype(F32) + msg[mine, :].astype(F32)
    for i, copy in enumerate(message_copies):
        copy.wait_recv()
        middle = middle + mbuf[i + 1].astype(F32)
    unit_ffn, scaling = normalize(middle, 1)
    ffn_input = (unit_ffn * fgain_ref[...]).astype(BF)
    fi_ref[...] = ffn_input
    cotangent = cf_ref[mine, :]
    out = middle
    g_input = jnp.zeros((rp, dn), F32)
    for c in range(parts):
        active, slope = gelu_pair(nt(ffn_input, wf_ref[c, EXPAND]))
        act_ref[c] = active.astype(BF)
        g_expand = (nt(cotangent, wf_ref[c, CONTRACT]) * slope).astype(BF)
        gex_ref[c] = g_expand
        g_input = g_input + nn(g_expand, wf_ref[c, EXPAND])
    g_middle = cotangent.astype(F32) + norm_back(g_input, unit_ffn, scaling, fgain_ref[...], 1)
    gm_ref[mine, :] = g_middle.astype(BF)
    start(gm_copies)
    gmid_ref[...] = g_middle
    fg_ref[...] = jnp.sum(g_input * unit_ffn, 0, keepdims=True)
    for c in range(parts):
        out = out + nn(act_ref[c], wf_ref[c, CONTRACT])
    out = out.astype(BF)
    for c in range(parts):
        nsp[c] = out[:, c * part : (c + 1) * part]
    start(out_copies)
    nn_ref[mine, :] = nsp[h]
    for c in range(max(parts - 2, 0), parts):
        save(c).wait()
    arrived(gm_copies + out_copies)
    net.finish()


def second(groups, parts, w, wf, tab, x1, e1, v, egain, inv, fgain, cf, cot):
    slots, cw, nres = e1.shape
    tabn, dn = tab.shape
    units = w.shape[2]
    rows = slots * nres
    rp = nres // parts
    part = dn // parts
    S, V = jax.ShapeDtypeStruct, pltpu.VMEM
    vm, anyspace = pl.BlockSpec(memory_space=pltpu.VMEM), pl.BlockSpec(memory_space=pltpu.MemorySpace.HBM)
    copies = 3 * (parts - 1)
    return pl.pallas_call(
        functools.partial(second_kernel, groups, parts),
        in_specs=[vm] * 10 + [anyspace],
        out_specs=[vm, vm, anyspace] + [vm] * 10,
        out_shape=[
            S((tabn + nres + 256, rows), BF),
            S((cw, rows), BF),
            S((parts, units, rows), BF),
            S((parts, units, nres), BF),
            S((parts, cw, units), BF),
            S(e1.shape, BF),
            S((nres, part), BF),
            S((nres, dn), BF),
            S((rp, dn), F32),
            S((parts, rp, units), BF),
            S((parts, rp, units), BF),
            S((rp, dn), BF),
            S((1, dn), F32),
        ],
        scratch_shapes=[
            V(e1.shape, BF),
            V((units, tabn + nres + 256), BF),
            V((cw, units), BF),
            V((cw, rows), F32),
            V((parts, units, nres), F32),
            V((2, units, rows), BF),
            V((nres, dn), BF),
            V((parts, rp, dn), BF),
            V((parts, rp, units), F32),
            V((parts, rp, part), BF),
            pltpu.SemaphoreType.DMA((copies,)),
            pltpu.SemaphoreType.DMA((copies,)),
            pltpu.SemaphoreType.DMA((1,)),
            pltpu.SemaphoreType.DMA((2,)),
        ],
        compiler_params=pltpu.CompilerParams(
            collective_id=1, has_side_effects=True, vmem_limit_bytes=36 << 20
        ),
        name="second_pass",
    )(w, wf, tab, x1, e1, v, egain, inv, fgain, cf, cot)


class PlaneSum:
    def __init__(self, net, p, h, groups, order, source, recv, acc, done):
        levels = groups.bit_length() - 1
        self.order, self.acc, self.recv, self.done = order, acc, recv, done
        self.levels, self.count = levels, groups
        self.own, self.kept, self.copies = [], [], []
        held = source
        for level in range(levels):
            bit = 0 if level == 0 else (level if order == 0 else levels - level)
            low = level == 0 or order == 0
            own = (p // (1 << bit)) % 2
            pick = lambda value: held.at[:, :, value] if low else held.at[:, value]
            self.kept.append(pick(own))
            self.copies.append(net.make(pick(1 - own), recv[level], (flip_bit(p, bit), h)))
            held = acc[level]

    def steps(self):
        return [functools.partial(self.step, level) for level in range(self.levels + 1)]

    def step(self, level):
        if level:
            k = level - 1
            self.copies[k].wait_recv()
            count = self.count >> level
            got, out, kept = self.recv[k], self.acc[k], self.kept[k]
            for i in range(count):
                total = (kept[:, i].astype(F32) + got[:, i].astype(F32)).astype(out.dtype)
                if count == 1:
                    out[...] = total
                elif self.order == 0:
                    out[:, i // 2, i % 2] = total
                else:
                    out[:, i // (count // 2), i % (count // 2)] = total
        if level < self.levels:
            self.copies[level].start()
        else:
            self.done(self.acc[-1])


class Plan:
    def __init__(self):
        self.points, self.active = {}, []

    def add(self, point, steps, first_now=True):
        steps = list(steps)
        if first_now:
            self.note(point, steps.pop(0))
        if steps:
            self.active.append(steps)

    def note(self, point, step):
        self.points.setdefault(point, []).append(step)

    def advance(self, point):
        for steps in self.active:
            self.note(point, steps.pop(0))
        self.active = [steps for steps in self.active if steps]

    def run(self, point):
        for step in self.points.get(point, ()):
            step()


def plane_scratch(groups, lead, rows, units, order, last):
    recv, acc = [], []
    count = groups
    while count > 1:
        count //= 2
        recv.append(pltpu.VMEM((lead, count, rows, units), BF))
        if count == 1:
            acc.append(pltpu.VMEM((lead, rows, units), last))
        elif order == 0:
            acc.append(pltpu.VMEM((lead, count // 2, 2, rows, units), BF))
        else:
            acc.append(pltpu.VMEM((lead, 2, count // 2, rows, units), BF))
    return recv + acc


def third_kernel(groups, parts, *refs):
    (w_ref, a_ref, gup, tab_ref, sid_ref, x1_ref, xf_ref, e1_ref, egain_ref, inv_ref, ngain_ref) = refs[:11]
    (gm_ref, gmid_ref, cf_ref, mean_ref, gwu_ref, act_ref, gex_ref, fi_ref, fg_ref) = refs[11:20]
    (dg_hbm, cot_hbm) = refs[20:22]
    (ge_ref, gnode_ref, ows_ref, own_ref, owe_ref, owm_ref, owu_ref, owx_ref, owc_ref, ovec_ref) = refs[22:32]
    (cot, tabt, we, gt, gbs, gen, gta, gtab, dgbuf, gown, first_n, first_e) = refs[32:44]
    (ret, gnp, gbuf, gnr, zown, zmean, actf, gexf, fif, vec, vz, vp) = refs[44:56]
    rest = list(refs[56:-4])
    ss, rs, ls, ds = refs[-4:]
    p, h, line, plane = place(groups, parts)
    nres, dn = gm_ref.shape
    cap = sid_ref.shape[2]
    slots, cw, _ = e1_ref.shape
    rp = nres // parts
    part = dn // parts
    units = w_ref.shape[2]
    tabn = tab_ref.shape[0]
    levels = groups.bit_length() - 1
    mine = pl.ds(pl.multiple_of(h * rp, rp), rp)
    asked = [lax.rem(p + groups - i, groups) for i in range(groups)]
    home = pl.ds(pl.multiple_of(nres + p * cap, 16), cap)

    def take(count):
        taken = rest[:count]
        del rest[:count]
        return taken

    net = Net(ss, rs)
    plan = Plan()
    load = pltpu.make_async_copy(cot_hbm, cot, ls.at[0])

    def fetch(i):
        return pltpu.make_async_copy(dg_hbm.at[lax.rem(i + 1, parts)], dgbuf.at[i % 2], ds.at[i % 2])

    load.start()
    fetch(0).start()

    zsum = {name: take(1)[0] for name in ("neigh", "edge")}
    chunk_sums = {}
    line_copies = {"neigh": {}, "edge": {}}
    own_total = {}
    for c in range(parts):
        for name, source, order in (("neigh", first_n, 0), ("edge", first_e, 1)):
            got = take(2 * levels)
            if c:
                line_copies[name][c] = net.make(got[-1].at[0], zsum[name].at[c], line[c])

            def done(acc, name=name, c=c):
                if c:
                    line_copies[name][c].start()
                else:
                    own_total[name] = acc

            chunk_sums[name, c] = PlaneSum(
                net, p, h, groups, order, source.at[pl.ds(c, 1)], got[:levels], got[levels:], done
            )
    got = take(2 * levels)
    zupd = take(1)[0]
    update_line = [net.make(got[-1].at[i], zupd.at[i], line[i]) for i in range(1, parts)]

    def update_done(acc):
        start(update_line)

    def update_finish():
        arrived(update_line)
        total = update_sum.acc[-1][0].astype(F32)
        for i in range(1, parts):
            total = total + zupd[i].astype(F32)
        owu_ref[...] = total

    update_sum = PlaneSum(net, p, h, groups, 1, gwu_ref, got[:levels], got[levels:], update_done)

    def unit_sum(order, out):
        source = take(1)[0]
        got = take(2 * levels)

        def done(acc):
            out[...] = acc[0]

        def fill(value):
            value = value.astype(BF)
            rows = value.shape[0] // groups
            for s in range(groups):
                source[0, s // 2, s % 2] = value[s * rows : (s + 1) * rows, :]

        item = PlaneSum(net, p, h, groups, order, source, got[:levels], got[levels:], done)
        return fill, item.steps()

    fill_self, steps_self = unit_sum(0, ows_ref)
    fill_message, steps_message = unit_sum(1, owm_ref)
    fill_expand, steps_expand = unit_sum(0, owx_ref)
    fill_contract, steps_contract = unit_sum(1, owc_ref)
    ret_copies = [
        net.make(
            gtab.at[pl.ds(pl.multiple_of(nres + lax.rem(p + i, groups) * cap, 16), cap), :],
            ret.at[i],
            plane[i],
        )
        for i in range(1, groups)
    ]
    own_copies = [net.make(gown.at[i], zown.at[i], line[i]) for i in range(1, parts)]
    mean_copies = [net.make(mean_ref.at[i], zmean.at[i], line[i]) for i in range(1, parts)]
    ffn_copies = []
    for i in range(1, parts):
        ffn_copies.append(net.make(act_ref.at[i], actf.at[mine, :], line[i]))
        ffn_copies.append(net.make(gex_ref.at[i], gexf.at[mine, :], line[i]))
        ffn_copies.append(net.make(fi_ref, fif.at[mine, :], line[i]))
    row_copies = [
        net.make(
            gnp.at[pl.ds(pl.multiple_of(lax.rem(h + i, parts) * rp, rp), rp), :],
            gbuf.at[i],
            line[i],
        )
        for i in range(1, parts)
    ]
    node_copies = [
        net.make(gnr.at[lax.rem(h + i, parts)], gnode_ref.at[mine, :], line[i])
        for i in range(1, parts)
    ]
    vec_line = [net.make(vec, vz.at[i], line[i]) for i in range(1, parts)]
    vec_plane = [net.make(vp.at[0], vp.at[i], plane[i]) for i in range(1, groups)]

    greet(line[1:] + plane[1:])
    start(ffn_copies)
    update_sum.step(0)
    start(mean_copies)
    actf[mine, :] = act_ref[0]
    gexf[mine, :] = gex_ref[0]
    fif[mine, :] = fi_ref[...]
    tabt[...] = tab_ref[...].T
    gen[...] = jnp.zeros_like(gen)
    gta[...] = jnp.zeros_like(gta)

    def ffn_sums():
        arrived(ffn_copies)
        fill_expand(tn(fif[...], gexf[...]))
        fill_contract(tn(cf_ref[...], actf[...]))

    def message_sums():
        value = mean_ref[0].astype(F32)
        arrived(mean_copies)
        for i in range(1, parts):
            value = value + zmean[i].astype(F32)
        fill_message(tn(gm_ref[...], value.astype(BF).T))

    plan.active.append(update_sum.steps()[1:] + [update_finish])
    for i in range(parts):
        plan.advance(("early", i))
        if i == min(1, parts - 1):
            plan.note(("early", i), message_sums)
            plan.add(("early", i), steps_message)
        slot = (i + 1) % parts
        if slot:
            plan.note(("late", i), own_copies[slot - 1].start)
            plan.advance(("late", i))
            for name in ("neigh", "edge"):
                plan.add(("late", i), chunk_sums[name, slot].steps())
        if i == 0:
            plan.note(("late", i), ffn_sums)
            plan.add(("late", i), steps_expand)
            plan.add(("late", i), steps_contract)
    plan.advance(("tail", 0))
    for name in ("neigh", "edge"):
        plan.add(("tail", 0), chunk_sums[name, 0].steps())
    plan.add(("tail", 1), steps_self)
    tail = 2
    while plan.active:
        plan.advance(("tail", tail))
        tail += 1

    def chunk(i, _):
        c = lax.rem(i + 1, parts)

        @pl.when(i + 1 < parts)
        def _():
            fetch(i + 1).start()

        gt[...] = nt(w_ref[c, MESSAGE], gm_ref[...]) * inv_ref[...]
        we[...] = w_ref[c, PAIR, :, :256].T[:cw]
        fetch(i).wait()
        raw = nn(w_ref[c, PAIR, :, 256 : 256 + cw], gup[...])
        g = ((raw + jnp.concatenate([gt[...]] * slots, axis=1)) * dgbuf[i % 2].astype(F32)).astype(BF)
        gbs[...] = g
        gen[...] += nn(we[...], g)
        for k in range(parts):

            @pl.when(i == k)
            def _():
                plan.run(("early", k))

        total = nt(a_ref[: tabn + nres + cw, :], gbs[...])
        gp = total[:tabn].astype(BF)
        go = total[tabn : tabn + nres].astype(BF)
        gown[c] = go
        edge_value = total[tabn + nres :].astype(BF)
        neigh_value = nn(tabt[...], gp).astype(BF)
        for s in range(groups):
            n, m = dn // groups, cw // groups
            first_n[c, s // 2, s % 2] = neigh_value[s * n : (s + 1) * n, :]
            first_e[c, s // 2, s % 2] = edge_value[s * m : (s + 1) * m, :]
        gta[...] += nn(gp, w_ref[c, NEIGH])
        gta[:nres, :] += nn(go, w_ref[c, SELF])
        for k in range(parts):

            @pl.when(i == k)
            def _():
                plan.run(("late", k))

        return 0

    lax.fori_loop(0, parts, chunk, 0)
    gtab[...] = gta[...].astype(BF)
    start(ret_copies)
    plan.run(("tail", 0))
    value = gown[0].astype(F32)
    arrived(own_copies)
    for i in range(1, parts):
        value = value + zown[i].astype(F32)
    fill_self(tn(tab_ref[:nres, :], value.astype(BF)))
    plan.run(("tail", 1))
    ids = lax.broadcasted_iota(jnp.int32, (nres, cap), 0)
    total = gta[:nres, :]
    for i in range(groups):
        if i:
            ret_copies[i - 1].wait_recv()
            rows = ret[i]
        else:
            rows = gtab[home, :]
        chosen = jnp.where(ids == sid_ref[asked[i]], 1.0, 0.0).astype(BF)
        total = total + nn(chosen, rows)
    gnp[...] = total.astype(BF)
    start(row_copies)
    load.wait()
    edge_gain = jnp.zeros((cw, nres), F32)
    for k in range(slots):
        unit, scaling = normalize(e1_ref[k].astype(F32), 0)
        grad = gen[:, k * nres : (k + 1) * nres]
        edge_gain = edge_gain + grad * unit
        ge_ref[k] = cot[k].astype(F32) + norm_back(grad, unit, scaling, egain_ref[...], 0)
    unit_full, _scale = normalize(xf_ref[...].astype(F32), 1)
    vec[:, :dn] = jnp.sum(total * unit_full, 0, keepdims=True)
    vec[:, dn : 2 * dn] = fg_ref[...]
    vec[:, 2 * dn :] = jnp.sum(edge_gain.T, 0, keepdims=True)
    start(vec_line)
    plan.run(("tail", 2))
    arrived(row_copies)
    g_normed = gnp[mine, :].astype(F32)
    for i in range(1, parts):
        g_normed = g_normed + gbuf[i].astype(F32)
    unit_node, scaling = normalize(x1_ref[...].astype(F32), 1)
    rows = gmid_ref[...] + norm_back(g_normed, unit_node, scaling, ngain_ref[...], 1)
    for c in range(parts):
        gnr[c] = rows[:, c * part : (c + 1) * part]
    start(node_copies)
    gnode_ref[mine, :] = gnr[h]
    arrived(vec_line)
    value = vec[...]
    for i in range(1, parts):
        value = value + vz[i]
    vp[0] = value
    start(vec_plane)
    for k in range(3, tail):
        plan.run(("tail", k))
    for name, out in (("neigh", own_ref), ("edge", owe_ref)):
        total = own_total[name][0].astype(F32)
        for i in range(1, parts):
            line_copies[name][i].wait_recv()
            total = total + zsum[name][i].astype(F32)
        out[...] = total
    arrived(vec_plane)
    value = vp[0]
    for i in range(1, groups):
        value = value + vp[i]
    ovec_ref[...] = value
    arrived(node_copies)
    net.finish()


def third(groups, parts, w, a, gup, tab, sid, x1, xf, e1, egain, inv, ngain, gm, gmid, cf, mean, gwu, act, gex, fi, fg, dg, cot):
    nres, dn = gm.shape
    cap = sid.shape[2]
    units = w.shape[2]
    slots, cw, _ = e1.shape
    rows = slots * nres
    tabn = tab.shape[0]
    rp = nres // parts
    part = dn // parts
    levels = groups.bit_length() - 1
    wide, narrow = dn // groups, cw // groups
    half = groups // 2
    S, V = jax.ShapeDtypeStruct, pltpu.VMEM
    total = 2 * dn + cw
    scratch = [
        V(e1.shape, BF),
        V((dn, tabn), BF),
        V((cw, units), BF),
        V((units, nres), F32),
        V((units, rows), BF),
        V((cw, rows), F32),
        V((tabn, dn), F32),
        V((tabn, dn), BF),
        V((2, units, rows), BF),
        V((parts, nres, units), BF),
        V((parts, half, 2, wide, units), BF),
        V((parts, half, 2, narrow, units), BF),
        V((groups, cap, dn), BF),
        V((nres, dn), BF),
        V((parts, rp, dn), BF),
        V((parts, rp, part), F32),
        V((parts, nres, units), BF),
        V((parts, units, nres), BF),
        V((nres, units), BF),
        V((nres, units), BF),
        V((nres, dn), BF),
        V((1, total), F32),
        V((parts, 1, total), F32),
        V((groups, 1, total), F32),
    ]
    scratch += [V((parts, wide, units), BF), V((parts, narrow, units), BF)]
    for c in range(parts):
        scratch += plane_scratch(groups, 1, wide, units, 0, BF)
        scratch += plane_scratch(groups, 1, narrow, units, 1, BF)
    scratch += plane_scratch(groups, parts, narrow, units, 1, BF)
    scratch += [V((parts, narrow, units), BF)]
    for order in (0, 1, 0, 1):
        scratch += [V((1, half, 2, wide, units), BF)]
        scratch += plane_scratch(groups, 1, wide, units, order, F32)
    copies = 2 * (groups - 1) + (parts - 1) * (2 + 1 + 1 + 1 + 3 + 1 + 1 + 1) + levels * (2 * parts + 5)
    scratch += [
        pltpu.SemaphoreType.DMA((copies,)),
        pltpu.SemaphoreType.DMA((copies,)),
        pltpu.SemaphoreType.DMA((1,)),
        pltpu.SemaphoreType.DMA((2,)),
    ]
    vm, anyspace = pl.BlockSpec(memory_space=pltpu.VMEM), pl.BlockSpec(memory_space=pltpu.MemorySpace.HBM)
    gwu = gwu.reshape(parts, half, 2, narrow, units)
    return pl.pallas_call(
        functools.partial(third_kernel, groups, parts),
        in_specs=[vm] * 20 + [anyspace] * 2,
        out_specs=[vm] * 10,
        out_shape=[
            S(e1.shape, F32),
            S((nres, part), F32),
            S((wide, units), F32),
            S((wide, units), F32),
            S((narrow, units), F32),
            S((wide, units), F32),
            S((narrow, units), F32),
            S((wide, units), F32),
            S((wide, units), F32),
            S((1, total), F32),
        ],
        scratch_shapes=scratch,
        compiler_params=pltpu.CompilerParams(
            collective_id=2, has_side_effects=True, vmem_limit_bytes=42 << 20
        ),
        name="gradients",
    )(w, a, gup, tab, sid, x1, xf, e1, egain, inv, ngain, gm, gmid, cf, mean, gwu, act, gex, fi, fg, dg, cot)


def per_device(
    node_state,
    edge_state,
    node_gain,
    edge_gain,
    ffn_gain,
    w_self,
    w_neigh,
    w_edge,
    w_message,
    w_update,
    w_expand,
    w_contract,
    neighbours,
    requests,
    counts,
    node_cotangent,
    edge_cotangent,
):
    groups, parts = lax.axis_size("res"), lax.axis_size("hid")
    nres, slot_count = neighbours.shape
    slot_part, cw = edge_state.shape[1:]
    h, p = lax.axis_index("hid"), lax.axis_index("res")
    live = lax.broadcasted_iota(jnp.int32, (nres, slot_count), 1) < counts[:, None]
    entry = jnp.where(live, neighbours, -1)
    entry = lax.dynamic_slice_in_dim(entry, h * slot_part, slot_part, 1).T[:, None, :]
    inverse = 1.0 / counts.astype(F32)[None]
    ngain, egain, fgain = node_gain[None], edge_gain[:, None], ffn_gain[None]
    edges = edge_state.transpose(1, 2, 0)
    cot = edge_cotangent.transpose(1, 2, 0)
    w, wf, tab, x1, xf, e1, cf, sid = first(
        groups,
        parts,
        node_state,
        node_cotangent,
        requests[0][:, None, :],
        entry,
        egain,
        inverse,
        ngain,
        fgain,
        edges,
        [w_neigh, w_self, w_edge, w_update.T, w_message, w_expand, w_contract],
    )
    a, gup, dg, mean, gwu, e2, node_two, gm, gmid, act, gex, fi, fg = second(
        groups, parts, w, wf, tab, x1, e1, entry, egain, inverse, fgain, cf, cot
    )
    ge, gnode, gws, gwn, gwe, gwm, gwu, gwx, gwc, vec = third(
        groups, parts, w, a, gup, tab, sid, x1, xf, e1, egain, inverse, ngain, gm, gmid, cf, mean, gwu, act, gex, fi, fg, dg, cot
    )
    dn = ngain.shape[1]
    cut = lambda begin, size: lax.dynamic_slice_in_dim(
        vec[0, begin : begin + size], p * (size // groups), size // groups, 0
    )
    return (
        node_two,
        e2.transpose(2, 0, 1),
        gnode,
        ge.transpose(2, 0, 1),
        cut(0, dn),
        cut(2 * dn, cw),
        cut(dn, dn),
        gws,
        gwn,
        gwe,
        gwm.T,
        gwu.T,
        gwx,
        gwc.T,
    )


def solution(mesh):
    return jax.shard_map(
        per_device,
        mesh=mesh,
        in_specs=(
            P("res", "hid"),
            P("res", "hid", None),
            P(),
            P(),
            P(),
            P(None, "hid"),
            P(None, "hid"),
            P(None, "hid"),
            P("hid", None),
            P("hid", None),
            P(None, "hid"),
            P("hid", None),
            P("res", None),
            P("res", None, None),
            P("res"),
            P("res", "hid"),
            P("res", "hid", None),
        ),
        out_specs=(
            P("res", "hid"),
            P("res", "hid", None),
            P("res", "hid"),
            P("res", "hid", None),
            P("res"),
            P("res"),
            P("res"),
            P("res", "hid"),
            P("res", "hid"),
            P("res", "hid"),
            P("hid", "res"),
            P("hid", "res"),
            P("res", "hid"),
            P("hid", "res"),
        ),
        check_vma=False,
    )
```

```python
import functools

import jax
import jax.numpy as jnp
from jax import lax
from jax.experimental import pallas as pl
from jax.experimental.pallas import tpu as pltpu
from jax.sharding import PartitionSpec as P

F32, BF = jnp.float32, jnp.bfloat16
EPSILON = 1e-05
TANH_SCALE = 0.7978845608028654
TANH_CUBE = 0.044715
MESH = pl.DeviceIdType.MESH
NEIGH, PAIR, SELF, MESSAGE = range(4)
EXPAND, CONTRACT = range(2)


def contract(a, b, dim_a, dim_b):
    return lax.dot_general(
        a, b, (((dim_a,), (dim_b,)), ((), ())), preferred_element_type=F32
    )


def nn(a, b):
    return contract(a, b, 1, 0)


def nt(a, b):
    return contract(a, b, 1, 1)


def tn(a, b):
    return contract(a, b, 0, 0)


def normalize(values, axis):
    centred = values - jnp.mean(values, axis, keepdims=True)
    scaling = lax.rsqrt(jnp.mean(centred * centred, axis, keepdims=True) + EPSILON)
    return centred * scaling, scaling


def norm_back(grad, unit, scaling, gain, axis):
    scaled = grad * gain
    return scaling * (
        scaled
        - jnp.mean(scaled, axis, keepdims=True)
        - unit * jnp.mean(scaled * unit, axis, keepdims=True)
    )


def gelu(x):
    return (0.5 * x) * (1.0 + jnp.tanh(x * (TANH_SCALE + TANH_SCALE * TANH_CUBE * (x * x))))


def gelu_pair(x):
    square = x * x
    bent = jnp.tanh(x * (TANH_SCALE + TANH_SCALE * TANH_CUBE * square))
    half = 0.5 * x
    slope = 0.5 + 0.5 * bent + half * (1.0 - bent * bent) * (
        TANH_SCALE + 3 * TANH_SCALE * TANH_CUBE * square
    )
    return half + half * bent, slope


class Net:
    def __init__(self, send_sems, recv_sems):
        self.send_sems, self.recv_sems, self.count, self.sent = send_sems, recv_sems, 0, []

    def make(self, src, dst, device):
        k = self.count
        self.count += 1
        copy = pltpu.make_async_remote_copy(
            src_ref=src,
            dst_ref=dst,
            send_sem=self.send_sems.at[k],
            recv_sem=self.recv_sems.at[k],
            device_id=device,
            device_id_type=MESH,
        )
        self.sent.append(copy)
        return copy

    def push(self, src, dst, device):
        copy = self.make(src, dst, device)
        copy.start()
        return copy

    def finish(self):
        for copy in self.sent:
            copy.wait_send()


def start(copies):
    for copy in copies:
        copy.start()


def arrived(copies):
    for copy in copies:
        copy.wait_recv()


def flip_bit(index, bit):
    step = 1 << bit
    return index + step - 2 * step * ((index // step) % 2)


def greet(devices):
    barrier = pltpu.get_barrier_semaphore()
    for device in devices:
        pl.semaphore_signal(barrier, inc=1, device_id=device, device_id_type=MESH)
    pl.semaphore_wait(barrier, len(devices))


def place(groups, parts):
    p, h = lax.axis_index("res"), lax.axis_index("hid")
    line = [None] + [(p, lax.rem(h + i, parts)) for i in range(1, parts)]
    plane = [None] + [(lax.rem(p + i, groups), h) for i in range(1, groups)]
    return p, h, line, plane


class Rows:
    def __init__(self, net, p, groups, plane, nres, cap, tab_ref, rows_buf):
        self.mine = pl.ds(pl.multiple_of(nres + p * cap, 16), cap)
        self.asked = [lax.rem(p + i, groups) for i in range(groups)]
        self.nres, self.cap, self.tab, self.buf = nres, cap, tab_ref, rows_buf
        self.copies = [
            net.make(rows_buf.at[i], tab_ref.at[self.mine, :], plane[i]) for i in range(1, groups)
        ]

    def send(self, normed, sid_ref):
        ids = lax.broadcasted_iota(jnp.int32, (self.nres, self.cap), 0)
        self.tab[: self.nres, :] = normed
        for i, q in enumerate(self.asked):
            chosen = jnp.where(ids == sid_ref[q], 1.0, 0.0).astype(BF)
            rows = tn(chosen, normed).astype(BF)
            if i == 0:
                self.tab[self.mine, :] = rows
            else:
                self.buf[i] = rows
                self.copies[i - 1].start()


class Gather:
    def __init__(self, net, p, h, groups, parts, edge_full, node_full, depth):
        self.levels = groups.bit_length() - 1
        low, half = p % 2, p // 2
        turned = sum(
            ((half // (1 << b)) % 2) * (1 << (self.levels - 2 - b)) for b in range(self.levels - 1)
        )
        starts = [low * (groups // 2) + half, low * (groups // 2) + turned]
        rows = depth // groups
        back = [(p, lax.rem(h + parts - i, parts)) for i in range(parts)]
        units = [(edge_full, w, r) for r in range(1, parts) for w in (NEIGH, PAIR, SELF)]
        self.chunk_slots = [0] + [(3 * k - 1) // 2 + self.levels + 1 for k in range(1, parts)]
        for full, w in ((edge_full, MESSAGE), (node_full, EXPAND), (node_full, CONTRACT)):
            units += [(full, w, r) for r in range(1, parts)]
        count = 3 * (parts - 1)
        self.weight_slots = [
            (count + k * (parts - 1) - 1) // 2 + self.levels + 1 for k in range(1, 4)
        ]
        self.batches = [[[] for _ in range(self.levels + 1)] for _ in range((len(units) + 1) // 2)]
        for u, (full, w, r) in enumerate(units):
            stages = self.batches[u // 2]
            turn = u % 2
            begin = starts[turn]
            own = pl.ds(pl.multiple_of(begin * rows, rows), rows)
            stages[0].append(net.make(full.at[0, w, own, :], full.at[r, w, own, :], back[r]))
            for level in range(self.levels):
                if level == self.levels - 1:
                    bit = 0
                else:
                    bit = 1 + (level if turn == 0 else self.levels - 2 - level)
                span = rows << level
                held = (begin // (1 << level)) * span
                view = full.at[r, w, pl.ds(pl.multiple_of(held, span), span), :]
                stages[level + 1].append(net.make(view, view, (flip_bit(p, bit), h)))
        self.slots = len(self.batches) + self.levels + 1

    def turn(self, slot):
        for stage in range(self.levels + 1, -1, -1):
            b = slot - stage
            if 0 <= b < len(self.batches):
                if stage:
                    arrived(self.batches[b][stage - 1])
                if stage <= self.levels:
                    start(self.batches[b][stage])


def bits_of(index, levels):
    return tuple((index >> b) & 1 for b in range(levels - 1, -1, -1))


def fill_rows(ref, value, lead):
    levels = len(ref.shape) - 3
    rows = ref.shape[-2]
    for s in range(1 << levels):
        ref[(lead,) + bits_of(s, levels)] = value[s * rows : (s + 1) * rows, :]


class PlaneSum:
    def __init__(self, net, p, h, levels, order, source, recv, done):
        self.levels, self.source, self.recv, self.done = levels, source, recv, done
        own = [(p // (1 << bit)) % 2 for bit in range(levels)]
        self.fixed, self.copies = [], []
        fixed = {}
        for level in range(levels):
            bit = 0 if level == 0 else (level if order == 0 else levels - level)
            other = dict(fixed)
            other[bit] = 1 - own[bit]
            fixed = dict(fixed)
            fixed[bit] = own[bit]
            self.fixed.append(fixed)
            self.copies.append(
                net.make(source.at[self.index(other)], recv[level], (flip_bit(p, bit), h))
            )

    def index(self, fixed):
        return (slice(None),) + tuple(
            fixed.get(bit, slice(None)) for bit in range(self.levels - 1, -1, -1)
        )

    def held(self):
        return self.source.at[self.index(self.fixed[-1])]

    def steps(self):
        return [functools.partial(self.step, level) for level in range(self.levels + 1)]

    def step(self, level):
        if level:
            k = level - 1
            self.copies[k].wait_recv()
            free = [bit for bit in range(self.levels) if bit not in self.fixed[k]]
            for n in range(1 << len(free)):
                fixed = dict(self.fixed[k])
                for j, bit in enumerate(free):
                    fixed[bit] = (n >> j) & 1
                at = self.index(fixed)
                got = (slice(None),) + tuple(fixed[bit] for bit in reversed(free))
                total = self.source[at].astype(F32) + self.recv[k][got].astype(F32)
                if level == self.levels and self.done(total):
                    continue
                self.source[at] = total.astype(BF)
        if level < self.levels:
            self.copies[level].start()


def build_inputs(a_ref, edges, v_ref, egain, tabn):
    slots, cw, nres = edges.shape
    index = lax.broadcasted_iota(jnp.int32, (tabn, nres), 0)
    own = lax.broadcasted_iota(jnp.int32, (nres, nres), 0) == lax.broadcasted_iota(
        jnp.int32, (nres, nres), 1
    )
    own = jnp.where(own, 1.0, 0.0).astype(BF)
    height = a_ref.shape[0]

    def one(k, _):
        cs = pl.ds(pl.multiple_of(k * nres, nres), nres)
        a_ref[:tabn, cs] = jnp.where(index == v_ref[k], 1.0, 0.0).astype(BF)
        a_ref[tabn : tabn + nres, cs] = own
        unit, _scale = normalize(edges[k].astype(F32), 0)
        a_ref[tabn + nres : tabn + nres + cw, cs] = (unit * egain).astype(BF)
        a_ref[tabn + nres + cw :, cs] = jnp.zeros((height - tabn - nres - cw, nres), BF)
        return 0

    lax.fori_loop(0, slots, one, 0)


def edge_chunk(c, w_ref, tab, a_ref, bt, wut, v_ref, upd, mean, inverse, cw, pause, second=None):
    tabn, nres = tab.shape[0], mean.shape[-1]
    slots = a_ref.shape[1] // nres
    bt[:, :tabn] = nt(w_ref[c, NEIGH], tab[...]).astype(BF)
    bt[:, tabn : tabn + nres] = nt(w_ref[c, SELF], tab[:nres, :]).astype(BF)
    bt[:, tabn + nres :] = w_ref[c, PAIR, :, :256]
    wut[...] = w_ref[c, PAIR, :, 256:].T[:cw]
    before = nn(bt[...], a_ref[...])
    pause()
    if second is None:
        hidden = gelu(before)
    else:
        dg, gup, gwu = second
        hidden, slope = gelu_pair(before)
    total, kept = None, []
    for k in range(slots):
        cs = slice(k * nres, (k + 1) * nres)
        live = (v_ref[k] >= 0).astype(F32)
        part = hidden[:, cs] * live
        total = part if total is None else total + part
        kept.append(part.astype(BF))
        if second is not None:
            dg[:, cs] = (slope[:, cs] * live).astype(BF)
    mean[c] = (total * inverse).astype(BF)
    kept = jnp.concatenate(kept, axis=1)
    upd[...] += nn(wut[...], kept)
    if second is not None:
        fill_rows(gwu, nt(gup[...], kept).astype(BF), c)


def message_part(w_ref, mean, parts):
    total = None
    for c in range(parts):
        term = tn(mean[c], w_ref[c, MESSAGE])
        total = term if total is None else total + term
    return total.astype(BF)


def add_update(edges, upd, out):
    slots, _, nres = edges.shape
    for k in range(slots):
        out[k] = (edges[k].astype(F32) + upd[:, k * nres : (k + 1) * nres]).astype(BF)


class Plan:
    def __init__(self):
        self.points, self.active = {}, []

    def add(self, point, steps, first_now=True):
        steps = list(steps)
        if first_now:
            self.note(point, steps.pop(0))
        if steps:
            self.active.append(steps)

    def note(self, point, step):
        self.points.setdefault(point, []).append(step)

    def advance(self, point):
        for steps in self.active:
            self.note(point, steps.pop(0))
        self.active = [steps for steps in self.active if steps]

    def run(self, point):
        for step in self.points.get(point, ()):
            step()


def plane_scratch(groups, lead, rows, units, order, last):
    recv, acc = [], []
    count = groups
    while count > 1:
        count //= 2
        recv.append(pltpu.VMEM((lead, count, rows, units), BF))
        if count == 1:
            acc.append(pltpu.VMEM((lead, rows, units), last))
        elif order == 0:
            acc.append(pltpu.VMEM((lead, count // 2, 2, rows, units), BF))
        else:
            acc.append(pltpu.VMEM((lead, 2, count // 2, rows, units), BF))
    return recv + acc


def layer_kernel(groups, parts, *refs):
    (node_ref, ncot_ref, req_ref, v_ref, egain_ref, inv_ref, ngain_ref, fgain_ref) = refs[:8]
    (edges_hbm, ecot_hbm, wn_hbm, ws_hbm, we_hbm, wu_hbm, wm_hbm, wx_hbm, wc_hbm) = refs[8:17]
    (nn_ref, gnode_ref, ows_ref, own_ref, owe_ref, owm_ref, owu_ref, owx_ref, owc_ref, ovec_ref) = refs[17:27]
    (e2_hbm, ge_hbm, dg_hbm) = refs[27:30]
    refs = list(refs[30:])

    def take(count):
        taken = refs[:count]
        del refs[:count]
        return taken

    w_ref, wf_ref, nbuf, cbuf, nfull, cf, xrows, x1, xf, sid = take(10)
    rows0, rows1, tab0, tab1, tabt, edges, e1, cot, a_ref, bt = take(10)
    wut, upd, mean, msg0, msg1, mbuf0, mbuf1, gup, dgbuf, slopes = take(10)
    nsp, gm, gmid, act, gex, fi, fg, gt, gta, gtab = take(10)
    gown, first_n, first_e, gwu, zown, zmean, actf, gexf, fif, ret = take(10)
    gnp, gbuf, gnr, vec, vz, vp, zn, ze, zu = take(9)
    ss, rs, ls, ds, os_ = refs[-5:]
    p, h, line, plane = place(groups, parts)
    nres, part = node_ref.shape
    dn = part * parts
    cap = req_ref.shape[2]
    slots, cw, _ = edges.shape
    rp = nres // parts
    units = w_ref.shape[2]
    tabn = tab0.shape[0]
    levels = groups.bit_length() - 1
    mine = pl.ds(pl.multiple_of(h * rp, rp), rp)
    home = pl.ds(pl.multiple_of(nres + p * cap, 16), cap)
    asked = [lax.rem(p + groups - i, groups) for i in range(groups)]
    inverse = inv_ref[...]
    egain = egain_ref[...]

    raw = [a_ref.at[:dn, k * units : (k + 1) * units] for k in range(3)]
    raw_e = [a_ref.at[dn + k * cw : dn + (k + 1) * cw, :units] for k in range(2)]
    loads = [
        pltpu.make_async_copy(src, dst, ls.at[k])
        for k, (src, dst) in enumerate(
            (
                (wn_hbm, raw[0]),
                (we_hbm, raw_e[0]),
                (wu_hbm, raw_e[1]),
                (ws_hbm, raw[1]),
                (wx_hbm, raw[2]),
                (edges_hbm, edges),
                (wm_hbm, w_ref.at[0, MESSAGE]),
                (wc_hbm, wf_ref.at[0, CONTRACT]),
                (ecot_hbm, cot),
            )
        )
    ]
    start(loads)
    net = Net(ss, rs)

    def to_parts(pair):
        copies = []
        for i in range(1, parts):
            src, dst = pair(i, lax.rem(h + i, parts))
            copies.append(net.make(src, dst, line[i]))
        return copies

    def rows_of(other):
        return pl.ds(pl.multiple_of(other * rp, rp), rp)

    node_copies = to_parts(lambda i, o: (node_ref, nbuf.at[h]))
    req_copies = [
        net.make(req_ref.at[lax.rem(p + i, groups)], sid.at[p], plane[i]) for i in range(1, groups)
    ]
    ncot_copies = to_parts(lambda i, o: (ncot_ref, cbuf.at[h]))
    rows_first = Rows(net, p, groups, plane, nres, cap, tab0, rows0)
    rows_next = Rows(net, p, groups, plane, nres, cap, tab1, rows1)
    message0 = to_parts(lambda i, o: (msg0.at[rows_of(o), :], mbuf0.at[i]))
    message1 = to_parts(lambda i, o: (msg1.at[rows_of(o), :], mbuf1.at[i]))
    x1_copies = to_parts(lambda i, o: (x1, xf.at[mine, :]))
    gather = Gather(net, p, h, groups, parts, w_ref, wf_ref, units)
    gm_copies = to_parts(lambda i, o: (gm.at[mine, :], gm.at[mine, :]))
    nn_copies = to_parts(lambda i, o: (nsp.at[o], nn_ref.at[mine, :]))
    ret_copies = [
        net.make(
            gtab.at[pl.ds(pl.multiple_of(nres + lax.rem(p + i, groups) * cap, 16), cap), :],
            ret.at[i],
            plane[i],
        )
        for i in range(1, groups)
    ]
    own_copies = to_parts(lambda i, o: (gown.at[i], zown.at[i]))
    mean_copies = to_parts(lambda i, o: (mean.at[i], zmean.at[i]))
    act_copies = to_parts(lambda i, o: (act.at[i], actf.at[mine, :]))
    gex_copies = to_parts(lambda i, o: (gex.at[i], gexf.at[mine, :]))
    fi_copies = to_parts(lambda i, o: (fi, fif.at[mine, :]))
    row_copies = to_parts(lambda i, o: (gnp.at[rows_of(o), :], gbuf.at[i]))
    gnode_copies = to_parts(lambda i, o: (gnr.at[o], gnode_ref.at[mine, :]))
    vec_line = to_parts(lambda i, o: (vec, vz.at[i]))
    vec_plane = [net.make(vp.at[0], vp.at[i], plane[i]) for i in range(1, groups)]

    own_total = {}
    chunk_sums, chunk_line = {}, {}
    for c in range(parts):
        for name, source, order, landing in (("neigh", first_n, 0, zn), ("edge", first_e, 1, ze)):
            recv = take(levels)

            def done(total, name=name, c=c):
                if not c:
                    own_total[name] = total
                return not c

            item = PlaneSum(net, p, h, levels, order, source.at[pl.ds(c, 1)], recv, done)
            steps = item.steps()
            if c:
                copy = net.make(item.held().at[0], landing.at[c], line[c])
                chunk_line[name, c] = copy
                last = steps.pop()

                def send_on(last=last, copy=copy):
                    last()
                    copy.start()

                steps.append(send_on)
            chunk_sums[name, c] = steps
    update_sum = PlaneSum(net, p, h, levels, 1, gwu, take(levels), lambda total: False)
    update_line = to_parts(lambda i, o: (update_sum.held().at[i], zu.at[i]))
    update_steps = update_sum.steps()

    def update_send():
        start(update_line)

    def update_finish():
        arrived(update_line)
        total = update_sum.held()[0].astype(F32)
        for i in range(1, parts):
            total = total + zu[i].astype(F32)
        owu_ref[...] = total

    def unit_sum(order, out):
        source = take(1)[0]

        def done(total):
            out[...] = total[0]
            return True

        item = PlaneSum(net, p, h, levels, order, source, take(levels), done)

        def fill(value):
            fill_rows(source, value.astype(BF), 0)

        return fill, item.steps()

    fill_self, steps_self = unit_sum(0, ows_ref)
    fill_message, steps_message = unit_sum(1, owm_ref)
    fill_expand, steps_expand = unit_sum(0, owx_ref)
    fill_contract, steps_contract = unit_sum(1, owc_ref)

    greet(line[1:] + plane[1:])
    start(node_copies)
    start(req_copies)
    start(ncot_copies)
    nbuf[h] = node_ref[...]
    cbuf[h] = ncot_ref[...]
    sid[p] = req_ref[p]
    loads[0].wait()
    w_ref[0, NEIGH] = raw[0][...].T
    loads[1].wait()
    loads[2].wait()
    w_ref[0, PAIR, :, :cw] = raw_e[0][...].T
    w_ref[0, PAIR, :, cw:256] = jnp.zeros((units, 256 - cw), BF)
    w_ref[0, PAIR, :, 256 : 256 + cw] = raw_e[1][...].T
    w_ref[0, PAIR, :, 256 + cw :] = jnp.zeros((units, 256 - cw), BF)
    gather.turn(0)
    loads[3].wait()
    w_ref[0, SELF] = raw[1][...].T
    arrived(node_copies)
    for c in range(parts):
        nfull[:, c * part : (c + 1) * part] = nbuf[c]
    unit_node, _scale = normalize(nfull[...].astype(F32), 1)
    normed = (unit_node * ngain_ref[...]).astype(BF)
    xrows[...] = nfull[mine, :]
    arrived(req_copies)
    rows_first.send(normed, sid)
    gather.turn(1)
    loads[4].wait()
    wf_ref[0, EXPAND] = raw[2][...].T
    loads[5].wait()
    build_inputs(a_ref, edges, v_ref, egain, tabn)
    gather.turn(2)
    loads[6].wait()
    loads[7].wait()
    arrived(ncot_copies)
    for c in range(parts):
        cf[:, c * part : (c + 1) * part] = cbuf[c]
    upd[...] = jnp.zeros_like(upd)
    gather.turn(3)
    arrived(rows_first.copies)

    slot = 4
    begin_slots, pause_slots = [], []
    for k in range(parts):
        upto = max(slot, gather.chunk_slots[k] + 1) if k else slot
        begin_slots.append(range(slot, upto))
        slot = min(upto + 1, gather.slots)
        pause_slots.append(range(upto, slot))

    def turns(c, table):
        for k in range(parts):
            if len(table[k]):

                @pl.when(c == k)
                def _():
                    for s in table[k]:
                        gather.turn(s)

    def first_chunk(c, _):
        turns(c, begin_slots)
        pause = lambda: turns(c, pause_slots)
        edge_chunk(c, w_ref, tab0, a_ref, bt, wut, v_ref, upd, mean, inverse, cw, pause)
        return 0

    lax.fori_loop(0, parts, first_chunk, 0)
    message_slot, expand_slot, contract_slot = gather.weight_slots
    for s in range(slot, message_slot + 1):
        gather.turn(s)
    slot = max(slot, message_slot + 1)
    msg0[...] = message_part(w_ref, mean, parts)
    start(message0)
    if slot < gather.slots:
        gather.turn(slot)
        slot += 1
    add_update(edges, upd, e1)
    build_inputs(a_ref, e1, v_ref, egain, tabn)
    middle = xrows[...].astype(F32) + msg0[mine, :].astype(F32)
    for i, copy in enumerate(message0):
        copy.wait_recv()
        middle = middle + mbuf0[i + 1].astype(F32)
    unit_ffn, _scale = normalize(middle, 1)
    ffn_input = (unit_ffn * fgain_ref[...]).astype(BF)
    for s in range(slot, expand_slot + 1):
        gather.turn(s)
    slot = max(slot, expand_slot + 1)
    hidden = [gelu(nt(ffn_input, wf_ref[c, EXPAND])).astype(BF) for c in range(parts)]
    for s in range(slot, gather.slots):
        gather.turn(s)
    out = middle
    for c in range(parts):
        out = out + nn(hidden[c], wf_ref[c, CONTRACT])
    out = out.astype(BF)
    x1[...] = out
    xf[mine, :] = out
    start(x1_copies)
    upd[...] = jnp.zeros_like(upd)
    loads[8].wait()
    for k in range(slots):
        live = (v_ref[k] >= 0).astype(F32)
        gup[:, k * nres : (k + 1) * nres] = (cot[k].astype(F32) * live).astype(BF)
    arrived(x1_copies)
    unit_full, _scale = normalize(xf[...].astype(F32), 1)
    rows_next.send((unit_full * ngain_ref[...]).astype(BF), sid)
    arrived(rows_next.copies)

    def save(c):
        return pltpu.make_async_copy(dgbuf.at[c % 2], dg_hbm.at[c], ds.at[c % 2])

    def second_chunk(c, _):
        @pl.when(c >= 2)
        def _():
            save(c - 2).wait()

        edge_chunk(
            c,
            w_ref,
            tab1,
            a_ref,
            bt,
            wut,
            v_ref,
            upd,
            mean,
            inverse,
            cw,
            lambda: None,
            (dgbuf.at[c % 2], gup, gwu),
        )
        save(c).start()
        return 0

    lax.fori_loop(0, parts, second_chunk, 0)
    msg1[...] = message_part(w_ref, mean, parts)
    start(message1)
    update_steps[0]()
    add_update(e1, upd, edges)
    e2_copy = pltpu.make_async_copy(edges, e2_hbm, os_.at[0])
    e2_copy.start()
    tabt[...] = tab1[...].T
    middle = x1[...].astype(F32) + msg1[mine, :].astype(F32)
    for i, copy in enumerate(message1):
        copy.wait_recv()
        middle = middle + mbuf1[i + 1].astype(F32)
    unit_ffn, scaling = normalize(middle, 1)
    ffn_input = (unit_ffn * fgain_ref[...]).astype(BF)
    fi[...] = ffn_input
    cotangent = cf[mine, :]
    g_input = jnp.zeros((rp, dn), F32)
    for c in range(parts):
        active, slope = gelu_pair(nt(ffn_input, wf_ref[c, EXPAND]))
        act[c] = active.astype(BF)
        g_expand = (nt(cotangent, wf_ref[c, CONTRACT]) * slope).astype(BF)
        gex[c] = g_expand
        g_input = g_input + nn(g_expand, wf_ref[c, EXPAND])
    g_middle = cotangent.astype(F32) + norm_back(g_input, unit_ffn, scaling, fgain_ref[...], 1)
    gm[mine, :] = g_middle.astype(BF)
    start(gm_copies)
    gmid[...] = g_middle
    fg[...] = jnp.sum(g_input * unit_ffn, 0, keepdims=True)
    out = middle
    for c in range(parts):
        out = out + nn(act[c], wf_ref[c, CONTRACT])
    out = out.astype(BF)
    for c in range(parts):
        nsp[c] = out[:, c * part : (c + 1) * part]
    start(nn_copies)
    nn_ref[mine, :] = nsp[h]
    actf[mine, :] = act[0]
    gexf[mine, :] = gex[0]
    fif[mine, :] = fi[...]
    upd[...] = jnp.zeros_like(upd)
    gta[...] = jnp.zeros_like(gta)
    for c in range(max(parts - 2, 0), parts):
        save(c).wait()
    arrived(gm_copies)
    start(act_copies)
    start(gex_copies)
    start(fi_copies)
    start(mean_copies)

    def ffn_sums():
        arrived(act_copies + gex_copies + fi_copies)
        fill_expand(tn(fif[...], gexf[...]))
        fill_contract(tn(cf[...], actf[...]))

    def message_sums():
        value = mean[0].astype(F32)
        arrived(mean_copies)
        for i in range(1, parts):
            value = value + zmean[i].astype(F32)
        fill_message(tn(gm[...], value.astype(BF).T))

    plan = Plan()
    plan.active.append(update_steps[1:] + [update_send, update_finish])
    for i in range(parts):
        plan.advance(("early", i))
        if i == min(1, parts - 1):
            plan.note(("early", i), message_sums)
            plan.add(("early", i), steps_message)
        c = (i + 1) % parts
        if c:
            plan.note(("late", i), own_copies[c - 1].start)
            plan.advance(("late", i))
            for name in ("neigh", "edge"):
                plan.add(("late", i), chunk_sums[name, c])
        if i == 0:
            plan.note(("late", i), ffn_sums)
            plan.add(("late", i), steps_expand)
            plan.add(("late", i), steps_contract)
    plan.advance(("tail", 0))
    for name in ("neigh", "edge"):
        plan.add(("tail", 0), chunk_sums[name, 0])
    plan.add(("tail", 1), steps_self)
    tail = 2
    while plan.active:
        plan.advance(("tail", tail))
        tail += 1

    def fetch(i):
        return pltpu.make_async_copy(dg_hbm.at[lax.rem(i + 1, parts)], dgbuf.at[i % 2], ds.at[i % 2])

    fetch(0).start()
    gen = upd

    def points(i, name):
        for k in range(parts):
            if (name, k) in plan.points:

                @pl.when(i == k)
                def _():
                    plan.run((name, k))

    def back_chunk(i, _):
        c = lax.rem(i + 1, parts)

        @pl.when(i + 1 < parts)
        def _():
            fetch(i + 1).start()

        gt[...] = nt(w_ref[c, MESSAGE], gm[...]) * inverse
        wut[...] = w_ref[c, PAIR, :, :256].T[:cw]
        fetch(i).wait()
        buf = dgbuf.at[i % 2]
        grad = nn(w_ref[c, PAIR, :, 256 : 256 + cw], gup[...])
        grad = grad + jnp.concatenate([gt[...]] * slots, axis=1)
        grad = (grad * buf[...].astype(F32)).astype(BF)
        buf[...] = grad
        gen[...] += nn(wut[...], grad)
        points(i, "early")
        total = nt(a_ref[: tabn + nres + cw, :], buf[...])
        gp = total[:tabn].astype(BF)
        go = total[tabn : tabn + nres].astype(BF)
        gown[c] = go
        fill_rows(first_e, total[tabn + nres :].astype(BF), c)
        fill_rows(first_n, nn(tabt[...], gp).astype(BF), c)
        gta[...] += nn(gp, w_ref[c, NEIGH])
        gta[:nres, :] += nn(go, w_ref[c, SELF])
        points(i, "late")
        return 0

    lax.fori_loop(0, parts, back_chunk, 0)
    gtab[...] = gta[...].astype(BF)
    start(ret_copies)
    plan.run(("tail", 0))
    value = gown[0].astype(F32)
    arrived(own_copies)
    for i in range(1, parts):
        value = value + zown[i].astype(F32)
    fill_self(tn(tab1[:nres, :], value.astype(BF)))
    plan.run(("tail", 1))
    ids = lax.broadcasted_iota(jnp.int32, (nres, cap), 0)
    total = gta[:nres, :]
    for i in range(groups):
        if i:
            ret_copies[i - 1].wait_recv()
            rows = ret[i]
        else:
            rows = gtab[home, :]
        chosen = jnp.where(ids == sid[asked[i]], 1.0, 0.0).astype(BF)
        total = total + nn(chosen, rows)
    gnp[...] = total.astype(BF)
    start(row_copies)
    edge_gain = jnp.zeros((cw, nres), F32)
    ge_copies = []
    for k in range(slots):
        cs = slice(k * nres, (k + 1) * nres)
        unit, scaling = normalize(e1[k].astype(F32), 0)
        grad = gen[:, cs]
        edge_gain = edge_gain + grad * unit
        gen[:, cs] = cot[k].astype(F32) + norm_back(grad, unit, scaling, egain, 0)
        copy = pltpu.make_async_copy(gen.at[:, cs], ge_hbm.at[k], os_.at[1 + k])
        copy.start()
        ge_copies.append(copy)
    unit_full, _scale = normalize(xf[...].astype(F32), 1)
    vec[:, :dn] = jnp.sum(total * unit_full, 0, keepdims=True)
    vec[:, dn : 2 * dn] = fg[...]
    vec[:, 2 * dn :] = jnp.sum(edge_gain.T, 0, keepdims=True)
    start(vec_line)
    plan.run(("tail", 2))
    arrived(row_copies)
    g_normed = gnp[mine, :].astype(F32)
    for i in range(1, parts):
        g_normed = g_normed + gbuf[i].astype(F32)
    unit_node, scaling = normalize(x1[...].astype(F32), 1)
    rows = gmid[...] + norm_back(g_normed, unit_node, scaling, ngain_ref[...], 1)
    for c in range(parts):
        gnr[c] = rows[:, c * part : (c + 1) * part]
    start(gnode_copies)
    gnode_ref[mine, :] = gnr[h]
    arrived(vec_line)
    value = vec[...]
    for i in range(1, parts):
        value = value + vz[i]
    vp[0] = value
    start(vec_plane)
    for k in range(3, tail):
        plan.run(("tail", k))
    for name, landing, out_ref in (("neigh", zn, own_ref), ("edge", ze, owe_ref)):
        total = own_total[name][0]
        for i in range(1, parts):
            chunk_line[name, i].wait_recv()
            total = total + landing[i].astype(F32)
        out_ref[...] = total
    arrived(vec_plane)
    value = vp[0]
    for i in range(1, groups):
        value = value + vp[i]
    ovec_ref[...] = value
    arrived(nn_copies + gnode_copies)
    e2_copy.wait()
    for copy in ge_copies:
        copy.wait()
    net.finish()


def layer(groups, parts, node, ncot, req, v, egain, inv, ngain, fgain, edges, ecot, weights):
    nres, part = node.shape
    dn = part * parts
    cap = req.shape[2]
    slots, cw, _ = edges.shape
    units = weights[0].shape[1]
    rows = slots * nres
    tabn = nres + groups * cap
    height = tabn + nres + 256
    rp = nres // parts
    levels = groups.bit_length() - 1
    wide, narrow = dn // groups, cw // groups
    total = 2 * dn + cw
    S, V = jax.ShapeDtypeStruct, pltpu.VMEM
    split = lambda lead, r: V((lead,) + (2,) * levels + (r, units), BF)

    def recv(lead, r):
        return [V((lead,) + (2,) * (levels - 1 - k) + (r, units), BF) for k in range(levels)]

    node_rows = lambda dtype: V((rp, dn), dtype)
    full_rows = lambda dtype: V((nres, dn), dtype)
    table = lambda dtype: V((tabn, dn), dtype)
    scratch = [
        V((parts, 4, units, dn), BF),
        V((parts, 2, units, dn), BF),
        V((parts, nres, part), BF),
        V((parts, nres, part), BF),
        full_rows(BF),
        full_rows(BF),
        node_rows(BF),
        node_rows(BF),
        full_rows(BF),
        V(req.shape, jnp.int32),
        V((groups, cap, dn), BF),
        V((groups, cap, dn), BF),
        table(BF),
        table(BF),
        V((dn, tabn), BF),
        V(edges.shape, BF),
        V(edges.shape, BF),
        V(edges.shape, BF),
        V((height, rows), BF),
        V((units, height), BF),
        V((cw, units), BF),
        V((cw, rows), F32),
        V((parts, units, nres), BF),
        full_rows(BF),
        full_rows(BF),
        V((parts, rp, dn), BF),
        V((parts, rp, dn), BF),
        V((cw, rows), BF),
        V((2, units, rows), BF),
        V((8, 128), F32),
        V((parts, rp, part), BF),
        full_rows(BF),
        node_rows(F32),
        V((parts, rp, units), BF),
        V((parts, rp, units), BF),
        node_rows(BF),
        V((1, dn), F32),
        V((units, nres), F32),
        table(F32),
        table(BF),
        V((parts, nres, units), BF),
        split(parts, wide),
        split(parts, narrow),
        split(parts, narrow),
        V((parts, nres, units), BF),
        V((parts, units, nres), BF),
        V((nres, units), BF),
        V((nres, units), BF),
        full_rows(BF),
        V((groups, cap, dn), BF),
        full_rows(BF),
        V((parts, rp, dn), BF),
        V((parts, rp, part), F32),
        V((1, total), F32),
        V((parts, 1, total), F32),
        V((groups, 1, total), F32),
        V((parts, wide, units), BF),
        V((parts, narrow, units), BF),
        V((parts, narrow, units), BF),
    ]
    for _ in range(parts):
        scratch += recv(1, wide) + recv(1, narrow)
    scratch += recv(parts, narrow)
    for _ in range(4):
        scratch += [split(1, wide)] + recv(1, wide)
    copies = (
        15 * (parts - 1)
        + 5 * (groups - 1)
        + 6 * (parts - 1) * (1 + levels)
        + (2 * parts + 5) * levels
        + 3 * (parts - 1)
    )
    scratch += [
        pltpu.SemaphoreType.DMA((copies,)),
        pltpu.SemaphoreType.DMA((copies,)),
        pltpu.SemaphoreType.DMA((9,)),
        pltpu.SemaphoreType.DMA((2,)),
        pltpu.SemaphoreType.DMA((1 + slots,)),
    ]
    vm = pl.BlockSpec(memory_space=pltpu.VMEM)
    hbm = pl.BlockSpec(memory_space=pltpu.MemorySpace.HBM)
    return pl.pallas_call(
        functools.partial(layer_kernel, groups, parts),
        in_specs=[vm] * 8 + [hbm] * 9,
        out_specs=[vm] * 10 + [hbm] * 3,
        out_shape=[
            S((nres, part), BF),
            S((nres, part), F32),
            S((wide, units), F32),
            S((wide, units), F32),
            S((narrow, units), F32),
            S((wide, units), F32),
            S((narrow, units), F32),
            S((wide, units), F32),
            S((wide, units), F32),
            S((1, total), F32),
            S(edges.shape, BF),
            S(edges.shape, F32),
            S((parts, units, rows), BF),
        ],
        scratch_shapes=scratch,
        compiler_params=pltpu.CompilerParams(
            collective_id=0, has_side_effects=True, vmem_limit_bytes=62 << 20
        ),
        name="layer",
    )(node, ncot, req, v, egain, inv, ngain, fgain, edges, ecot, *weights)


def publish_kernel(groups, sizes, *refs):
    count = (len(refs) - 7) // 3
    ins, vec_ref = refs[:count], refs[count]
    outs, gains = refs[count + 1 : 2 * count + 1], refs[2 * count + 1 : 2 * count + 4]
    stage, (table, sems, out_sems) = refs[2 * count + 4 : 3 * count + 4], refs[3 * count + 4 :]
    loads = [pltpu.make_async_copy(a, b, sems.at[k]) for k, (a, b) in enumerate(zip(ins, stage))]
    saves = [pltpu.make_async_copy(a, b, out_sems.at[k]) for k, (a, b) in enumerate(zip(stage, outs))]
    start(loads)
    begin = 0
    for size, out in zip(sizes, gains):
        each = size // groups
        for q in range(groups):
            table[q : q + 1, :each] = vec_ref[:, begin + q * each : begin + (q + 1) * each]
        begin += size
        out[...] = table[pl.ds(lax.axis_index("res"), 1), :each]
    for load, save in zip(loads, saves):
        load.wait()
        save.start()
    for save in saves:
        save.wait()


def publish(groups, sizes, arrays, vec):
    S = jax.ShapeDtypeStruct
    vm = pl.BlockSpec(memory_space=pltpu.VMEM)
    hbm = pl.BlockSpec(memory_space=pltpu.MemorySpace.HBM)
    return pl.pallas_call(
        functools.partial(publish_kernel, groups, sizes),
        in_specs=[hbm] * len(arrays) + [vm],
        out_specs=[hbm] * len(arrays) + [vm] * len(sizes),
        out_shape=[S(a.shape, a.dtype) for a in arrays]
        + [S((1, size // groups), F32) for size in sizes],
        scratch_shapes=[pltpu.VMEM(a.shape, a.dtype) for a in arrays]
        + [
            pltpu.VMEM((groups, 128), F32),
            pltpu.SemaphoreType.DMA((len(arrays),)),
            pltpu.SemaphoreType.DMA((len(arrays),)),
        ],
        compiler_params=pltpu.CompilerParams(vmem_limit_bytes=60 << 20),
        name="publish",
    )(*arrays, vec)


def per_device(
    node_state,
    edge_state,
    node_gain,
    edge_gain,
    ffn_gain,
    w_self,
    w_neigh,
    w_edge,
    w_message,
    w_update,
    w_expand,
    w_contract,
    neighbours,
    requests,
    counts,
    node_cotangent,
    edge_cotangent,
):
    groups, parts = lax.axis_size("res"), lax.axis_size("hid")
    nres, slot_count = neighbours.shape
    slot_part, cw = edge_state.shape[1:]
    h = lax.axis_index("hid")
    live = lax.broadcasted_iota(jnp.int32, (nres, slot_count), 1) < counts[:, None]
    entry = jnp.where(live, neighbours, -1)
    entry = lax.dynamic_slice_in_dim(entry, h * slot_part, slot_part, 1).T[:, None, :]
    inverse = 1.0 / counts.astype(F32)[None]
    ngain, egain, fgain = node_gain[None], edge_gain[:, None], ffn_gain[None]
    edges = edge_state.transpose(1, 2, 0)
    cot = edge_cotangent.transpose(1, 2, 0)
    node_two, gnode, gws, gwn, gwe, gwm, gwu, gwx, gwc, vec, e2, ge, _slopes = layer(
        groups,
        parts,
        node_state,
        node_cotangent,
        requests[0][:, None, :],
        entry,
        egain,
        inverse,
        ngain,
        fgain,
        edges,
        cot,
        [w_neigh, w_self, w_edge, w_update.T, w_message, w_expand, w_contract],
    )
    dn = ngain.shape[1]
    node_two, gnode, gws, gwn, gwe, gwm, gwu, gwx, gwc, e2, ge, gng, gfg, geg = publish(
        groups, (dn, dn, cw), (node_two, gnode, gws, gwn, gwe, gwm, gwu, gwx, gwc, e2, ge), vec
    )
    return (
        node_two,
        e2.transpose(2, 0, 1),
        gnode,
        ge.transpose(2, 0, 1),
        gng[0],
        geg[0],
        gfg[0],
        gws,
        gwn,
        gwe,
        gwm.T,
        gwu.T,
        gwx,
        gwc.T,
    )


def solution(mesh):
    return jax.shard_map(
        per_device,
        mesh=mesh,
        in_specs=(
            P("res", "hid"),
            P("res", "hid", None),
            P(),
            P(),
            P(),
            P(None, "hid"),
            P(None, "hid"),
            P(None, "hid"),
            P("hid", None),
            P("hid", None),
            P(None, "hid"),
            P("hid", None),
            P("res", None),
            P("res", None, None),
            P("res"),
            P("res", "hid"),
            P("res", "hid", None),
        ),
        out_specs=(
            P("res", "hid"),
            P("res", "hid", None),
            P("res", "hid"),
            P("res", "hid", None),
            P("res"),
            P("res"),
            P("res"),
            P("res", "hid"),
            P("res", "hid"),
            P("res", "hid"),
            P("hid", "res"),
            P("hid", "res"),
            P("res", "hid"),
            P("hid", "res"),
        ),
        check_vma=False,
    )
```

```python
import functools

import jax
import jax.numpy as jnp
from jax import lax
from jax.experimental import pallas as pl
from jax.experimental.pallas import tpu as pltpu
from jax.sharding import PartitionSpec as P

F32, BF = jnp.float32, jnp.bfloat16
EPSILON = 1e-05
TANH_SCALE = 0.7978845608028654
TANH_CUBE = 0.044715
MESH = pl.DeviceIdType.MESH
NEIGH, PAIR, SELF, MESSAGE = range(4)
EXPAND, CONTRACT = range(2)


def contract(a, b, dim_a, dim_b):
    return lax.dot_general(
        a, b, (((dim_a,), (dim_b,)), ((), ())), preferred_element_type=F32
    )


def nn(a, b):
    return contract(a, b, 1, 0)


def nt(a, b):
    return contract(a, b, 1, 1)


def tn(a, b):
    return contract(a, b, 0, 0)


def normalize(values, axis):
    centred = values - jnp.mean(values, axis, keepdims=True)
    scaling = lax.rsqrt(jnp.mean(centred * centred, axis, keepdims=True) + EPSILON)
    return centred * scaling, scaling


def norm_back(grad, unit, scaling, gain, axis):
    scaled = grad * gain
    return scaling * (
        scaled
        - jnp.mean(scaled, axis, keepdims=True)
        - unit * jnp.mean(scaled * unit, axis, keepdims=True)
    )


def gelu(x):
    return (0.5 * x) * (1.0 + jnp.tanh(x * (TANH_SCALE + TANH_SCALE * TANH_CUBE * (x * x))))


def gelu_pair(x):
    square = x * x
    bent = jnp.tanh(x * (TANH_SCALE + TANH_SCALE * TANH_CUBE * square))
    half = 0.5 * x
    slope = 0.5 + 0.5 * bent + half * (1.0 - bent * bent) * (
        TANH_SCALE + 3 * TANH_SCALE * TANH_CUBE * square
    )
    return half + half * bent, slope


class Net:
    def __init__(self, send_sems, recv_sems):
        self.send_sems, self.recv_sems, self.count, self.sent = send_sems, recv_sems, 0, []

    def make(self, src, dst, device):
        k = self.count
        self.count += 1
        copy = pltpu.make_async_remote_copy(
            src_ref=src,
            dst_ref=dst,
            send_sem=self.send_sems.at[k],
            recv_sem=self.recv_sems.at[k],
            device_id=device,
            device_id_type=MESH,
        )
        self.sent.append(copy)
        return copy

    def push(self, src, dst, device):
        copy = self.make(src, dst, device)
        copy.start()
        return copy

    def finish(self):
        for copy in self.sent:
            copy.wait_send()


def start(copies):
    for copy in copies:
        copy.start()


def arrived(copies):
    for copy in copies:
        copy.wait_recv()


def flip_bit(index, bit):
    step = 1 << bit
    return index + step - 2 * step * ((index // step) % 2)


def greet(devices):
    barrier = pltpu.get_barrier_semaphore()
    for device in devices:
        pl.semaphore_signal(barrier, inc=1, device_id=device, device_id_type=MESH)


def greeted(devices):
    pl.semaphore_wait(pltpu.get_barrier_semaphore(), len(devices))


def place(groups, parts):
    p, h = lax.axis_index("res"), lax.axis_index("hid")
    line = [None] + [(p, lax.rem(h + i, parts)) for i in range(1, parts)]
    plane = [None] + [(lax.rem(p + i, groups), h) for i in range(1, groups)]
    return p, h, line, plane


class Rows:
    def __init__(self, net, p, groups, plane, nres, cap, tab_ref, rows_buf):
        self.mine = pl.ds(pl.multiple_of(nres + p * cap, 16), cap)
        self.asked = [lax.rem(p + i, groups) for i in range(groups)]
        self.nres, self.cap, self.tab, self.buf = nres, cap, tab_ref, rows_buf
        self.copies = [
            net.make(rows_buf.at[i], tab_ref.at[self.mine, :], plane[i]) for i in range(1, groups)
        ]

    def send(self, normed, sid_ref):
        ids = lax.broadcasted_iota(jnp.int32, (self.nres, self.cap), 0)
        self.tab[: self.nres, :] = normed
        for i, q in enumerate(self.asked):
            chosen = jnp.where(ids == sid_ref[q], 1.0, 0.0).astype(BF)
            rows = tn(chosen, normed).astype(BF)
            if i == 0:
                self.tab[self.mine, :] = rows
            else:
                self.buf[i] = rows
                self.copies[i - 1].start()


class Gather:
    def __init__(self, net, p, h, groups, parts, edge_full, node_full, depth):
        self.levels = groups.bit_length() - 1
        low, half = p % 2, p // 2
        turned = sum(
            ((half // (1 << b)) % 2) * (1 << (self.levels - 2 - b)) for b in range(self.levels - 1)
        )
        starts = [low * (groups // 2) + half, low * (groups // 2) + turned]
        rows = depth // groups
        back = [(p, lax.rem(h + parts - i, parts)) for i in range(parts)]
        units = [(edge_full, w, r) for r in range(1, parts) for w in (NEIGH, PAIR, SELF)]
        self.lag = 2 * (self.levels + 1)
        self.chunk_slots = [0] + [3 * k - 1 + self.lag for k in range(1, parts)]
        for full, w in ((edge_full, MESSAGE), (node_full, EXPAND), (node_full, CONTRACT)):
            units += [(full, w, r) for r in range(1, parts)]
        count = 3 * (parts - 1)
        self.weight_slots = [count + k * (parts - 1) - 1 + self.lag for k in range(1, 4)]
        self.batches = []
        for u, (full, w, r) in enumerate(units):
            stages, turn = [], u % 2
            begin = starts[turn]
            own = pl.ds(pl.multiple_of(begin * rows, rows), rows)
            stages.append(net.make(full.at[0, w, own, :], full.at[r, w, own, :], back[r]))
            for level in range(self.levels):
                if level == self.levels - 1:
                    bit = 0
                else:
                    bit = 1 + (level if turn == 0 else self.levels - 2 - level)
                span = rows << level
                held = (begin // (1 << level)) * span
                view = full.at[r, w, pl.ds(pl.multiple_of(held, span), span), :]
                stages.append(net.make(view, view, (flip_bit(p, bit), h)))
            self.batches.append(stages)
        self.slots = len(units) + self.lag

    def turn(self, slot):
        for stage in range(self.levels + 1, -1, -1):
            b = slot - 2 * stage
            if 0 <= b < len(self.batches):
                if stage:
                    self.batches[b][stage - 1].wait_recv()
                if stage <= self.levels:
                    self.batches[b][stage].start()


def bits_of(index, levels):
    return tuple((index >> b) & 1 for b in range(levels - 1, -1, -1))


def fill_rows(ref, value, lead):
    levels = len(ref.shape) - 3
    rows = ref.shape[-2]
    for s in range(1 << levels):
        ref[(lead,) + bits_of(s, levels)] = value[s * rows : (s + 1) * rows, :]


class PlaneSum:
    def __init__(self, net, p, h, levels, order, source, recv, done):
        self.levels, self.source, self.recv, self.done = levels, source, recv, done
        own = [(p // (1 << bit)) % 2 for bit in range(levels)]
        self.fixed, self.copies = [], []
        fixed = {}
        for level in range(levels):
            bit = 0 if level == 0 else (level if order == 0 else levels - level)
            other = dict(fixed)
            other[bit] = 1 - own[bit]
            fixed = dict(fixed)
            fixed[bit] = own[bit]
            self.fixed.append(fixed)
            self.copies.append(
                net.make(source.at[self.index(other)], recv[level], (flip_bit(p, bit), h))
            )

    def index(self, fixed):
        return (slice(None),) + tuple(
            fixed.get(bit, slice(None)) for bit in range(self.levels - 1, -1, -1)
        )

    def held(self):
        return self.source.at[self.index(self.fixed[-1])]

    def steps(self):
        return [functools.partial(self.step, level) for level in range(self.levels + 1)]

    def step(self, level):
        if level:
            k = level - 1
            self.copies[k].wait_recv()
            free = [bit for bit in range(self.levels) if bit not in self.fixed[k]]
            for n in range(1 << len(free)):
                fixed = dict(self.fixed[k])
                for j, bit in enumerate(free):
                    fixed[bit] = (n >> j) & 1
                at = self.index(fixed)
                got = (slice(None),) + tuple(fixed[bit] for bit in reversed(free))
                total = self.source[at].astype(F32) + self.recv[k][got].astype(F32)
                if level == self.levels and self.done(total):
                    continue
                self.source[at] = total.astype(BF)
        if level < self.levels:
            self.copies[level].start()


def build_inputs(a_ref, edges, v_ref, egain, tabn):
    slots, cw, nres = edges.shape
    index = lax.broadcasted_iota(jnp.int32, (tabn, nres), 0)
    own = lax.broadcasted_iota(jnp.int32, (nres, nres), 0) == lax.broadcasted_iota(
        jnp.int32, (nres, nres), 1
    )
    own = jnp.where(own, 1.0, 0.0).astype(BF)
    height = a_ref.shape[0]

    def one(k, _):
        cs = pl.ds(pl.multiple_of(k * nres, nres), nres)
        a_ref[:tabn, cs] = jnp.where(index == v_ref[k], 1.0, 0.0).astype(BF)
        a_ref[tabn : tabn + nres, cs] = own
        unit, _scale = normalize(edges[k].astype(F32), 0)
        a_ref[tabn + nres : tabn + nres + cw, cs] = (unit * egain).astype(BF)
        a_ref[tabn + nres + cw :, cs] = jnp.zeros((height - tabn - nres - cw, nres), BF)
        return 0

    lax.fori_loop(0, slots, one, 0)


def edge_chunk(c, w_ref, tab, a_ref, bt, wut, v_ref, upd, mean, inverse, cw, pause, second=None):
    tabn, nres = tab.shape[0], mean.shape[-1]
    slots = a_ref.shape[1] // nres
    bt[:, :tabn] = nt(w_ref[c, NEIGH], tab[...]).astype(BF)
    bt[:, tabn : tabn + nres] = nt(w_ref[c, SELF], tab[:nres, :]).astype(BF)
    bt[:, tabn + nres :] = w_ref[c, PAIR, :, :256]
    wut[...] = w_ref[c, PAIR, :, 256:].T[:cw]
    pause(0)
    before = nn(bt[...], a_ref[...])
    pause(1)
    if second is None:
        hidden = gelu(before)
    else:
        dg, gup, gwu = second
        hidden, slope = gelu_pair(before)
    total, kept = None, []
    for k in range(slots):
        cs = slice(k * nres, (k + 1) * nres)
        live = (v_ref[k] >= 0).astype(F32)
        part = hidden[:, cs] * live
        total = part if total is None else total + part
        kept.append(part.astype(BF))
        if second is not None:
            dg[:, cs] = (slope[:, cs] * live).astype(BF)
    mean[c] = (total * inverse).astype(BF)
    kept = jnp.concatenate(kept, axis=1)
    upd[...] += nn(wut[...], kept)
    if second is not None:
        fill_rows(gwu, nt(gup[...], kept).astype(BF), c)


def message_part(w_ref, mean, parts):
    total = None
    for c in range(parts):
        term = tn(mean[c], w_ref[c, MESSAGE])
        total = term if total is None else total + term
    return total.astype(BF)


def add_update(edges, upd, out):
    slots, _, nres = edges.shape
    for k in range(slots):
        out[k] = (edges[k].astype(F32) + upd[:, k * nres : (k + 1) * nres]).astype(BF)


class Plan:
    def __init__(self):
        self.points, self.active = {}, []

    def add(self, point, steps, first_now=True):
        steps = list(steps)
        if first_now:
            self.note(point, steps.pop(0))
        if steps:
            self.active.append(steps)

    def note(self, point, step):
        self.points.setdefault(point, []).append(step)

    def advance(self, point):
        for steps in self.active:
            self.note(point, steps.pop(0))
        self.active = [steps for steps in self.active if steps]

    def run(self, point):
        for step in self.points.get(point, ()):
            step()


def plane_scratch(groups, lead, rows, units, order, last):
    recv, acc = [], []
    count = groups
    while count > 1:
        count //= 2
        recv.append(pltpu.VMEM((lead, count, rows, units), BF))
        if count == 1:
            acc.append(pltpu.VMEM((lead, rows, units), last))
        elif order == 0:
            acc.append(pltpu.VMEM((lead, count // 2, 2, rows, units), BF))
        else:
            acc.append(pltpu.VMEM((lead, 2, count // 2, rows, units), BF))
    return recv + acc


def layer_kernel(groups, parts, *refs):
    (node_ref, ncot_ref, req_ref, nbr_ref, egain_ref, count_ref, ngain_ref, fgain_ref) = refs[:8]
    (edges_hbm, ecot_hbm, wn_hbm, ws_hbm, we_hbm, wu_hbm, wm_hbm, wx_hbm, wc_hbm) = refs[8:17]
    (nn_ref, gnode_ref, ows_ref, own_ref, owe_ref, owm_ref, owu_ref, owx_ref, owc_ref, ovec_ref) = refs[17:27]
    (e2_hbm, ge_hbm, dg_hbm) = refs[27:30]
    refs = list(refs[30:])

    def take(count):
        taken = refs[:count]
        del refs[:count]
        return taken

    w_ref, wf_ref, nbuf, cbuf, nfull, cf, xrows, x1, xf, sid = take(10)
    rows0, rows1, tab0, tab1, tabt, edges, e1, cot, a_ref, bt = take(10)
    wut, upd, mean, msg0, msg1, mbuf0, mbuf1, gup, dgbuf = take(9)
    nsp, gm, gmid, act, gex, fi, fg, gt, gta, gtab = take(10)
    v_ref, ecol = take(2)
    gown, first_n, first_e, gwu, zown, zmean, actf, gexf, fif, ret = take(10)
    gnp, gbuf, gnr, vec, vz, vp, zn, ze, zu = take(9)
    ss, rs, ls, ds, os_ = refs[-5:]
    p, h, line, plane = place(groups, parts)
    nres, part = node_ref.shape
    dn = part * parts
    cap = req_ref.shape[2]
    slots, cw, _ = edges.shape
    rp = nres // parts
    units = w_ref.shape[2]
    tabn = tab0.shape[0]
    levels = groups.bit_length() - 1
    mine = pl.ds(pl.multiple_of(h * rp, rp), rp)
    home = pl.ds(pl.multiple_of(nres + p * cap, 16), cap)
    asked = [lax.rem(p + groups - i, groups) for i in range(groups)]
    inverse = 1.0 / count_ref[...].astype(F32)

    raw = [a_ref.at[:dn, k * units : (k + 1) * units] for k in range(3)]
    raw_e = [a_ref.at[dn + k * cw : dn + (k + 1) * cw, :units] for k in range(2)]
    loads = [
        pltpu.make_async_copy(src, dst, ls.at[k])
        for k, (src, dst) in enumerate(
            (
                (wn_hbm, raw[0]),
                (we_hbm, raw_e[0]),
                (wu_hbm, raw_e[1]),
                (ws_hbm, raw[1]),
                (wx_hbm, raw[2]),
                (edges_hbm, edges),
                (wm_hbm, w_ref.at[0, MESSAGE]),
                (wc_hbm, wf_ref.at[0, CONTRACT]),
                (ecot_hbm, cot),
            )
        )
    ]
    start(loads)
    net = Net(ss, rs)

    def to_parts(pair):
        copies = []
        for i in range(1, parts):
            src, dst = pair(i, lax.rem(h + i, parts))
            copies.append(net.make(src, dst, line[i]))
        return copies

    def rows_of(other):
        return pl.ds(pl.multiple_of(other * rp, rp), rp)

    node_copies = to_parts(lambda i, o: (node_ref, nbuf.at[h]))
    req_copies = [
        net.make(req_ref.at[lax.rem(p + i, groups)], sid.at[p], plane[i]) for i in range(1, groups)
    ]
    ncot_copies = to_parts(lambda i, o: (ncot_ref, cbuf.at[h]))
    rows_first = Rows(net, p, groups, plane, nres, cap, tab0, rows0)
    rows_next = Rows(net, p, groups, plane, nres, cap, tab1, rows1)
    message0 = to_parts(lambda i, o: (msg0.at[rows_of(o), :], mbuf0.at[i]))
    message1 = to_parts(lambda i, o: (msg1.at[rows_of(o), :], mbuf1.at[i]))
    x1_copies = to_parts(lambda i, o: (x1, xf.at[mine, :]))
    gather = Gather(net, p, h, groups, parts, w_ref, wf_ref, units)
    gm_copies = to_parts(lambda i, o: (gm.at[mine, :], gm.at[mine, :]))
    nn_copies = to_parts(lambda i, o: (nsp.at[o], nn_ref.at[mine, :]))
    ret_copies = [
        net.make(
            gtab.at[pl.ds(pl.multiple_of(nres + lax.rem(p + i, groups) * cap, 16), cap), :],
            ret.at[i],
            plane[i],
        )
        for i in range(1, groups)
    ]
    own_copies = to_parts(lambda i, o: (gown.at[i], zown.at[i]))
    mean_copies = to_parts(lambda i, o: (mean.at[i], zmean.at[i]))
    act_copies = to_parts(lambda i, o: (act.at[i], actf.at[mine, :]))
    gex_copies = to_parts(lambda i, o: (gex.at[i], gexf.at[mine, :]))
    fi_copies = to_parts(lambda i, o: (fi, fif.at[mine, :]))
    row_copies = to_parts(lambda i, o: (gnp.at[rows_of(o), :], gbuf.at[i]))
    gnode_copies = to_parts(lambda i, o: (gnr.at[o], gnode_ref.at[mine, :]))
    vec_line = to_parts(lambda i, o: (vec, vz.at[i]))
    vec_plane = [net.make(vp.at[0], vp.at[i], plane[i]) for i in range(1, groups)]

    chunk_sums, chunk_line, chunk_own = {}, {}, {}
    for c in range(parts):
        for name, source, order, landing in (
            ("neigh", first_n, 0, zn),
            ("edge", first_e, 1, ze),
            ("update", gwu, c % 2, zu),
        ):
            recv = take(levels)
            item = PlaneSum(
                net, p, h, levels, order, source.at[pl.ds(c, 1)], recv, lambda total: False
            )
            steps = item.steps()
            if c:
                copy = net.make(item.held().at[0], landing.at[c], line[c])
                chunk_line[name, c] = copy
                last = steps.pop()

                def send_on(last=last, copy=copy):
                    last()
                    copy.start()

                steps.append(send_on)
            else:
                chunk_own[name] = item
            chunk_sums[name, c] = steps
    def unit_sum(order, out):
        source = take(1)[0]

        def done(total):
            out[...] = total[0]
            return True

        item = PlaneSum(net, p, h, levels, order, source, take(levels), done)

        def fill(value):
            fill_rows(source, value.astype(BF), 0)

        return fill, item.steps()

    fill_self, steps_self = unit_sum(0, ows_ref)
    fill_message, steps_message = unit_sum(1, owm_ref)
    fill_expand, steps_expand = unit_sum(0, owx_ref)
    fill_contract, steps_contract = unit_sum(1, owc_ref)

    peers = line[1:] + plane[1:]
    greet(peers)
    nbuf[h] = node_ref[...]
    cbuf[h] = ncot_ref[...]
    sid[p] = req_ref[p]
    loads[0].wait()
    w_ref[0, NEIGH] = raw[0][...].T
    greeted(peers)
    start(node_copies)
    start(req_copies)
    gather.turn(0)
    loads[1].wait()
    loads[2].wait()
    w_ref[0, PAIR, :, :cw] = raw_e[0][...].T
    w_ref[0, PAIR, :, cw:256] = jnp.zeros((units, 256 - cw), BF)
    w_ref[0, PAIR, :, 256 : 256 + cw] = raw_e[1][...].T
    w_ref[0, PAIR, :, 256 + cw :] = jnp.zeros((units, 256 - cw), BF)
    gather.turn(1)
    counts = count_ref[...]
    for k in range(slots):
        row = nbr_ref[pl.ds(h * slots + k, 1), :]
        v_ref[k] = jnp.where(h * slots + k < counts, row, -1)
    ecol[...] = jnp.broadcast_to(egain_ref[...], (nres, cw)).T
    arrived(node_copies)
    for c in range(parts):
        nfull[:, c * part : (c + 1) * part] = nbuf[c]
    unit_node, _scale = normalize(nfull[...].astype(F32), 1)
    normed = (unit_node * ngain_ref[...]).astype(BF)
    xrows[...] = nfull[mine, :]
    arrived(req_copies)
    rows_first.send(normed, sid)
    start(ncot_copies)
    loads[3].wait()
    w_ref[0, SELF] = raw[1][...].T
    gather.turn(2)
    loads[4].wait()
    wf_ref[0, EXPAND] = raw[2][...].T
    gather.turn(3)
    loads[5].wait()
    egain = ecol[...]
    build_inputs(a_ref, edges, v_ref, egain, tabn)
    gather.turn(4)
    loads[6].wait()
    loads[7].wait()
    arrived(ncot_copies)
    for c in range(parts):
        cf[:, c * part : (c + 1) * part] = cbuf[c]
    upd[...] = jnp.zeros_like(upd)
    gather.turn(5)
    first_slot = 6
    arrived(rows_first.copies)

    slot = first_slot
    turns_at = {}
    for k in range(parts):
        upto = max(slot + (k == 0), gather.chunk_slots[k] + 1)
        turns_at["begin", k] = range(slot, min(upto, gather.slots))
        turns_at[0, k] = range(upto, min(upto + 1, gather.slots))
        turns_at[1, k] = range(upto + 1, min(upto + 2, gather.slots))
        slot = min(upto + 2, gather.slots)

    def turns(c, at):
        for k in range(parts):
            if len(turns_at[at, k]):

                @pl.when(c == k)
                def _():
                    for s in turns_at[at, k]:
                        gather.turn(s)

    def first_chunk(c, _):
        turns(c, "begin")
        pause = lambda at: turns(c, at)
        edge_chunk(c, w_ref, tab0, a_ref, bt, wut, v_ref, upd, mean, inverse, cw, pause)
        return 0

    lax.fori_loop(0, parts, first_chunk, 0)
    message_slot, expand_slot, contract_slot = gather.weight_slots
    for s in range(slot, message_slot + 1):
        gather.turn(s)
    slot = max(slot, message_slot + 1)
    msg0[...] = message_part(w_ref, mean, parts)
    start(message0)
    if slot < gather.slots:
        gather.turn(slot)
        slot += 1
    add_update(edges, upd, e1)
    build_inputs(a_ref, e1, v_ref, egain, tabn)
    middle = xrows[...].astype(F32) + msg0[mine, :].astype(F32)
    for i, copy in enumerate(message0):
        copy.wait_recv()
        middle = middle + mbuf0[i + 1].astype(F32)
    unit_ffn, _scale = normalize(middle, 1)
    ffn_input = (unit_ffn * fgain_ref[...]).astype(BF)
    for s in range(slot, expand_slot + 1):
        gather.turn(s)
    slot = max(slot, expand_slot + 1)
    hidden = [gelu(nt(ffn_input, wf_ref[c, EXPAND])).astype(BF) for c in range(parts)]
    for s in range(slot, gather.slots):
        gather.turn(s)
    out = middle
    for c in range(parts):
        out = out + nn(hidden[c], wf_ref[c, CONTRACT])
    out = out.astype(BF)
    x1[...] = out
    xf[mine, :] = out
    start(x1_copies)
    upd[...] = jnp.zeros_like(upd)
    loads[8].wait()
    for k in range(slots):
        live = (v_ref[k] >= 0).astype(F32)
        gup[:, k * nres : (k + 1) * nres] = (cot[k].astype(F32) * live).astype(BF)
    arrived(x1_copies)
    unit_full, _scale = normalize(xf[...].astype(F32), 1)
    rows_next.send((unit_full * ngain_ref[...]).astype(BF), sid)
    arrived(rows_next.copies)

    def ffn_sums():
        arrived(act_copies + gex_copies + fi_copies)
        fill_expand(tn(fif[...], gexf[...]))
        fill_contract(tn(cf[...], actf[...]))

    def message_sums():
        value = mean[0].astype(F32)
        arrived(mean_copies)
        for i in range(1, parts):
            value = value + zmean[i].astype(F32)
        fill_message(tn(gm[...], value.astype(BF).T))

    plan = Plan()
    for i in range(parts):
        plan.advance(("second", i))
        c = (i + 1) % parts
        if c:
            plan.note(("second", i), mean_copies[c - 1].start)
        plan.add(("second", i), chunk_sums["update", c])
    for name in ("node", "ffn"):
        plan.advance((name, 0))
    for i in range(parts):
        plan.advance(("early", i))
        if i == min(1, parts - 1):
            plan.note(("early", i), ffn_sums)
            plan.add(("early", i), steps_expand)
            plan.add(("early", i), steps_contract)
        c = (i + 1) % parts
        if c:
            plan.note(("late", i), own_copies[c - 1].start)
            plan.advance(("late", i))
            for name in ("neigh", "edge"):
                plan.add(("late", i), chunk_sums[name, c])
        if i == 0:
            plan.note(("late", i), message_sums)
            plan.add(("late", i), steps_message)
    plan.advance(("tail", 0))
    for name in ("neigh", "edge"):
        plan.add(("tail", 0), chunk_sums[name, 0])
    plan.add(("tail", 1), steps_self)
    tail = 2
    while plan.active:
        plan.advance(("tail", tail))
        tail += 1

    def points(i, name):
        for k in range(parts):
            if (name, k) in plan.points:

                @pl.when(i == k)
                def _():
                    plan.run((name, k))

    def save(i):
        return pltpu.make_async_copy(dgbuf.at[i % 2], dg_hbm.at[lax.rem(i + 1, parts)], ds.at[i % 2])

    def second_chunk(i, _):
        @pl.when(i >= 2)
        def _():
            save(i - 2).wait()

        edge_chunk(
            lax.rem(i + 1, parts),
            w_ref,
            tab1,
            a_ref,
            bt,
            wut,
            v_ref,
            upd,
            mean,
            inverse,
            cw,
            lambda at: None,
            (dgbuf.at[i % 2], gup, gwu),
        )
        save(i).start()
        points(i, "second")
        return 0

    lax.fori_loop(0, parts, second_chunk, 0)
    msg1[...] = message_part(w_ref, mean, parts)
    start(message1)
    plan.run(("node", 0))
    add_update(e1, upd, edges)
    e2_copy = pltpu.make_async_copy(edges, e2_hbm, os_.at[0])
    e2_copy.start()
    tabt[...] = tab1[...].T
    middle = x1[...].astype(F32) + msg1[mine, :].astype(F32)
    for i, copy in enumerate(message1):
        copy.wait_recv()
        middle = middle + mbuf1[i + 1].astype(F32)
    unit_ffn, scaling = normalize(middle, 1)
    ffn_input = (unit_ffn * fgain_ref[...]).astype(BF)
    fi[...] = ffn_input
    cotangent = cf[mine, :]
    g_input = jnp.zeros((rp, dn), F32)
    for c in range(parts):
        active, slope = gelu_pair(nt(ffn_input, wf_ref[c, EXPAND]))
        act[c] = active.astype(BF)
        g_expand = (nt(cotangent, wf_ref[c, CONTRACT]) * slope).astype(BF)
        gex[c] = g_expand
        g_input = g_input + nn(g_expand, wf_ref[c, EXPAND])
    g_middle = cotangent.astype(F32) + norm_back(g_input, unit_ffn, scaling, fgain_ref[...], 1)
    gm[mine, :] = g_middle.astype(BF)
    start(gm_copies)
    gmid[...] = g_middle
    fg[...] = jnp.sum(g_input * unit_ffn, 0, keepdims=True)
    out = middle
    for c in range(parts):
        out = out + nn(act[c], wf_ref[c, CONTRACT])
    out = out.astype(BF)
    for c in range(parts):
        nsp[c] = out[:, c * part : (c + 1) * part]
    start(nn_copies)
    nn_ref[mine, :] = nsp[h]
    actf[mine, :] = act[0]
    gexf[mine, :] = gex[0]
    fif[mine, :] = fi[...]
    upd[...] = jnp.zeros_like(upd)
    gta[...] = jnp.zeros_like(gta)
    for c in range(max(parts - 2, 0), parts):
        save(c).wait()
    arrived(gm_copies)
    start(act_copies)
    start(gex_copies)
    start(fi_copies)
    plan.run(("ffn", 0))

    def fetch(i):
        return pltpu.make_async_copy(dg_hbm.at[lax.rem(i + 1, parts)], dgbuf.at[i % 2], ds.at[i % 2])

    fetch(0).start()
    gen = upd

    def back_chunk(i, _):
        c = lax.rem(i + 1, parts)

        @pl.when(i + 1 < parts)
        def _():
            fetch(i + 1).start()

        gt[...] = nt(w_ref[c, MESSAGE], gm[...]) * inverse
        wut[...] = w_ref[c, PAIR, :, :256].T[:cw]
        fetch(i).wait()
        buf = dgbuf.at[i % 2]
        grad = nn(w_ref[c, PAIR, :, 256 : 256 + cw], gup[...])
        grad = grad + jnp.concatenate([gt[...]] * slots, axis=1)
        grad = (grad * buf[...].astype(F32)).astype(BF)
        buf[...] = grad
        gen[...] += nn(wut[...], grad)
        points(i, "early")
        total = nt(a_ref[: tabn + nres + cw, :], buf[...])
        gp = total[:tabn].astype(BF)
        go = total[tabn : tabn + nres].astype(BF)
        gown[c] = go
        gta[...] += nn(gp, w_ref[c, NEIGH])
        gta[:nres, :] += nn(go, w_ref[c, SELF])

        @pl.when(i == parts - 1)
        def _():
            gtab[...] = gta[...].astype(BF)
            start(ret_copies)

        fill_rows(first_e, total[tabn + nres :].astype(BF), c)
        fill_rows(first_n, nn(tabt[...], gp).astype(BF), c)
        points(i, "late")
        return 0

    lax.fori_loop(0, parts, back_chunk, 0)
    plan.run(("tail", 0))
    value = gown[0].astype(F32)
    arrived(own_copies)
    for i in range(1, parts):
        value = value + zown[i].astype(F32)
    fill_self(tn(tab1[:nres, :], value.astype(BF)))
    plan.run(("tail", 1))
    edge_gain = jnp.zeros((cw, nres), F32)
    ge_copies = []
    for k in range(slots):
        cs = slice(k * nres, (k + 1) * nres)
        unit, scaling = normalize(e1[k].astype(F32), 0)
        grad = gen[:, cs]
        edge_gain = edge_gain + grad * unit
        gen[:, cs] = cot[k].astype(F32) + norm_back(grad, unit, scaling, egain, 0)
        copy = pltpu.make_async_copy(gen.at[:, cs], ge_hbm.at[k], os_.at[1 + k])
        copy.start()
        ge_copies.append(copy)
    plan.run(("tail", 2))
    ids = lax.broadcasted_iota(jnp.int32, (nres, cap), 0)
    total = gta[:nres, :]
    for i in range(groups):
        if i:
            ret_copies[i - 1].wait_recv()
            rows = ret[i]
        else:
            rows = gtab[home, :]
        chosen = jnp.where(ids == sid[asked[i]], 1.0, 0.0).astype(BF)
        total = total + nn(chosen, rows)
    gnp[...] = total.astype(BF)
    start(row_copies)
    unit_full, _scale = normalize(xf[...].astype(F32), 1)
    vec[:, :dn] = jnp.sum(total * unit_full, 0, keepdims=True)
    vec[:, dn : 2 * dn] = fg[...]
    vec[:, 2 * dn :] = jnp.sum(edge_gain.T, 0, keepdims=True)
    start(vec_line)
    plan.run(("tail", 3))
    arrived(row_copies)
    g_normed = gnp[mine, :].astype(F32)
    for i in range(1, parts):
        g_normed = g_normed + gbuf[i].astype(F32)
    unit_node, scaling = normalize(x1[...].astype(F32), 1)
    rows = gmid[...] + norm_back(g_normed, unit_node, scaling, ngain_ref[...], 1)
    for c in range(parts):
        gnr[c] = rows[:, c * part : (c + 1) * part]
    start(gnode_copies)
    gnode_ref[mine, :] = gnr[h]
    arrived(vec_line)
    value = vec[...]
    for i in range(1, parts):
        value = value + vz[i]
    vp[0] = value
    start(vec_plane)
    for k in range(4, tail):
        plan.run(("tail", k))
    for name, landing, out_ref in (
        ("update", zu, owu_ref),
        ("neigh", zn, own_ref),
        ("edge", ze, owe_ref),
    ):
        total = chunk_own[name].held()[0].astype(F32)
        for i in range(1, parts):
            chunk_line[name, i].wait_recv()
            total = total + landing[i].astype(F32)
        out_ref[...] = total
    arrived(vec_plane)
    value = vp[0]
    for i in range(1, groups):
        value = value + vp[i]
    ovec_ref[...] = value
    arrived(nn_copies + gnode_copies)
    e2_copy.wait()
    for copy in ge_copies:
        copy.wait()
    net.finish()


def layer(groups, parts, node, ncot, req, nbr, egain, counts, ngain, fgain, edges, ecot, weights):
    nres, part = node.shape
    dn = part * parts
    cap = req.shape[2]
    slots, cw, _ = edges.shape
    units = weights[0].shape[1]
    rows = slots * nres
    tabn = nres + groups * cap
    height = tabn + nres + 256
    rp = nres // parts
    levels = groups.bit_length() - 1
    wide, narrow = dn // groups, cw // groups
    total = 2 * dn + cw
    S, V = jax.ShapeDtypeStruct, pltpu.VMEM
    split = lambda lead, r: V((lead,) + (2,) * levels + (r, units), BF)

    def recv(lead, r):
        return [V((lead,) + (2,) * (levels - 1 - k) + (r, units), BF) for k in range(levels)]

    node_rows = lambda dtype: V((rp, dn), dtype)
    full_rows = lambda dtype: V((nres, dn), dtype)
    table = lambda dtype: V((tabn, dn), dtype)
    scratch = [
        V((parts, 4, units, dn), BF),
        V((parts, 2, units, dn), BF),
        V((parts, nres, part), BF),
        V((parts, nres, part), BF),
        full_rows(BF),
        full_rows(BF),
        node_rows(BF),
        node_rows(BF),
        full_rows(BF),
        V(req.shape, jnp.int32),
        V((groups, cap, dn), BF),
        V((groups, cap, dn), BF),
        table(BF),
        table(BF),
        V((dn, tabn), BF),
        V(edges.shape, BF),
        V(edges.shape, BF),
        V(edges.shape, BF),
        V((height, rows), BF),
        V((units, height), BF),
        V((cw, units), BF),
        V((cw, rows), F32),
        V((parts, units, nres), BF),
        full_rows(BF),
        full_rows(BF),
        V((parts, rp, dn), BF),
        V((parts, rp, dn), BF),
        V((cw, rows), BF),
        V((2, units, rows), BF),
        V((parts, rp, part), BF),
        full_rows(BF),
        node_rows(F32),
        V((parts, rp, units), BF),
        V((parts, rp, units), BF),
        node_rows(BF),
        V((1, dn), F32),
        V((units, nres), F32),
        table(F32),
        table(BF),
        V((slots, 1, nres), jnp.int32),
        V((cw, nres), F32),
        V((parts, nres, units), BF),
        split(parts, wide),
        split(parts, narrow),
        split(parts, narrow),
        V((parts, nres, units), BF),
        V((parts, units, nres), BF),
        V((nres, units), BF),
        V((nres, units), BF),
        full_rows(BF),
        V((groups, cap, dn), BF),
        full_rows(BF),
        V((parts, rp, dn), BF),
        V((parts, rp, part), F32),
        V((1, total), F32),
        V((parts, 1, total), F32),
        V((groups, 1, total), F32),
        V((parts, wide, units), BF),
        V((parts, narrow, units), BF),
        V((parts, narrow, units), BF),
    ]
    for _ in range(parts):
        scratch += recv(1, wide) + recv(1, narrow) + recv(1, narrow)
    for _ in range(4):
        scratch += [split(1, wide)] + recv(1, wide)
    copies = (
        15 * (parts - 1)
        + 5 * (groups - 1)
        + 6 * (parts - 1) * (1 + levels)
        + (3 * parts + 4) * levels
        + 3 * (parts - 1)
    )
    scratch += [
        pltpu.SemaphoreType.DMA((copies,)),
        pltpu.SemaphoreType.DMA((copies,)),
        pltpu.SemaphoreType.DMA((9,)),
        pltpu.SemaphoreType.DMA((2,)),
        pltpu.SemaphoreType.DMA((1 + slots,)),
    ]
    vm = pl.BlockSpec(memory_space=pltpu.VMEM)
    hbm = pl.BlockSpec(memory_space=pltpu.MemorySpace.HBM)
    return pl.pallas_call(
        functools.partial(layer_kernel, groups, parts),
        in_specs=[vm] * 8 + [hbm] * 9,
        out_specs=[vm] * 10 + [hbm] * 3,
        out_shape=[
            S((nres, part), BF),
            S((nres, part), F32),
            S((wide, units), F32),
            S((wide, units), F32),
            S((narrow, units), F32),
            S((wide, units), F32),
            S((narrow, units), F32),
            S((wide, units), F32),
            S((wide, units), F32),
            S((1, total), F32),
            S(edges.shape, BF),
            S(edges.shape, F32),
            S((parts, units, rows), BF),
        ],
        scratch_shapes=scratch,
        compiler_params=pltpu.CompilerParams(
            collective_id=0, has_side_effects=True, vmem_limit_bytes=62 << 20
        ),
        name="layer",
    )(node, ncot, req, nbr, egain, counts, ngain, fgain, edges, ecot, *weights)


def publish_kernel(groups, sizes, *refs):
    count = (len(refs) - 7) // 3
    ins, vec_ref = refs[:count], refs[count]
    outs, gains = refs[count + 1 : 2 * count + 1], refs[2 * count + 1 : 2 * count + 4]
    stage, (table, sems, out_sems) = refs[2 * count + 4 : 3 * count + 4], refs[3 * count + 4 :]
    loads = [pltpu.make_async_copy(a, b, sems.at[k]) for k, (a, b) in enumerate(zip(ins, stage))]
    saves = [pltpu.make_async_copy(a, b, out_sems.at[k]) for k, (a, b) in enumerate(zip(stage, outs))]
    start(loads)
    begin = 0
    for size, out in zip(sizes, gains):
        each = size // groups
        for q in range(groups):
            table[q : q + 1, :each] = vec_ref[:, begin + q * each : begin + (q + 1) * each]
        begin += size
        out[...] = table[pl.ds(lax.axis_index("res"), 1), :each]
    for load, save in zip(loads, saves):
        load.wait()
        save.start()
    for save in saves:
        save.wait()


def publish(groups, sizes, arrays, vec):
    S = jax.ShapeDtypeStruct
    vm = pl.BlockSpec(memory_space=pltpu.VMEM)
    hbm = pl.BlockSpec(memory_space=pltpu.MemorySpace.HBM)
    return pl.pallas_call(
        functools.partial(publish_kernel, groups, sizes),
        in_specs=[hbm] * len(arrays) + [vm],
        out_specs=[hbm] * len(arrays) + [vm] * len(sizes),
        out_shape=[S(a.shape, a.dtype) for a in arrays]
        + [S((1, size // groups), F32) for size in sizes],
        scratch_shapes=[pltpu.VMEM(a.shape, a.dtype) for a in arrays]
        + [
            pltpu.VMEM((groups, 128), F32),
            pltpu.SemaphoreType.DMA((len(arrays),)),
            pltpu.SemaphoreType.DMA((len(arrays),)),
        ],
        compiler_params=pltpu.CompilerParams(vmem_limit_bytes=60 << 20),
        name="publish",
    )(*arrays, vec)


def per_device(
    node_state,
    edge_state,
    node_gain,
    edge_gain,
    ffn_gain,
    w_self,
    w_neigh,
    w_edge,
    w_message,
    w_update,
    w_expand,
    w_contract,
    neighbours,
    requests,
    counts,
    node_cotangent,
    edge_cotangent,
):
    groups, parts = lax.axis_size("res"), lax.axis_size("hid")
    nres, slot_part, cw = edge_state.shape
    ngain, egain, fgain = node_gain[None], edge_gain[None], ffn_gain[None]
    edges = edge_state.transpose(1, 2, 0)
    cot = edge_cotangent.transpose(1, 2, 0)
    node_two, gnode, gws, gwn, gwe, gwm, gwu, gwx, gwc, vec, e2, ge, _slopes = layer(
        groups,
        parts,
        node_state,
        node_cotangent,
        requests[0][:, None, :],
        neighbours.T,
        egain,
        counts[None],
        ngain,
        fgain,
        edges,
        cot,
        [w_neigh, w_self, w_edge, w_update.T, w_message, w_expand, w_contract],
    )
    dn = ngain.shape[1]
    node_two, gnode, gws, gwn, gwe, gwm, gwu, gwx, gwc, e2, ge, gng, gfg, geg = publish(
        groups, (dn, dn, cw), (node_two, gnode, gws, gwn, gwe, gwm, gwu, gwx, gwc, e2, ge), vec
    )
    return (
        node_two,
        e2.transpose(2, 0, 1),
        gnode,
        ge.transpose(2, 0, 1),
        gng[0],
        geg[0],
        gfg[0],
        gws,
        gwn,
        gwe,
        gwm.T,
        gwu.T,
        gwx,
        gwc.T,
    )


def solution(mesh):
    return jax.shard_map(
        per_device,
        mesh=mesh,
        in_specs=(
            P("res", "hid"),
            P("res", "hid", None),
            P(),
            P(),
            P(),
            P(None, "hid"),
            P(None, "hid"),
            P(None, "hid"),
            P("hid", None),
            P("hid", None),
            P(None, "hid"),
            P("hid", None),
            P("res", None),
            P("res", None, None),
            P("res"),
            P("res", "hid"),
            P("res", "hid", None),
        ),
        out_specs=(
            P("res", "hid"),
            P("res", "hid", None),
            P("res", "hid"),
            P("res", "hid", None),
            P("res"),
            P("res"),
            P("res"),
            P("res", "hid"),
            P("res", "hid"),
            P("res", "hid"),
            P("hid", "res"),
            P("hid", "res"),
            P("res", "hid"),
            P("hid", "res"),
        ),
        check_vma=False,
    )
```

```python
import functools

import jax
import jax.numpy as jnp
from jax import lax
from jax.experimental import pallas as pl
from jax.experimental.pallas import tpu as pltpu
from jax.sharding import PartitionSpec as P

F32, BF = jnp.float32, jnp.bfloat16
EPSILON = 1e-05
TANH_SCALE = 0.7978845608028654
TANH_CUBE = 0.044715
MESH = pl.DeviceIdType.MESH
GAP = 2
NEIGH, SELF, MESSAGE = range(3)
EXPAND, CONTRACT = range(2)


def contract(a, b, dim_a, dim_b):
    return lax.dot_general(
        a, b, (((dim_a,), (dim_b,)), ((), ())), preferred_element_type=F32
    )


def nn(a, b):
    return contract(a, b, 1, 0)


def nt(a, b):
    return contract(a, b, 1, 1)


def tn(a, b):
    return contract(a, b, 0, 0)


def normalize(values, axis):
    centred = values - jnp.mean(values, axis, keepdims=True)
    scaling = lax.rsqrt(jnp.mean(centred * centred, axis, keepdims=True) + EPSILON)
    return centred * scaling, scaling


def norm_back(grad, unit, scaling, gain, axis):
    scaled = grad * gain
    return scaling * (
        scaled
        - jnp.mean(scaled, axis, keepdims=True)
        - unit * jnp.mean(scaled * unit, axis, keepdims=True)
    )


def gelu(x):
    return (0.5 * x) * (1.0 + jnp.tanh(x * (TANH_SCALE + TANH_SCALE * TANH_CUBE * (x * x))))


def gelu_pair(x):
    square = x * x
    bent = jnp.tanh(x * (TANH_SCALE + TANH_SCALE * TANH_CUBE * square))
    half = 0.5 * x
    slope = 0.5 + 0.5 * bent + half * (1.0 - bent * bent) * (
        TANH_SCALE + 3 * TANH_SCALE * TANH_CUBE * square
    )
    return half + half * bent, slope


class Net:
    def __init__(self, send_sems, recv_sems):
        self.send_sems, self.recv_sems, self.count, self.sent = send_sems, recv_sems, 0, []

    def make(self, src, dst, device):
        k = self.count
        self.count += 1
        copy = pltpu.make_async_remote_copy(
            src_ref=src,
            dst_ref=dst,
            send_sem=self.send_sems.at[k],
            recv_sem=self.recv_sems.at[k],
            device_id=device,
            device_id_type=MESH,
        )
        self.sent.append(copy)
        return copy

    def push(self, src, dst, device):
        copy = self.make(src, dst, device)
        copy.start()
        return copy

    def finish(self):
        for copy in self.sent:
            copy.wait_send()


def start(copies):
    for copy in copies:
        copy.start()


def arrived(copies):
    for copy in copies:
        copy.wait_recv()


def flip_bit(index, bit):
    step = 1 << bit
    return index + step - 2 * step * ((index // step) % 2)


def greet(devices):
    barrier = pltpu.get_barrier_semaphore()
    for device in devices:
        pl.semaphore_signal(barrier, inc=1, device_id=device, device_id_type=MESH)


def greeted(devices):
    pl.semaphore_wait(pltpu.get_barrier_semaphore(), len(devices))


def place(groups, parts):
    p, h = lax.axis_index("res"), lax.axis_index("hid")
    line = [None] + [(p, lax.rem(h + i, parts)) for i in range(1, parts)]
    plane = [None] + [(lax.rem(p + i, groups), h) for i in range(1, groups)]
    return p, h, line, plane


class Rows:
    def __init__(self, net, p, groups, plane, nres, cap, tab_ref, rows_buf):
        self.mine = pl.ds(pl.multiple_of(nres + p * cap, 16), cap)
        self.asked = [lax.rem(p + i, groups) for i in range(groups)]
        self.nres, self.cap, self.tab, self.buf = nres, cap, tab_ref, rows_buf
        self.copies = [
            net.make(rows_buf.at[i], tab_ref.at[self.mine, :], plane[i]) for i in range(1, groups)
        ]

    def send(self, normed, sid_ref):
        ids = lax.broadcasted_iota(jnp.int32, (self.nres, self.cap), 0)
        self.tab[: self.nres, :] = normed
        for i, q in enumerate(self.asked):
            chosen = jnp.where(ids == sid_ref[q], 1.0, 0.0).astype(BF)
            rows = tn(chosen, normed).astype(BF)
            if i == 0:
                self.tab[self.mine, :] = rows
            else:
                self.buf[i] = rows
                self.copies[i - 1].start()


class Gather:
    def __init__(self, net, p, h, groups, parts, units, depth):
        self.levels = groups.bit_length() - 1
        low, half = p % 2, p // 2
        turned = sum(
            ((half // (1 << b)) % 2) * (1 << (self.levels - 2 - b)) for b in range(self.levels - 1)
        )
        starts = [low * (groups // 2) + half, low * (groups // 2) + turned]
        rows = depth // groups
        back = [(p, lax.rem(h + parts - i, parts)) for i in range(parts)]
        self.lag = 2 * (self.levels + 1)
        self.batches = []
        for u, (full, w, r) in enumerate(units):
            stages, turn = [], u % 2
            begin = starts[turn]
            own = pl.ds(pl.multiple_of(begin * rows, rows), rows)
            stages.append(net.make(full.at[0, w, own, :], full.at[r, w, own, :], back[r]))
            for level in range(self.levels):
                if level == self.levels - 1:
                    bit = 0
                else:
                    bit = 1 + (level if turn == 0 else self.levels - 2 - level)
                span = rows << level
                held = (begin // (1 << level)) * span
                view = full.at[r, w, pl.ds(pl.multiple_of(held, span), span), :]
                stages.append(net.make(view, view, (flip_bit(p, bit), h)))
            self.batches.append(stages)
        self.slots = len(units) + self.lag

    def turn(self, slot):
        for stage in range(self.levels + 1, -1, -1):
            b = slot - 2 * stage
            if 0 <= b < len(self.batches):
                if stage:
                    self.batches[b][stage - 1].wait_recv()
                if stage <= self.levels:
                    self.batches[b][stage].start()


def bits_of(index, levels):
    return tuple((index >> b) & 1 for b in range(levels - 1, -1, -1))


def fill_rows(ref, value, lead):
    levels = len(ref.shape) - 3
    rows = ref.shape[-2]
    for s in range(1 << levels):
        ref[(lead,) + bits_of(s, levels)] = value[s * rows : (s + 1) * rows, :]


class PlaneSum:
    def __init__(self, net, p, h, levels, order, source, recv, done):
        self.levels, self.source, self.recv, self.done = levels, source, recv, done
        own = [(p // (1 << bit)) % 2 for bit in range(levels)]
        self.fixed, self.copies = [], []
        fixed = {}
        for level in range(levels):
            bit = 0 if level == 0 else (level if order == 0 else levels - level)
            other = dict(fixed)
            other[bit] = 1 - own[bit]
            fixed = dict(fixed)
            fixed[bit] = own[bit]
            self.fixed.append(fixed)
            self.copies.append(
                net.make(source.at[self.index(other)], recv[level], (flip_bit(p, bit), h))
            )

    def index(self, fixed):
        return (slice(None),) + tuple(
            fixed.get(bit, slice(None)) for bit in range(self.levels - 1, -1, -1)
        )

    def held(self):
        return self.source.at[self.index(self.fixed[-1])]

    def steps(self):
        return [functools.partial(self.step, level) for level in range(self.levels + 1)]

    def step(self, level):
        if level:
            k = level - 1
            self.copies[k].wait_recv()
            free = [bit for bit in range(self.levels) if bit not in self.fixed[k]]
            for n in range(1 << len(free)):
                fixed = dict(self.fixed[k])
                for j, bit in enumerate(free):
                    fixed[bit] = (n >> j) & 1
                at = self.index(fixed)
                got = (slice(None),) + tuple(fixed[bit] for bit in reversed(free))
                total = self.source[at].astype(F32) + self.recv[k][got].astype(F32)
                if level == self.levels and self.done(total):
                    continue
                self.source[at] = total.astype(BF)
        if level < self.levels:
            self.copies[level].start()


def build_inputs(a_ref, edges, v_ref, egain, tabn):
    slots, cw, nres = edges.shape
    index = lax.broadcasted_iota(jnp.int32, (tabn, nres), 0)
    own = lax.broadcasted_iota(jnp.int32, (nres, nres), 0) == lax.broadcasted_iota(
        jnp.int32, (nres, nres), 1
    )
    own = jnp.where(own, 1.0, 0.0).astype(BF)
    height = a_ref.shape[0]

    def one(k, _):
        cs = pl.ds(pl.multiple_of(k * nres, nres), nres)
        a_ref[:tabn, cs] = jnp.where(index == v_ref[k], 1.0, 0.0).astype(BF)
        a_ref[tabn : tabn + nres, cs] = own
        unit, _scale = normalize(edges[k].astype(F32), 0)
        a_ref[tabn + nres : tabn + nres + cw, cs] = (unit * egain).astype(BF)
        a_ref[tabn + nres + cw :, cs] = jnp.zeros((height - tabn - nres - cw, nres), BF)
        return 0

    lax.fori_loop(0, slots, one, 0)


def edge_chunk(c, w_ref, pair_ref, tab, a_ref, bt, wut, v_ref, upd, mean, inverse, cw, pause, second=None):
    tabn, nres = tab.shape[0], mean.shape[-1]
    slots = a_ref.shape[1] // nres
    bt[:, :tabn] = nt(w_ref[c, NEIGH], tab[...]).astype(BF)
    bt[:, tabn : tabn + nres] = nt(w_ref[c, SELF], tab[:nres, :]).astype(BF)
    bt[:, tabn + nres :] = pair_ref[c, 0, :, :256]
    wut[...] = pair_ref[c, 0, :, 2 * cw - 256 :].T[256 - cw :]
    pause(0)
    before = nn(bt[...], a_ref[...])
    pause(1)
    square = before * before
    gate = 0.5 + 0.5 * jnp.tanh(before * (TANH_SCALE + TANH_SCALE * TANH_CUBE * square))
    if second is not None:
        dg, gup, gwu = second
        bend = (2 * TANH_SCALE + 6 * TANH_SCALE * TANH_CUBE * square) * (1.0 - gate)
    total, kept = None, []
    for k in range(slots):
        cs = slice(k * nres, (k + 1) * nres)
        open_gate = gate[:, cs] * (v_ref[k] >= 0).astype(F32)
        part = before[:, cs] * open_gate
        total = part if total is None else total + part
        kept.append(part.astype(BF))
        if second is not None:
            dg[:, cs] = (open_gate + part * bend[:, cs]).astype(BF)
    mean[c] = (total * inverse).astype(BF)
    kept = jnp.concatenate(kept, axis=1)
    upd[...] += nn(wut[...], kept)
    if second is not None:
        fill_rows(gwu, nt(gup[256 - cw :, :], kept).astype(BF), c)


def message_part(w_ref, mean, parts):
    total = None
    for c in range(parts):
        term = tn(mean[c], w_ref[c, MESSAGE])
        total = term if total is None else total + term
    return total.astype(BF)


def add_update(edges, upd, out):
    slots, _, nres = edges.shape
    for k in range(slots):
        out[k] = (edges[k].astype(F32) + upd[:, k * nres : (k + 1) * nres]).astype(BF)


class Plan:
    def __init__(self):
        self.points, self.active, self.now = {}, [], 0

    def add(self, point, steps):
        steps = list(steps)
        self.note(point, steps.pop(0))
        if steps:
            self.active.append([self.now, steps])

    def note(self, point, step):
        self.points.setdefault(point, []).append(step)

    def advance(self, point, gap=1):
        self.now += 1
        for item in self.active:
            if self.now - item[0] >= gap:
                self.note(point, item[1].pop(0))
                item[0] = self.now
        self.active = [item for item in self.active if item[1]]

    def run(self, point):
        for step in self.points.get(point, ()):
            step()


def plane_scratch(groups, lead, rows, units, order, last):
    recv, acc = [], []
    count = groups
    while count > 1:
        count //= 2
        recv.append(pltpu.VMEM((lead, count, rows, units), BF))
        if count == 1:
            acc.append(pltpu.VMEM((lead, rows, units), last))
        elif order == 0:
            acc.append(pltpu.VMEM((lead, count // 2, 2, rows, units), BF))
        else:
            acc.append(pltpu.VMEM((lead, 2, count // 2, rows, units), BF))
    return recv + acc


def layer_kernel(groups, parts, *refs):
    (node_ref, ncot_ref, req_ref, nbr_ref, egain_ref, count_ref, ngain_ref, fgain_ref) = refs[:8]
    (edges_hbm, ecot_hbm, wn_hbm, ws_hbm, we_hbm, wu_hbm, wm_hbm, wx_hbm, wc_hbm) = refs[8:17]
    (nn_ref, gnode_ref, ows_ref, own_ref, owe_ref, owm_ref, owu_ref, owx_ref, owc_ref, ovec_ref) = refs[17:27]
    (e2_hbm, ge_hbm, dg_hbm) = refs[27:30]
    refs = list(refs[30:])

    def take(count):
        taken = refs[:count]
        del refs[:count]
        return taken

    w_ref, pair_ref, wf_ref, nbuf, cbuf, nfull, cf, xrows, x1, xf, sid = take(11)
    rows0, rows1, tab0, tab1, tabt, edges, e1, cot, a_ref, bt = take(10)
    wut, upd, mean, msg0, msg1, mbuf0, mbuf1, gup, dgbuf = take(9)
    nsp, gm, act, gex, fi, fg, gt, gta, gtab = take(9)
    v_ref, ecol = take(2)
    gown, first_n, first_e, gwu, zown, zmean, actf, gexf, fif, ret = take(10)
    gsend, gbuf, stat, uslice, gslice, mslice, vec, vz, vp, zn, ze, zu = take(12)
    ss, rs, ls, ds, os_ = refs[-5:]
    p, h, line, plane = place(groups, parts)
    nres, part = node_ref.shape
    dn = part * parts
    cap = req_ref.shape[2]
    slots, cw, _ = edges.shape
    rp = nres // parts
    units = w_ref.shape[2]
    tabn = tab0.shape[0]
    levels = groups.bit_length() - 1
    mine = pl.ds(pl.multiple_of(h * rp, rp), rp)
    home = pl.ds(pl.multiple_of(nres + p * cap, 16), cap)
    asked = [lax.rem(p + groups - i, groups) for i in range(groups)]
    inverse = 1.0 / count_ref[...].astype(F32)

    raw = [a_ref.at[:dn, k * units : (k + 1) * units] for k in range(3)]
    raw_e = [a_ref.at[dn + k * cw : dn + (k + 1) * cw, :units] for k in range(2)]
    loads = [
        pltpu.make_async_copy(src, dst, ls.at[k])
        for k, (src, dst) in enumerate(
            (
                (wn_hbm, raw[0]),
                (we_hbm, raw_e[0]),
                (wu_hbm, raw_e[1]),
                (ws_hbm, raw[1]),
                (wx_hbm, raw[2]),
                (edges_hbm, edges),
                (wm_hbm, w_ref.at[0, MESSAGE]),
                (wc_hbm, wf_ref.at[0, CONTRACT]),
                (ecot_hbm, cot),
            )
        )
    ]
    start(loads)
    net = Net(ss, rs)

    def to_parts(pair):
        copies = []
        for i in range(1, parts):
            src, dst = pair(i, lax.rem(h + i, parts))
            copies.append(net.make(src, dst, line[i]))
        return copies

    def rows_of(other):
        return pl.ds(pl.multiple_of(other * rp, rp), rp)

    node_copies = to_parts(lambda i, o: (node_ref, nbuf.at[h]))
    req_copies = [
        net.make(req_ref.at[lax.rem(p + i, groups)], sid.at[p], plane[i]) for i in range(1, groups)
    ]
    ncot_copies = to_parts(lambda i, o: (ncot_ref, cbuf.at[h]))
    rows_first = Rows(net, p, groups, plane, nres, cap, tab0, rows0)
    rows_next = Rows(net, p, groups, plane, nres, cap, tab1, rows1)
    message0 = to_parts(lambda i, o: (msg0.at[rows_of(o), :], mbuf0.at[i]))
    message1 = to_parts(lambda i, o: (msg1.at[rows_of(o), :], mbuf1.at[i]))
    x1_copies = to_parts(lambda i, o: (x1, xf.at[mine, :]))
    edge_units = []
    for r in range(1, parts):
        edge_units += [(w_ref, NEIGH, r), (pair_ref, 0, r), (w_ref, SELF, r)]
    edge_units += [(w_ref, MESSAGE, r) for r in range(1, parts)]
    node_units = [(wf_ref, w, r) for w in (EXPAND, CONTRACT) for r in range(1, parts)]
    gather = Gather(net, p, h, groups, parts, edge_units + node_units, units)
    chunk_slots = [0] + [3 * k - 1 + gather.lag for k in range(1, parts)]
    message_slot, expand_slot = ((3 + k) * (parts - 1) - 1 + gather.lag for k in (1, 2))
    gm_copies = to_parts(lambda i, o: (gm.at[mine, :], gm.at[mine, :]))
    nn_copies = to_parts(lambda i, o: (nsp.at[o], nn_ref.at[mine, :]))
    ret_copies = [
        net.make(
            gtab.at[pl.ds(pl.multiple_of(nres + lax.rem(p + i, groups) * cap, 16), cap), :],
            ret.at[i],
            plane[i],
        )
        for i in range(1, groups)
    ]
    own_copies = to_parts(lambda i, o: (gown.at[i], zown.at[i]))
    mean_copies = to_parts(lambda i, o: (mean.at[i], zmean.at[i]))
    act_copies = to_parts(lambda i, o: (act.at[i], actf.at[mine, :]))
    gex_copies = to_parts(lambda i, o: (gex.at[i], gexf.at[mine, :]))
    fi_copies = to_parts(lambda i, o: (fi, fif.at[mine, :]))
    slice_copies = to_parts(lambda i, o: (gsend.at[o], gbuf.at[i]))
    stat_copies = to_parts(lambda i, o: (stat.at[0], stat.at[i]))
    vec_line = to_parts(lambda i, o: (vec, vz.at[i]))
    vec_plane = [net.make(vp.at[0], vp.at[i], plane[i]) for i in range(1, groups)]

    chunk_sums, chunk_line, chunk_own = {}, {}, {}
    for c in range(parts):
        for name, source, order, landing in (
            ("neigh", first_n, 0, zn),
            ("edge", first_e, 1, ze),
            ("update", gwu, c % 2, zu),
        ):
            recv = take(levels)
            item = PlaneSum(
                net, p, h, levels, order, source.at[pl.ds(c, 1)], recv, lambda total: False
            )
            steps = item.steps()
            if c:
                copy = net.make(item.held().at[0], landing.at[c], line[c])
                chunk_line[name, c] = copy
                last = steps.pop()

                def send_on(last=last, copy=copy):
                    last()
                    copy.start()

                steps.append(send_on)
            else:
                chunk_own[name] = item
            chunk_sums[name, c] = steps
    def unit_sum(order, out):
        source = take(1)[0]

        def done(total):
            out[...] = total[0]
            return True

        item = PlaneSum(net, p, h, levels, order, source, take(levels), done)

        def fill(value):
            fill_rows(source, value.astype(BF), 0)

        return fill, item.steps()

    fill_self, steps_self = unit_sum(0, ows_ref)
    fill_message, steps_message = unit_sum(1, owm_ref)
    fill_expand, steps_expand = unit_sum(0, owx_ref)
    fill_contract, steps_contract = unit_sum(1, owc_ref)

    peers = line[1:] + plane[1:]
    greet(peers)
    nbuf[h] = node_ref[...]
    cbuf[h] = ncot_ref[...]
    sid[p] = req_ref[p]
    loads[0].wait()
    w_ref[0, NEIGH] = raw[0][...].T
    greeted(peers)
    start(node_copies)
    start(req_copies)
    gather.turn(0)
    loads[1].wait()
    loads[2].wait()
    pair_ref[0, 0] = a_ref[dn : dn + 2 * cw, :units].T
    gather.turn(1)
    counts = count_ref[...]
    for k in range(slots):
        row = nbr_ref[pl.ds(h * slots + k, 1), :]
        v_ref[k] = jnp.where(h * slots + k < counts, row, -1)
    ecol[...] = jnp.broadcast_to(egain_ref[...], (nres, cw)).T
    arrived(node_copies)
    for c in range(parts):
        nfull[:, c * part : (c + 1) * part] = nbuf[c]
    unit_node, _scale = normalize(nfull[...].astype(F32), 1)
    normed = (unit_node * ngain_ref[...]).astype(BF)
    xrows[...] = nfull[mine, :]
    arrived(req_copies)
    rows_first.send(normed, sid)
    start(ncot_copies)
    loads[3].wait()
    w_ref[0, SELF] = raw[1][...].T
    gather.turn(2)
    loads[4].wait()
    wf_ref[0, EXPAND] = raw[2][...].T
    gather.turn(3)
    loads[5].wait()
    egain = ecol[...]
    build_inputs(a_ref, edges, v_ref, egain, tabn)
    gather.turn(4)
    loads[6].wait()
    loads[7].wait()
    arrived(ncot_copies)
    for c in range(parts):
        cf[:, c * part : (c + 1) * part] = cbuf[c]
    upd[...] = jnp.zeros_like(upd)
    gather.turn(5)
    first_slot = 6
    arrived(rows_first.copies)

    slot = first_slot
    turns_at = {}
    for k in range(parts):
        upto = max(slot + (k == 0), chunk_slots[k] + 1)
        turns_at["begin", k] = range(slot, min(upto, gather.slots))
        turns_at[0, k] = range(upto, min(upto + 1, gather.slots))
        turns_at[1, k] = range(upto + 1, min(upto + 2, gather.slots))
        slot = min(upto + 2, gather.slots)

    def turns(c, at):
        for k in range(parts):
            if len(turns_at[at, k]):

                @pl.when(c == k)
                def _():
                    for s in turns_at[at, k]:
                        gather.turn(s)

    def first_chunk(c, _):
        turns(c, "begin")
        pause = lambda at: turns(c, at)
        edge_chunk(c, w_ref, pair_ref, tab0, a_ref, bt, wut, v_ref, upd, mean, inverse, cw, pause)
        return 0

    lax.fori_loop(0, parts, first_chunk, 0)
    for s in range(slot, message_slot + 1):
        gather.turn(s)
    slot = max(slot, message_slot + 1)
    msg0[...] = message_part(w_ref, mean, parts)
    start(message0)
    if slot < gather.slots:
        gather.turn(slot)
        slot += 1
    add_update(edges, upd, e1)
    build_inputs(a_ref, e1, v_ref, egain, tabn)
    middle = xrows[...].astype(F32) + msg0[mine, :].astype(F32)
    for i, copy in enumerate(message0):
        copy.wait_recv()
        middle = middle + mbuf0[i + 1].astype(F32)
    unit_ffn, _scale = normalize(middle, 1)
    ffn_input = (unit_ffn * fgain_ref[...]).astype(BF)
    for s in range(slot, expand_slot + 1):
        gather.turn(s)
    slot = max(slot, expand_slot + 1)
    hidden = [gelu(nt(ffn_input, wf_ref[c, EXPAND])).astype(BF) for c in range(parts)]
    for s in range(slot, gather.slots):
        gather.turn(s)
    out = middle
    for c in range(parts):
        out = out + nn(hidden[c], wf_ref[c, CONTRACT])
    out = out.astype(BF)
    upd[...] = jnp.zeros_like(upd)
    x1[...] = out
    xf[mine, :] = out
    start(x1_copies)
    loads[8].wait()
    gup[: 256 - cw, :] = jnp.zeros((256 - cw, slots * nres), BF)
    for k in range(slots):
        live = (v_ref[k] >= 0).astype(F32)
        gup[256 - cw :, k * nres : (k + 1) * nres] = (cot[k].astype(F32) * live).astype(BF)
    arrived(x1_copies)
    unit_full, _scale = normalize(xf[...].astype(F32), 1)
    rows_next.send((unit_full * ngain_ref[...]).astype(BF), sid)
    arrived(rows_next.copies)

    def ffn_sums():
        arrived(act_copies + gex_copies + fi_copies)
        fill_expand(tn(fif[...], gexf[...]))
        fill_contract(tn(cf[...], actf[...]))

    def message_sums():
        value = mean[0].astype(F32)
        arrived(mean_copies)
        for i in range(1, parts):
            value = value + zmean[i].astype(F32)
        fill_message(tn(gm[...], value.astype(BF).T))

    plan = Plan()
    for i in range(parts):
        plan.advance(("second", i))
        c = (i + 1) % parts
        if c:
            plan.note(("second", i), mean_copies[c - 1].start)
        plan.add(("second", i), chunk_sums["update", c])
    for name in ("node", "ffn"):
        plan.advance((name, 0))
    for i in range(parts):
        plan.advance(("early", i), GAP)
        if i == min(1, parts - 1):
            plan.note(("early", i), ffn_sums)
            plan.add(("early", i), steps_expand)
            plan.add(("early", i), steps_contract)
        c = (i + 1) % parts
        if c:
            plan.note(("late", i), own_copies[c - 1].start)
        plan.advance(("late", i), GAP)
        if c:
            for name in ("neigh", "edge"):
                plan.add(("late", i), chunk_sums[name, c])
        if i == 0:
            plan.note(("late", i), message_sums)
            plan.add(("late", i), steps_message)
    plan.advance(("tail", 0))
    for name in ("neigh", "edge"):
        plan.add(("tail", 0), chunk_sums[name, 0])
    plan.add(("tail", 1), steps_self)
    tail = 2
    while plan.active:
        plan.advance(("tail", tail))
        tail += 1

    def points(i, name):
        for k in range(parts):
            if (name, k) in plan.points:

                @pl.when(i == k)
                def _():
                    plan.run((name, k))

    def save(i):
        return pltpu.make_async_copy(dgbuf.at[i % 2], dg_hbm.at[lax.rem(i + 1, parts)], ds.at[i % 2])

    def second_chunk(i, _):
        @pl.when(i >= 2)
        def _():
            save(i - 2).wait()

        edge_chunk(
            lax.rem(i + 1, parts),
            w_ref,
            pair_ref,
            tab1,
            a_ref,
            bt,
            wut,
            v_ref,
            upd,
            mean,
            inverse,
            cw,
            lambda at: None,
            (dgbuf.at[i % 2], gup, gwu),
        )
        save(i).start()
        points(i, "second")
        return 0

    lax.fori_loop(0, parts, second_chunk, 0)
    msg1[...] = message_part(w_ref, mean, parts)
    start(message1)
    plan.run(("node", 0))
    add_update(e1, upd, edges)
    e2_copy = pltpu.make_async_copy(edges, e2_hbm, os_.at[0])
    e2_copy.start()
    tabt[...] = tab1[...].T
    middle = x1[...].astype(F32) + msg1[mine, :].astype(F32)
    for i, copy in enumerate(message1):
        copy.wait_recv()
        middle = middle + mbuf1[i + 1].astype(F32)
    unit_ffn, scaling = normalize(middle, 1)
    ffn_input = (unit_ffn * fgain_ref[...]).astype(BF)
    fi[...] = ffn_input
    cotangent = cf[mine, :]
    g_input = jnp.zeros((rp, dn), F32)
    for c in range(parts):
        active, slope = gelu_pair(nt(ffn_input, wf_ref[c, EXPAND]))
        act[c] = active.astype(BF)
        g_expand = (nt(cotangent, wf_ref[c, CONTRACT]) * slope).astype(BF)
        gex[c] = g_expand
        g_input = g_input + nn(g_expand, wf_ref[c, EXPAND])
    g_middle = cotangent.astype(F32) + norm_back(g_input, unit_ffn, scaling, fgain_ref[...], 1)
    gm[mine, :] = g_middle.astype(BF)
    start(gm_copies)
    fg[...] = jnp.sum(g_input * unit_ffn, 0, keepdims=True)
    out = middle
    for c in range(parts):
        out = out + nn(act[c], wf_ref[c, CONTRACT])
    out = out.astype(BF)
    for c in range(parts):
        nsp[c] = out[:, c * part : (c + 1) * part]
    start(nn_copies)
    nn_ref[mine, :] = nsp[h]
    actf[mine, :] = act[0]
    gexf[mine, :] = gex[0]
    fif[mine, :] = fi[...]
    upd[...] = jnp.zeros_like(upd)
    gta[...] = jnp.zeros_like(gta)
    for c in range(max(parts - 2, 0), parts):
        save(c).wait()
    arrived(gm_copies)
    start(act_copies)
    start(gex_copies)
    start(fi_copies)
    plan.run(("ffn", 0))

    def fetch(i):
        return pltpu.make_async_copy(dg_hbm.at[lax.rem(i + 1, parts)], dgbuf.at[i % 2], ds.at[i % 2])

    fetch(0).start()
    gen = upd

    def back_chunk(i, _):
        c = lax.rem(i + 1, parts)

        @pl.when(i + 1 < parts)
        def _():
            fetch(i + 1).start()

        gt[...] = nt(w_ref[c, MESSAGE], gm[...]) * inverse
        wut[...] = pair_ref[c, 0, :, :256].T[:cw]
        fetch(i).wait()
        buf = dgbuf.at[i % 2]
        grad = nn(pair_ref[c, 0, :, 2 * cw - 256 :], gup[...])
        grad = grad + jnp.concatenate([gt[...]] * slots, axis=1)
        grad = (grad * buf[...].astype(F32)).astype(BF)
        buf[...] = grad
        gen[...] += nn(wut[...], grad)
        points(i, "early")
        total = nt(a_ref[: tabn + nres + cw, :], buf[...])
        gp = total[:tabn].astype(BF)
        go = total[tabn : tabn + nres].astype(BF)
        gown[c] = go
        gta[...] += nn(gp, w_ref[c, NEIGH])
        gta[:nres, :] += nn(go, w_ref[c, SELF])

        @pl.when(i == parts - 1)
        def _():
            gtab[...] = gta[...].astype(BF)
            start(ret_copies)

        fill_rows(first_e, total[tabn + nres :].astype(BF), c)
        fill_rows(first_n, nn(tabt[...], gp).astype(BF), c)
        points(i, "late")
        return 0

    lax.fori_loop(0, parts, back_chunk, 0)
    plan.run(("tail", 0))
    value = gown[0].astype(F32)
    arrived(own_copies)
    for i in range(1, parts):
        value = value + zown[i].astype(F32)
    fill_self(tn(tab1[:nres, :], value.astype(BF)))
    plan.run(("tail", 1))
    edge_gain = jnp.zeros((cw, nres), F32)
    ge_copies = []
    for k in range(slots):
        cs = slice(k * nres, (k + 1) * nres)
        unit, scaling = normalize(e1[k].astype(F32), 0)
        grad = gen[:, cs]
        edge_gain = edge_gain + grad * unit
        gen[:, cs] = cot[k].astype(F32) + norm_back(grad, unit, scaling, egain, 0)
        copy = pltpu.make_async_copy(gen.at[:, cs], ge_hbm.at[k], os_.at[1 + k])
        copy.start()
        ge_copies.append(copy)
    plan.run(("tail", 2))
    ids = lax.broadcasted_iota(jnp.int32, (nres, cap), 0)
    total = gta[:nres, :]
    for i in range(groups):
        if i:
            ret_copies[i - 1].wait_recv()
            rows = ret[i]
        else:
            rows = gtab[home, :]
        chosen = jnp.where(ids == sid[asked[i]], 1.0, 0.0).astype(BF)
        total = total + nn(chosen, rows)
    unit_full, scale_full = normalize(xf[...].astype(F32), 1)
    for c in range(parts):
        gsend[c] = total[:, c * part : (c + 1) * part].astype(BF)
    start(slice_copies)
    scaled = total * ngain_ref[...]
    lane = lax.broadcasted_iota(jnp.int32, (nres, 128), 1)
    both = jnp.where(
        lane == 0,
        jnp.sum(scaled, 1, keepdims=True),
        jnp.where(lane == 1, jnp.sum(scaled * unit_full, 1, keepdims=True), 0.0),
    )
    stat[0] = both.T[:8]
    start(stat_copies)
    vec[:, :dn] = jnp.sum(total * unit_full, 0, keepdims=True)
    vec[:, dn : 2 * dn] = fg[...]
    vec[:, 2 * dn :] = jnp.sum(edge_gain.T, 0, keepdims=True)
    start(vec_line)
    for c in range(parts):
        cs = slice(c * part, (c + 1) * part)
        uslice[c] = unit_full[:, cs]
        gslice[c] = ngain_ref[:, cs]
        mslice[c] = gm[:, cs]
    plan.run(("tail", 3))
    arrived(slice_copies + stat_copies)
    g_normed = gsend[h].astype(F32)
    sums = stat[0]
    for i in range(1, parts):
        g_normed = g_normed + gbuf[i].astype(F32)
        sums = sums + stat[i]
    sums = jnp.concatenate([sums, jnp.zeros((120, nres), F32)], axis=0).T * (1.0 / dn)
    gnode_ref[...] = mslice[h].astype(F32) + scale_full * (
        g_normed * gslice[h] - sums[:, 0:1] - uslice[h] * sums[:, 1:2]
    )
    arrived(vec_line)
    value = vec[...]
    for i in range(1, parts):
        value = value + vz[i]
    vp[0] = value
    start(vec_plane)
    for k in range(4, tail):
        plan.run(("tail", k))
    for name, landing, out_ref in (
        ("update", zu, owu_ref),
        ("neigh", zn, own_ref),
        ("edge", ze, owe_ref),
    ):
        total = chunk_own[name].held()[0].astype(F32)
        for i in range(1, parts):
            chunk_line[name, i].wait_recv()
            total = total + landing[i].astype(F32)
        out_ref[...] = total
    arrived(vec_plane)
    value = vp[0]
    for i in range(1, groups):
        value = value + vp[i]
    ovec_ref[...] = value
    arrived(nn_copies)
    e2_copy.wait()
    for copy in ge_copies:
        copy.wait()
    net.finish()


def layer(groups, parts, node, ncot, req, nbr, egain, counts, ngain, fgain, edges, ecot, weights):
    nres, part = node.shape
    dn = part * parts
    cap = req.shape[2]
    slots, cw, _ = edges.shape
    units = weights[0].shape[1]
    rows = slots * nres
    tabn = nres + groups * cap
    height = tabn + nres + 256
    rp = nres // parts
    levels = groups.bit_length() - 1
    wide, narrow = dn // groups, cw // groups
    total = 2 * dn + cw
    S, V = jax.ShapeDtypeStruct, pltpu.VMEM
    split = lambda lead, r: V((lead,) + (2,) * levels + (r, units), BF)

    def recv(lead, r):
        return [V((lead,) + (2,) * (levels - 1 - k) + (r, units), BF) for k in range(levels)]

    node_rows = lambda dtype: V((rp, dn), dtype)
    full_rows = lambda dtype: V((nres, dn), dtype)
    table = lambda dtype: V((tabn, dn), dtype)
    scratch = [
        V((parts, 3, units, dn), BF),
        V((parts, 1, units, 2 * cw), BF),
        V((parts, 2, units, dn), BF),
        V((parts, nres, part), BF),
        V((parts, nres, part), BF),
        full_rows(BF),
        full_rows(BF),
        node_rows(BF),
        node_rows(BF),
        full_rows(BF),
        V(req.shape, jnp.int32),
        V((groups, cap, dn), BF),
        V((groups, cap, dn), BF),
        table(BF),
        table(BF),
        V((dn, tabn), BF),
        V(edges.shape, BF),
        V(edges.shape, BF),
        V(edges.shape, BF),
        V((height, rows), BF),
        V((units, height), BF),
        V((cw, units), BF),
        V((cw, rows), F32),
        V((parts, units, nres), BF),
        full_rows(BF),
        full_rows(BF),
        V((parts, rp, dn), BF),
        V((parts, rp, dn), BF),
        V((256, rows), BF),
        V((2, units, rows), BF),
        V((parts, rp, part), BF),
        full_rows(BF),
        V((parts, rp, units), BF),
        V((parts, rp, units), BF),
        node_rows(BF),
        V((1, dn), F32),
        V((units, nres), F32),
        table(F32),
        table(BF),
        V((slots, 1, nres), jnp.int32),
        V((cw, nres), F32),
        V((parts, nres, units), BF),
        split(parts, wide),
        split(parts, narrow),
        split(parts, narrow),
        V((parts, nres, units), BF),
        V((parts, units, nres), BF),
        V((nres, units), BF),
        V((nres, units), BF),
        full_rows(BF),
        V((groups, cap, dn), BF),
        V((parts, nres, part), BF),
        V((parts, nres, part), BF),
        V((parts, 8, nres), F32),
        V((parts, nres, part), F32),
        V((parts, 1, part), F32),
        V((parts, nres, part), BF),
        V((1, total), F32),
        V((parts, 1, total), F32),
        V((groups, 1, total), F32),
        V((parts, wide, units), BF),
        V((parts, narrow, units), BF),
        V((parts, narrow, units), BF),
    ]
    for _ in range(parts):
        scratch += recv(1, wide) + recv(1, narrow) + recv(1, narrow)
    for _ in range(4):
        scratch += [split(1, wide)] + recv(1, wide)
    copies = (
        15 * (parts - 1)
        + 5 * (groups - 1)
        + 6 * (parts - 1) * (1 + levels)
        + (3 * parts + 4) * levels
        + 3 * (parts - 1)
    )
    scratch += [
        pltpu.SemaphoreType.DMA((copies,)),
        pltpu.SemaphoreType.DMA((copies,)),
        pltpu.SemaphoreType.DMA((9,)),
        pltpu.SemaphoreType.DMA((2,)),
        pltpu.SemaphoreType.DMA((1 + slots,)),
    ]
    vm = pl.BlockSpec(memory_space=pltpu.VMEM)
    hbm = pl.BlockSpec(memory_space=pltpu.MemorySpace.HBM)
    return pl.pallas_call(
        functools.partial(layer_kernel, groups, parts),
        in_specs=[vm] * 8 + [hbm] * 9,
        out_specs=[vm] * 10 + [hbm] * 3,
        out_shape=[
            S((nres, part), BF),
            S((nres, part), F32),
            S((wide, units), F32),
            S((wide, units), F32),
            S((narrow, units), F32),
            S((wide, units), F32),
            S((narrow, units), F32),
            S((wide, units), F32),
            S((wide, units), F32),
            S((1, total), F32),
            S(edges.shape, BF),
            S(edges.shape, F32),
            S((parts, units, rows), BF),
        ],
        scratch_shapes=scratch,
        compiler_params=pltpu.CompilerParams(
            collective_id=0, has_side_effects=True, vmem_limit_bytes=62 << 20
        ),
        name="layer",
    )(node, ncot, req, nbr, egain, counts, ngain, fgain, edges, ecot, *weights)


def publish_kernel(groups, sizes, *refs):
    count = (len(refs) - 7) // 3
    ins, vec_ref = refs[:count], refs[count]
    outs, gains = refs[count + 1 : 2 * count + 1], refs[2 * count + 1 : 2 * count + 4]
    stage, (table, sems, out_sems) = refs[2 * count + 4 : 3 * count + 4], refs[3 * count + 4 :]
    loads = [pltpu.make_async_copy(a, b, sems.at[k]) for k, (a, b) in enumerate(zip(ins, stage))]
    saves = [pltpu.make_async_copy(a, b, out_sems.at[k]) for k, (a, b) in enumerate(zip(stage, outs))]
    start(loads)
    begin = 0
    for size, out in zip(sizes, gains):
        each = size // groups
        for q in range(groups):
            table[q : q + 1, :each] = vec_ref[:, begin + q * each : begin + (q + 1) * each]
        begin += size
        out[...] = table[pl.ds(lax.axis_index("res"), 1), :each]
    for load, save in zip(loads, saves):
        load.wait()
        save.start()
    for save in saves:
        save.wait()


def publish(groups, sizes, arrays, vec):
    S = jax.ShapeDtypeStruct
    vm = pl.BlockSpec(memory_space=pltpu.VMEM)
    hbm = pl.BlockSpec(memory_space=pltpu.MemorySpace.HBM)
    return pl.pallas_call(
        functools.partial(publish_kernel, groups, sizes),
        in_specs=[hbm] * len(arrays) + [vm],
        out_specs=[hbm] * len(arrays) + [vm] * len(sizes),
        out_shape=[S(a.shape, a.dtype) for a in arrays]
        + [S((1, size // groups), F32) for size in sizes],
        scratch_shapes=[pltpu.VMEM(a.shape, a.dtype) for a in arrays]
        + [
            pltpu.VMEM((groups, 128), F32),
            pltpu.SemaphoreType.DMA((len(arrays),)),
            pltpu.SemaphoreType.DMA((len(arrays),)),
        ],
        compiler_params=pltpu.CompilerParams(vmem_limit_bytes=60 << 20),
        name="publish",
    )(*arrays, vec)


def per_device(
    node_state,
    edge_state,
    node_gain,
    edge_gain,
    ffn_gain,
    w_self,
    w_neigh,
    w_edge,
    w_message,
    w_update,
    w_expand,
    w_contract,
    neighbours,
    requests,
    counts,
    node_cotangent,
    edge_cotangent,
):
    groups, parts = lax.axis_size("res"), lax.axis_size("hid")
    nres, slot_part, cw = edge_state.shape
    ngain, egain, fgain = node_gain[None], edge_gain[None], ffn_gain[None]
    edges = edge_state.transpose(1, 2, 0)
    cot = edge_cotangent.transpose(1, 2, 0)
    node_two, gnode, gws, gwn, gwe, gwm, gwu, gwx, gwc, vec, e2, ge, _slopes = layer(
        groups,
        parts,
        node_state,
        node_cotangent,
        requests[0][:, None, :],
        neighbours.T,
        egain,
        counts[None],
        ngain,
        fgain,
        edges,
        cot,
        [w_neigh, w_self, w_edge, w_update.T, w_message, w_expand, w_contract],
    )
    dn = ngain.shape[1]
    node_two, gnode, gws, gwn, gwe, gwm, gwu, gwx, gwc, e2, ge, gng, gfg, geg = publish(
        groups, (dn, dn, cw), (node_two, gnode, gws, gwn, gwe, gwm, gwu, gwx, gwc, e2, ge), vec
    )
    return (
        node_two,
        e2.transpose(2, 0, 1),
        gnode,
        ge.transpose(2, 0, 1),
        gng[0],
        geg[0],
        gfg[0],
        gws,
        gwn,
        gwe,
        gwm.T,
        gwu.T,
        gwx,
        gwc.T,
    )


def solution(mesh):
    return jax.shard_map(
        per_device,
        mesh=mesh,
        in_specs=(
            P("res", "hid"),
            P("res", "hid", None),
            P(),
            P(),
            P(),
            P(None, "hid"),
            P(None, "hid"),
            P(None, "hid"),
            P("hid", None),
            P("hid", None),
            P(None, "hid"),
            P("hid", None),
            P("res", None),
            P("res", None, None),
            P("res"),
            P("res", "hid"),
            P("res", "hid", None),
        ),
        out_specs=(
            P("res", "hid"),
            P("res", "hid", None),
            P("res", "hid"),
            P("res", "hid", None),
            P("res"),
            P("res"),
            P("res"),
            P("res", "hid"),
            P("res", "hid"),
            P("res", "hid"),
            P("hid", "res"),
            P("hid", "res"),
            P("res", "hid"),
            P("hid", "res"),
        ),
        check_vma=False,
    )
```

```python
import functools

import jax
import jax.numpy as jnp
from jax import lax
from jax.experimental import pallas as pl
from jax.experimental.pallas import tpu as pltpu
from jax.sharding import PartitionSpec as P

F32, BF = jnp.float32, jnp.bfloat16
EPSILON = 1e-05
TANH_SCALE = 0.7978845608028654
TANH_CUBE = 0.044715
MESH = pl.DeviceIdType.MESH
GAP = 2
NEIGH, SELF, MESSAGE = range(3)
EXPAND, CONTRACT = range(2)


def contract(a, b, dim_a, dim_b):
    return lax.dot_general(
        a, b, (((dim_a,), (dim_b,)), ((), ())), preferred_element_type=F32
    )


def nn(a, b):
    return contract(a, b, 1, 0)


def nt(a, b):
    return contract(a, b, 1, 1)


def tn(a, b):
    return contract(a, b, 0, 0)


def normalize(values, axis):
    centred = values - jnp.mean(values, axis, keepdims=True)
    scaling = lax.rsqrt(jnp.mean(centred * centred, axis, keepdims=True) + EPSILON)
    return centred * scaling, scaling


def norm_back(grad, unit, scaling, gain, axis):
    scaled = grad * gain
    return scaling * (
        scaled
        - jnp.mean(scaled, axis, keepdims=True)
        - unit * jnp.mean(scaled * unit, axis, keepdims=True)
    )


def gelu(x):
    return (0.5 * x) * (1.0 + jnp.tanh(x * (TANH_SCALE + TANH_SCALE * TANH_CUBE * (x * x))))


def gelu_pair(x):
    square = x * x
    bent = jnp.tanh(x * (TANH_SCALE + TANH_SCALE * TANH_CUBE * square))
    half = 0.5 * x
    slope = 0.5 + 0.5 * bent + half * (1.0 - bent * bent) * (
        TANH_SCALE + 3 * TANH_SCALE * TANH_CUBE * square
    )
    return half + half * bent, slope


class Net:
    def __init__(self, send_sems, recv_sems):
        self.send_sems, self.recv_sems, self.count, self.sent = send_sems, recv_sems, 0, []

    def make(self, src, dst, device):
        k = self.count
        self.count += 1
        copy = pltpu.make_async_remote_copy(
            src_ref=src,
            dst_ref=dst,
            send_sem=self.send_sems.at[k],
            recv_sem=self.recv_sems.at[k],
            device_id=device,
            device_id_type=MESH,
        )
        self.sent.append(copy)
        return copy

    def push(self, src, dst, device):
        copy = self.make(src, dst, device)
        copy.start()
        return copy

    def finish(self):
        for copy in self.sent:
            copy.wait_send()


def start(copies):
    for copy in copies:
        copy.start()


def arrived(copies):
    for copy in copies:
        copy.wait_recv()


def flip_bit(index, bit):
    step = 1 << bit
    return index + step - 2 * step * ((index // step) % 2)


def greet(devices):
    barrier = pltpu.get_barrier_semaphore()
    for device in devices:
        pl.semaphore_signal(barrier, inc=1, device_id=device, device_id_type=MESH)


def greeted(devices):
    pl.semaphore_wait(pltpu.get_barrier_semaphore(), len(devices))


def place(groups, parts):
    p, h = lax.axis_index("res"), lax.axis_index("hid")
    line = [None] + [(p, lax.rem(h + i, parts)) for i in range(1, parts)]
    plane = [None] + [(lax.rem(p + i, groups), h) for i in range(1, groups)]
    return p, h, line, plane


class Rows:
    def __init__(self, net, p, groups, plane, nres, cap, tab_ref, rows_buf):
        self.mine = pl.ds(pl.multiple_of(nres + p * cap, 16), cap)
        self.asked = [lax.rem(p + i, groups) for i in range(groups)]
        self.nres, self.cap, self.tab, self.buf = nres, cap, tab_ref, rows_buf
        self.copies = [
            net.make(rows_buf.at[i], tab_ref.at[self.mine, :], plane[i]) for i in range(1, groups)
        ]

    def send(self, normed, sid_ref):
        ids = lax.broadcasted_iota(jnp.int32, (self.nres, self.cap), 0)
        self.tab[: self.nres, :] = normed
        for i, q in enumerate(self.asked):
            chosen = jnp.where(ids == sid_ref[q], 1.0, 0.0).astype(BF)
            rows = tn(chosen, normed).astype(BF)
            if i == 0:
                self.tab[self.mine, :] = rows
            else:
                self.buf[i] = rows
                self.copies[i - 1].start()


class Gather:
    def __init__(self, net, p, h, groups, parts, units, depth):
        self.levels = groups.bit_length() - 1
        low, half = p % 2, p // 2
        turned = sum(
            ((half // (1 << b)) % 2) * (1 << (self.levels - 2 - b)) for b in range(self.levels - 1)
        )
        starts = [low * (groups // 2) + half, low * (groups // 2) + turned]
        rows = depth // groups
        back = [(p, lax.rem(h + parts - i, parts)) for i in range(parts)]
        self.lag = 2 * (self.levels + 1)
        self.batches = []
        for u, (full, w, r) in enumerate(units):
            stages, turn = [], u % 2
            begin = starts[turn]
            own = pl.ds(pl.multiple_of(begin * rows, rows), rows)
            stages.append(net.make(full.at[0, w, own, :], full.at[r, w, own, :], back[r]))
            for level in range(self.levels):
                if level == self.levels - 1:
                    bit = 0
                else:
                    bit = 1 + (level if turn == 0 else self.levels - 2 - level)
                span = rows << level
                held = (begin // (1 << level)) * span
                view = full.at[r, w, pl.ds(pl.multiple_of(held, span), span), :]
                stages.append(net.make(view, view, (flip_bit(p, bit), h)))
            self.batches.append(stages)
        self.slots = len(units) + self.lag

    def turn(self, slot):
        for stage in range(self.levels + 1, -1, -1):
            b = slot - 2 * stage
            if 0 <= b < len(self.batches):
                if stage:
                    self.batches[b][stage - 1].wait_recv()
                if stage <= self.levels:
                    self.batches[b][stage].start()


def bits_of(index, levels):
    return tuple((index >> b) & 1 for b in range(levels - 1, -1, -1))


def fill_rows(ref, value, lead):
    levels = len(ref.shape) - 3
    rows = ref.shape[-2]
    for s in range(1 << levels):
        ref[(lead,) + bits_of(s, levels)] = value[s * rows : (s + 1) * rows, :]


class PlaneSum:
    def __init__(self, net, p, h, levels, order, source, recv, done):
        self.levels, self.source, self.recv, self.done = levels, source, recv, done
        own = [(p // (1 << bit)) % 2 for bit in range(levels)]
        self.fixed, self.copies = [], []
        fixed = {}
        for level in range(levels):
            bit = 0 if level == 0 else (level if order == 0 else levels - level)
            other = dict(fixed)
            other[bit] = 1 - own[bit]
            fixed = dict(fixed)
            fixed[bit] = own[bit]
            self.fixed.append(fixed)
            self.copies.append(
                net.make(source.at[self.index(other)], recv[level], (flip_bit(p, bit), h))
            )

    def index(self, fixed):
        return (slice(None),) + tuple(
            fixed.get(bit, slice(None)) for bit in range(self.levels - 1, -1, -1)
        )

    def held(self):
        return self.source.at[self.index(self.fixed[-1])]

    def steps(self):
        return [functools.partial(self.step, level) for level in range(self.levels + 1)]

    def step(self, level):
        if level:
            k = level - 1
            self.copies[k].wait_recv()
            free = [bit for bit in range(self.levels) if bit not in self.fixed[k]]
            for n in range(1 << len(free)):
                fixed = dict(self.fixed[k])
                for j, bit in enumerate(free):
                    fixed[bit] = (n >> j) & 1
                at = self.index(fixed)
                got = (slice(None),) + tuple(fixed[bit] for bit in reversed(free))
                total = self.source[at].astype(F32) + self.recv[k][got].astype(F32)
                if level == self.levels and self.done(total):
                    continue
                self.source[at] = total.astype(BF)
        if level < self.levels:
            self.copies[level].start()


def build_inputs(a_ref, edges, v_ref, egain, tabn):
    slots, cw, nres = edges.shape
    index = lax.broadcasted_iota(jnp.int32, (tabn, nres), 0)
    own = lax.broadcasted_iota(jnp.int32, (nres, nres), 0) == lax.broadcasted_iota(
        jnp.int32, (nres, nres), 1
    )
    own = jnp.where(own, 1.0, 0.0).astype(BF)
    height = a_ref.shape[0]

    def one(k, _):
        cs = pl.ds(pl.multiple_of(k * nres, nres), nres)
        a_ref[:tabn, cs] = jnp.where(index == v_ref[k], 1.0, 0.0).astype(BF)
        a_ref[tabn : tabn + nres, cs] = own
        unit, _scale = normalize(edges[k].astype(F32), 0)
        a_ref[tabn + nres : tabn + nres + cw, cs] = (unit * egain).astype(BF)
        a_ref[tabn + nres + cw :, cs] = jnp.zeros((height - tabn - nres - cw, nres), BF)
        return 0

    lax.fori_loop(0, slots, one, 0)


def edge_chunk(c, w_ref, pair_ref, tab, a_ref, bt, wut, v_ref, upd, mean, inverse, cw, pause, second=None):
    tabn, nres = tab.shape[0], mean.shape[-1]
    slots = a_ref.shape[1] // nres
    bt[:, :tabn] = nt(w_ref[c, NEIGH], tab[...]).astype(BF)
    bt[:, tabn : tabn + nres] = nt(w_ref[c, SELF], tab[:nres, :]).astype(BF)
    bt[:, tabn + nres :] = pair_ref[c, 0, :, :256]
    wut[...] = pair_ref[c, 0, :, 2 * cw - 256 :].T[256 - cw :]
    pause(0)
    before = nn(bt[...], a_ref[...])
    pause(1)
    square = before * before
    gate = 0.5 + 0.5 * jnp.tanh(before * (TANH_SCALE + TANH_SCALE * TANH_CUBE * square))
    if second is not None:
        dg, gup, gwu = second
        bend = (2 * TANH_SCALE + 6 * TANH_SCALE * TANH_CUBE * square) * (1.0 - gate)
    total, kept = None, []
    for k in range(slots):
        cs = slice(k * nres, (k + 1) * nres)
        open_gate = gate[:, cs] * (v_ref[k] >= 0).astype(F32)
        part = before[:, cs] * open_gate
        total = part if total is None else total + part
        kept.append(part.astype(BF))
        if second is not None:
            dg[:, cs] = (open_gate + part * bend[:, cs]).astype(BF)
    mean[c] = (total * inverse).astype(BF)
    kept = jnp.concatenate(kept, axis=1)
    upd[...] += nn(wut[...], kept)
    if second is not None:
        fill_rows(gwu, nt(gup[256 - cw :, :], kept).astype(BF), c)


def message_part(w_ref, mean, parts):
    total = None
    for c in range(parts):
        term = tn(mean[c], w_ref[c, MESSAGE])
        total = term if total is None else total + term
    return total.astype(BF)


def add_update(edges, upd, out):
    slots, _, nres = edges.shape
    for k in range(slots):
        out[k] = (edges[k].astype(F32) + upd[:, k * nres : (k + 1) * nres]).astype(BF)


class Plan:
    def __init__(self):
        self.points, self.active, self.now = {}, [], 0

    def add(self, point, steps):
        steps = list(steps)
        self.note(point, steps.pop(0))
        if steps:
            self.active.append([self.now, steps])

    def note(self, point, step):
        self.points.setdefault(point, []).append(step)

    def advance(self, point, gap=1):
        self.now += 1
        for item in self.active:
            if self.now - item[0] >= gap:
                self.note(point, item[1].pop(0))
                item[0] = self.now
        self.active = [item for item in self.active if item[1]]

    def run(self, point):
        for step in self.points.get(point, ()):
            step()


def plane_scratch(groups, lead, rows, units, order, last):
    recv, acc = [], []
    count = groups
    while count > 1:
        count //= 2
        recv.append(pltpu.VMEM((lead, count, rows, units), BF))
        if count == 1:
            acc.append(pltpu.VMEM((lead, rows, units), last))
        elif order == 0:
            acc.append(pltpu.VMEM((lead, count // 2, 2, rows, units), BF))
        else:
            acc.append(pltpu.VMEM((lead, 2, count // 2, rows, units), BF))
    return recv + acc


def layer_kernel(groups, parts, *refs):
    (node_ref, ncot_ref, req_ref, nbr_ref, egain_ref, count_ref, ngain_ref, fgain_ref) = refs[:8]
    (edges_hbm, ecot_hbm, wn_hbm, ws_hbm, we_hbm, wu_hbm, wm_hbm, wx_hbm, wc_hbm) = refs[8:17]
    (nn_ref, gnode_ref, ows_ref, own_ref, owe_ref, owm_ref, owu_ref, owx_ref, owc_ref, ovec_ref) = refs[17:27]
    (e2_hbm, ge_hbm, dg_hbm) = refs[27:30]
    refs = list(refs[30:])

    def take(count):
        taken = refs[:count]
        del refs[:count]
        return taken

    w_ref, pair_ref, wf_ref, nbuf, cbuf, nfull, cf, xrows, x1, xf, sid = take(11)
    rows0, rows1, tab0, tab1, tabt, edges, e1, cot, a_ref, bt = take(10)
    wut, upd, mean, msg0, msg1, mbuf0, mbuf1, gup, dgbuf = take(9)
    nsp, gm, act, gex, fi, fg, gt, gta, gtab = take(9)
    v_ref, ecol = take(2)
    gown, first_n, first_e, gwu, zown, zmean, actf, gexf, fif, ret = take(10)
    gsend, gbuf, stat, uslice, gslice, mslice, vec, vz, vp, zn, ze, zu = take(12)
    ss, rs, ls, ds, os_ = refs[-5:]
    p, h, line, plane = place(groups, parts)
    nres, part = node_ref.shape
    dn = part * parts
    cap = req_ref.shape[2]
    slots, cw, _ = edges.shape
    rp = nres // parts
    units = w_ref.shape[2]
    tabn = tab0.shape[0]
    levels = groups.bit_length() - 1
    mine = pl.ds(pl.multiple_of(h * rp, rp), rp)
    home = pl.ds(pl.multiple_of(nres + p * cap, 16), cap)
    asked = [lax.rem(p + groups - i, groups) for i in range(groups)]
    inverse = 1.0 / count_ref[...].astype(F32)

    raw = [a_ref.at[:dn, k * units : (k + 1) * units] for k in range(3)]
    raw_e = [a_ref.at[dn + k * cw : dn + (k + 1) * cw, :units] for k in range(2)]
    loads = [
        pltpu.make_async_copy(src, dst, ls.at[k])
        for k, (src, dst) in enumerate(
            (
                (wn_hbm, raw[0]),
                (we_hbm, raw_e[0]),
                (wu_hbm, raw_e[1]),
                (ws_hbm, raw[1]),
                (wx_hbm, raw[2]),
                (edges_hbm, edges),
                (wm_hbm, w_ref.at[0, MESSAGE]),
                (wc_hbm, wf_ref.at[0, CONTRACT]),
                (ecot_hbm, cot),
            )
        )
    ]
    start(loads)
    net = Net(ss, rs)

    def to_parts(pair):
        copies = []
        for i in range(1, parts):
            src, dst = pair(i, lax.rem(h + i, parts))
            copies.append(net.make(src, dst, line[i]))
        return copies

    def rows_of(other):
        return pl.ds(pl.multiple_of(other * rp, rp), rp)

    node_copies = to_parts(lambda i, o: (node_ref, nbuf.at[h]))
    req_copies = [
        net.make(req_ref.at[lax.rem(p + i, groups)], sid.at[p], plane[i]) for i in range(1, groups)
    ]
    ncot_copies = to_parts(lambda i, o: (ncot_ref, cbuf.at[h]))
    rows_first = Rows(net, p, groups, plane, nres, cap, tab0, rows0)
    rows_next = Rows(net, p, groups, plane, nres, cap, tab1, rows1)
    message0 = to_parts(lambda i, o: (msg0.at[rows_of(o), :], mbuf0.at[i]))
    message1 = to_parts(lambda i, o: (msg1.at[rows_of(o), :], mbuf1.at[i]))
    x1_copies = to_parts(lambda i, o: (x1, xf.at[mine, :]))
    edge_units = []
    for r in range(1, parts):
        edge_units += [(w_ref, NEIGH, r), (pair_ref, 0, r), (w_ref, SELF, r)]
    edge_units += [(w_ref, MESSAGE, r) for r in range(1, parts)]
    node_units = [(wf_ref, w, r) for w in (EXPAND, CONTRACT) for r in range(1, parts)]
    gather = Gather(net, p, h, groups, parts, edge_units + node_units, units)
    chunk_slots = [0] + [3 * k - 1 + gather.lag for k in range(1, parts)]
    message_slot, expand_slot = ((3 + k) * (parts - 1) - 1 + gather.lag for k in (1, 2))
    gm_copies = to_parts(lambda i, o: (gm.at[mine, :], gm.at[mine, :]))
    nn_copies = to_parts(lambda i, o: (nsp.at[o], nn_ref.at[mine, :]))
    ret_copies = [
        net.make(
            gtab.at[pl.ds(pl.multiple_of(nres + lax.rem(p + i, groups) * cap, 16), cap), :],
            ret.at[i],
            plane[i],
        )
        for i in range(1, groups)
    ]
    own_copies = to_parts(lambda i, o: (gown.at[i], zown.at[i]))
    mean_copies = to_parts(lambda i, o: (mean.at[i], zmean.at[i]))
    act_copies = to_parts(lambda i, o: (act.at[i], actf.at[mine, :]))
    gex_copies = to_parts(lambda i, o: (gex.at[i], gexf.at[mine, :]))
    fi_copies = to_parts(lambda i, o: (fi, fif.at[mine, :]))
    slice_copies = to_parts(lambda i, o: (gsend.at[o], gbuf.at[i]))
    stat_copies = to_parts(lambda i, o: (stat.at[0], stat.at[i]))
    vec_line = to_parts(lambda i, o: (vec, vz.at[i]))
    vec_plane = [net.make(vp.at[0], vp.at[i], plane[i]) for i in range(1, groups)]

    chunk_sums, chunk_line, chunk_own = {}, {}, {}
    for c in range(parts):
        for name, source, order, landing in (
            ("neigh", first_n, 0, zn),
            ("edge", first_e, 1, ze),
            ("update", gwu, c % 2, zu),
        ):
            recv = take(levels)
            item = PlaneSum(
                net, p, h, levels, order, source.at[pl.ds(c, 1)], recv, lambda total: False
            )
            steps = item.steps()
            if c:
                copy = net.make(item.held().at[0], landing.at[c], line[c])
                chunk_line[name, c] = copy
                last = steps.pop()

                def send_on(last=last, copy=copy):
                    last()
                    copy.start()

                steps.append(send_on)
            else:
                chunk_own[name] = item
            chunk_sums[name, c] = steps
    def unit_sum(order, out):
        source = take(1)[0]

        def done(total):
            out[...] = total[0]
            return True

        item = PlaneSum(net, p, h, levels, order, source, take(levels), done)

        def fill(value):
            fill_rows(source, value.astype(BF), 0)

        return fill, item.steps()

    fill_self, steps_self = unit_sum(0, ows_ref)
    fill_message, steps_message = unit_sum(1, owm_ref)
    fill_expand, steps_expand = unit_sum(0, owx_ref)
    fill_contract, steps_contract = unit_sum(1, owc_ref)

    peers = line[1:] + plane[1:]
    greet(peers)
    nbuf[h] = node_ref[...]
    cbuf[h] = ncot_ref[...]
    sid[p] = req_ref[p]
    loads[0].wait()
    w_ref[0, NEIGH] = raw[0][...].T
    greeted(peers)
    start(node_copies)
    start(req_copies)
    gather.turn(0)
    loads[1].wait()
    loads[2].wait()
    pair_ref[0, 0] = a_ref[dn : dn + 2 * cw, :units].T
    gather.turn(1)
    counts = count_ref[...]
    for k in range(slots):
        row = nbr_ref[pl.ds(h * slots + k, 1), :]
        v_ref[k] = jnp.where(h * slots + k < counts, row, -1)
    ecol[...] = jnp.broadcast_to(egain_ref[...], (nres, cw)).T
    arrived(node_copies)
    for c in range(parts):
        nfull[:, c * part : (c + 1) * part] = nbuf[c]
    unit_node, _scale = normalize(nfull[...].astype(F32), 1)
    normed = (unit_node * ngain_ref[...]).astype(BF)
    xrows[...] = nfull[mine, :]
    arrived(req_copies)
    rows_first.send(normed, sid)
    start(ncot_copies)
    loads[3].wait()
    w_ref[0, SELF] = raw[1][...].T
    gather.turn(2)
    loads[4].wait()
    wf_ref[0, EXPAND] = raw[2][...].T
    gather.turn(3)
    loads[5].wait()
    egain = ecol[...]
    build_inputs(a_ref, edges, v_ref, egain, tabn)
    gather.turn(4)
    loads[6].wait()
    loads[7].wait()
    arrived(ncot_copies)
    for c in range(parts):
        cf[:, c * part : (c + 1) * part] = cbuf[c]
    upd[...] = jnp.zeros_like(upd)
    gather.turn(5)
    first_slot = 6
    arrived(rows_first.copies)

    slot = first_slot
    turns_at = {}
    for k in range(parts):
        upto = max(slot + (k == 0), chunk_slots[k] + 1)
        turns_at["begin", k] = range(slot, min(upto, gather.slots))
        turns_at[0, k] = range(upto, min(upto + 1, gather.slots))
        turns_at[1, k] = range(upto + 1, min(upto + 2, gather.slots))
        slot = min(upto + 2, gather.slots)

    def turns(c, at):
        for k in range(parts):
            if len(turns_at[at, k]):

                @pl.when(c == k)
                def _():
                    for s in turns_at[at, k]:
                        gather.turn(s)

    def first_chunk(c, _):
        turns(c, "begin")
        pause = lambda at: turns(c, at)
        edge_chunk(c, w_ref, pair_ref, tab0, a_ref, bt, wut, v_ref, upd, mean, inverse, cw, pause)
        return 0

    lax.fori_loop(0, parts, first_chunk, 0)
    for s in range(slot, message_slot + 1):
        gather.turn(s)
    slot = max(slot, message_slot + 1)
    msg0[...] = message_part(w_ref, mean, parts)
    start(message0)
    if slot < gather.slots:
        gather.turn(slot)
        slot += 1
    add_update(edges, upd, e1)
    build_inputs(a_ref, e1, v_ref, egain, tabn)
    middle = xrows[...].astype(F32) + msg0[mine, :].astype(F32)
    for i, copy in enumerate(message0):
        copy.wait_recv()
        middle = middle + mbuf0[i + 1].astype(F32)
    unit_ffn, _scale = normalize(middle, 1)
    ffn_input = (unit_ffn * fgain_ref[...]).astype(BF)
    for s in range(slot, expand_slot + 1):
        gather.turn(s)
    slot = max(slot, expand_slot + 1)
    hidden = [gelu(nt(ffn_input, wf_ref[c, EXPAND])).astype(BF) for c in range(parts)]
    for s in range(slot, gather.slots):
        gather.turn(s)
    out = middle
    for c in range(parts):
        out = out + nn(hidden[c], wf_ref[c, CONTRACT])
    out = out.astype(BF)
    upd[...] = jnp.zeros_like(upd)
    x1[...] = out
    xf[mine, :] = out
    start(x1_copies)
    loads[8].wait()
    gup[: 256 - cw, :] = jnp.zeros((256 - cw, slots * nres), BF)
    for k in range(slots):
        live = (v_ref[k] >= 0).astype(F32)
        gup[256 - cw :, k * nres : (k + 1) * nres] = (cot[k].astype(F32) * live).astype(BF)
    arrived(x1_copies)
    unit_full, _scale = normalize(xf[...].astype(F32), 1)
    rows_next.send((unit_full * ngain_ref[...]).astype(BF), sid)
    arrived(rows_next.copies)

    def ffn_sums():
        arrived(act_copies + gex_copies + fi_copies)
        fill_expand(tn(fif[...], gexf[...]))
        fill_contract(tn(cf[...], actf[...]))

    def message_sums():
        value = mean[0].astype(F32)
        arrived(mean_copies)
        for i in range(1, parts):
            value = value + zmean[i].astype(F32)
        fill_message(tn(gm[...], value.astype(BF).T))

    plan = Plan()
    for i in range(parts):
        plan.advance(("second", i))
        c = (i + 1) % parts
        if c:
            plan.note(("second", i), mean_copies[c - 1].start)
        plan.add(("second", i), chunk_sums["update", c])
    for name in ("node", "ffn"):
        plan.advance((name, 0))
    for i in range(parts):
        plan.advance(("early", i), GAP)
        if i == min(1, parts - 1):
            plan.note(("early", i), ffn_sums)
            plan.add(("early", i), steps_expand)
            plan.add(("early", i), steps_contract)
        c = (i + 1) % parts
        if c:
            plan.note(("late", i), own_copies[c - 1].start)
        plan.advance(("late", i), GAP)
        if c:
            for name in ("neigh", "edge"):
                plan.add(("late", i), chunk_sums[name, c])
        if i == 0:
            plan.note(("late", i), message_sums)
            plan.add(("late", i), steps_message)
    plan.advance(("tail", 0))
    for name in ("neigh", "edge"):
        plan.add(("tail", 0), chunk_sums[name, 0])
    plan.add(("tail", 1), steps_self)
    tail = 2
    while plan.active:
        plan.advance(("tail", tail))
        tail += 1

    def points(i, name):
        for k in range(parts):
            if (name, k) in plan.points:

                @pl.when(i == k)
                def _():
                    plan.run((name, k))

    def save(i):
        return pltpu.make_async_copy(dgbuf.at[i % 2], dg_hbm.at[lax.rem(i + 1, parts)], ds.at[i % 2])

    def second_chunk(i, _):
        @pl.when(i >= 2)
        def _():
            save(i - 2).wait()

        edge_chunk(
            lax.rem(i + 1, parts),
            w_ref,
            pair_ref,
            tab1,
            a_ref,
            bt,
            wut,
            v_ref,
            upd,
            mean,
            inverse,
            cw,
            lambda at: None,
            (dgbuf.at[i % 2], gup, gwu),
        )
        save(i).start()
        points(i, "second")
        return 0

    lax.fori_loop(0, parts, second_chunk, 0)
    msg1[...] = message_part(w_ref, mean, parts)
    start(message1)
    plan.run(("node", 0))
    add_update(e1, upd, edges)
    e2_copy = pltpu.make_async_copy(edges, e2_hbm, os_.at[0])
    e2_copy.start()
    tabt[...] = tab1[...].T
    middle = x1[...].astype(F32) + msg1[mine, :].astype(F32)
    for i, copy in enumerate(message1):
        copy.wait_recv()
        middle = middle + mbuf1[i + 1].astype(F32)
    unit_ffn, scaling = normalize(middle, 1)
    ffn_input = (unit_ffn * fgain_ref[...]).astype(BF)
    fi[...] = ffn_input
    cotangent = cf[mine, :]
    g_input = jnp.zeros((rp, dn), F32)
    for c in range(parts):
        active, slope = gelu_pair(nt(ffn_input, wf_ref[c, EXPAND]))
        act[c] = active.astype(BF)
        g_expand = (nt(cotangent, wf_ref[c, CONTRACT]) * slope).astype(BF)
        gex[c] = g_expand
        g_input = g_input + nn(g_expand, wf_ref[c, EXPAND])
    g_middle = cotangent.astype(F32) + norm_back(g_input, unit_ffn, scaling, fgain_ref[...], 1)
    gm[mine, :] = g_middle.astype(BF)
    start(gm_copies)
    fg[...] = jnp.sum(g_input * unit_ffn, 0, keepdims=True)
    out = middle
    for c in range(parts):
        out = out + nn(act[c], wf_ref[c, CONTRACT])
    out = out.astype(BF)
    for c in range(parts):
        nsp[c] = out[:, c * part : (c + 1) * part]
    start(nn_copies)
    nn_ref[mine, :] = nsp[h]
    actf[mine, :] = act[0]
    gexf[mine, :] = gex[0]
    fif[mine, :] = fi[...]
    upd[...] = jnp.zeros_like(upd)
    gta[...] = jnp.zeros_like(gta)
    for c in range(max(parts - 2, 0), parts):
        save(c).wait()
    arrived(gm_copies)
    start(act_copies)
    start(gex_copies)
    start(fi_copies)
    plan.run(("ffn", 0))

    def fetch(i):
        return pltpu.make_async_copy(dg_hbm.at[lax.rem(i + 1, parts)], dgbuf.at[i % 2], ds.at[i % 2])

    fetch(0).start()
    gen = upd

    def back_chunk(i, _):
        c = lax.rem(i + 1, parts)

        @pl.when(i + 1 < parts)
        def _():
            fetch(i + 1).start()

        gt[...] = nt(w_ref[c, MESSAGE], gm[...]) * inverse
        wut[...] = pair_ref[c, 0, :, :256].T[:cw]
        fetch(i).wait()
        buf = dgbuf.at[i % 2]
        grad = nn(pair_ref[c, 0, :, 2 * cw - 256 :], gup[...])
        grad = grad + jnp.concatenate([gt[...]] * slots, axis=1)
        grad = (grad * buf[...].astype(F32)).astype(BF)
        buf[...] = grad
        gen[...] += nn(wut[...], grad)
        points(i, "early")
        total = nt(a_ref[: tabn + nres + cw, :], buf[...])
        gp = total[:tabn].astype(BF)
        go = total[tabn : tabn + nres].astype(BF)
        gown[c] = go
        gta[...] += nn(gp, w_ref[c, NEIGH])
        gta[:nres, :] += nn(go, w_ref[c, SELF])

        @pl.when(i == parts - 1)
        def _():
            gtab[...] = gta[...].astype(BF)
            start(ret_copies)

        fill_rows(first_e, total[tabn + nres :].astype(BF), c)
        fill_rows(first_n, nn(tabt[...], gp).astype(BF), c)
        points(i, "late")
        return 0

    lax.fori_loop(0, parts, back_chunk, 0)
    plan.run(("tail", 0))
    value = gown[0].astype(F32)
    arrived(own_copies)
    for i in range(1, parts):
        value = value + zown[i].astype(F32)
    fill_self(tn(tab1[:nres, :], value.astype(BF)))
    plan.run(("tail", 1))
    edge_gain = jnp.zeros((cw, nres), F32)
    ge_copies = []
    for k in range(slots):
        cs = slice(k * nres, (k + 1) * nres)
        unit, scaling = normalize(e1[k].astype(F32), 0)
        grad = gen[:, cs]
        edge_gain = edge_gain + grad * unit
        gen[:, cs] = cot[k].astype(F32) + norm_back(grad, unit, scaling, egain, 0)
        copy = pltpu.make_async_copy(gen.at[:, cs], ge_hbm.at[k], os_.at[1 + k])
        copy.start()
        ge_copies.append(copy)
    plan.run(("tail", 2))
    ids = lax.broadcasted_iota(jnp.int32, (nres, cap), 0)
    total = gta[:nres, :]
    for i in range(groups):
        if i:
            ret_copies[i - 1].wait_recv()
            rows = ret[i]
        else:
            rows = gtab[home, :]
        chosen = jnp.where(ids == sid[asked[i]], 1.0, 0.0).astype(BF)
        total = total + nn(chosen, rows)
    unit_full, scale_full = normalize(xf[...].astype(F32), 1)
    for c in range(parts):
        gsend[c] = total[:, c * part : (c + 1) * part].astype(BF)
    start(slice_copies)
    scaled = total * ngain_ref[...]
    lane = lax.broadcasted_iota(jnp.int32, (nres, 128), 1)
    both = jnp.where(
        lane == 0,
        jnp.sum(scaled, 1, keepdims=True),
        jnp.where(lane == 1, jnp.sum(scaled * unit_full, 1, keepdims=True), 0.0),
    )
    stat[0] = both.T[:8]
    start(stat_copies)
    vec[:, :dn] = jnp.sum(total * unit_full, 0, keepdims=True)
    vec[:, dn : 2 * dn] = fg[...]
    vec[:, 2 * dn :] = jnp.sum(edge_gain.T, 0, keepdims=True)
    start(vec_line)
    for c in range(parts):
        cs = slice(c * part, (c + 1) * part)
        uslice[c] = unit_full[:, cs]
        gslice[c] = ngain_ref[:, cs]
        mslice[c] = gm[:, cs]
    plan.run(("tail", 3))
    arrived(slice_copies + stat_copies)
    g_normed = gsend[h].astype(F32)
    sums = stat[0]
    for i in range(1, parts):
        g_normed = g_normed + gbuf[i].astype(F32)
        sums = sums + stat[i]
    sums = jnp.concatenate([sums, jnp.zeros((120, nres), F32)], axis=0).T * (1.0 / dn)
    gnode_ref[...] = mslice[h].astype(F32) + scale_full * (
        g_normed * gslice[h] - sums[:, 0:1] - uslice[h] * sums[:, 1:2]
    )
    arrived(vec_line)
    value = vec[...]
    for i in range(1, parts):
        value = value + vz[i]
    vp[0] = value
    start(vec_plane)
    for k in range(4, tail):
        plan.run(("tail", k))
    for name, landing, out_ref in (
        ("update", zu, owu_ref),
        ("neigh", zn, own_ref),
        ("edge", ze, owe_ref),
    ):
        total = chunk_own[name].held()[0].astype(F32)
        for i in range(1, parts):
            chunk_line[name, i].wait_recv()
            total = total + landing[i].astype(F32)
        out_ref[...] = total
    arrived(vec_plane)
    value = vp[0]
    for i in range(1, groups):
        value = value + vp[i]
    ovec_ref[...] = value
    arrived(nn_copies)
    e2_copy.wait()
    for copy in ge_copies:
        copy.wait()
    net.finish()


def layer(groups, parts, node, ncot, req, nbr, egain, counts, ngain, fgain, edges, ecot, weights):
    nres, part = node.shape
    dn = part * parts
    cap = req.shape[2]
    slots, cw, _ = edges.shape
    units = weights[0].shape[1]
    rows = slots * nres
    tabn = nres + groups * cap
    height = tabn + nres + 256
    rp = nres // parts
    levels = groups.bit_length() - 1
    wide, narrow = dn // groups, cw // groups
    total = 2 * dn + cw
    S, V = jax.ShapeDtypeStruct, pltpu.VMEM
    split = lambda lead, r: V((lead,) + (2,) * levels + (r, units), BF)

    def recv(lead, r):
        return [V((lead,) + (2,) * (levels - 1 - k) + (r, units), BF) for k in range(levels)]

    node_rows = lambda dtype: V((rp, dn), dtype)
    full_rows = lambda dtype: V((nres, dn), dtype)
    table = lambda dtype: V((tabn, dn), dtype)
    scratch = [
        V((parts, 3, units, dn), BF),
        V((parts, 1, units, 2 * cw), BF),
        V((parts, 2, units, dn), BF),
        V((parts, nres, part), BF),
        V((parts, nres, part), BF),
        full_rows(BF),
        full_rows(BF),
        node_rows(BF),
        node_rows(BF),
        full_rows(BF),
        V(req.shape, jnp.int32),
        V((groups, cap, dn), BF),
        V((groups, cap, dn), BF),
        table(BF),
        table(BF),
        V((dn, tabn), BF),
        V(edges.shape, BF),
        V(edges.shape, BF),
        V(edges.shape, BF),
        V((height, rows), BF),
        V((units, height), BF),
        V((cw, units), BF),
        V((cw, rows), F32),
        V((parts, units, nres), BF),
        full_rows(BF),
        full_rows(BF),
        V((parts, rp, dn), BF),
        V((parts, rp, dn), BF),
        V((256, rows), BF),
        V((2, units, rows), BF),
        V((parts, rp, part), BF),
        full_rows(BF),
        V((parts, rp, units), BF),
        V((parts, rp, units), BF),
        node_rows(BF),
        V((1, dn), F32),
        V((units, nres), F32),
        table(F32),
        table(BF),
        V((slots, 1, nres), jnp.int32),
        V((cw, nres), F32),
        V((parts, nres, units), BF),
        split(parts, wide),
        split(parts, narrow),
        split(parts, narrow),
        V((parts, nres, units), BF),
        V((parts, units, nres), BF),
        V((nres, units), BF),
        V((nres, units), BF),
        full_rows(BF),
        V((groups, cap, dn), BF),
        V((parts, nres, part), BF),
        V((parts, nres, part), BF),
        V((parts, 8, nres), F32),
        V((parts, nres, part), F32),
        V((parts, 1, part), F32),
        V((parts, nres, part), BF),
        V((1, total), F32),
        V((parts, 1, total), F32),
        V((groups, 1, total), F32),
        V((parts, wide, units), BF),
        V((parts, narrow, units), BF),
        V((parts, narrow, units), BF),
    ]
    for _ in range(parts):
        scratch += recv(1, wide) + recv(1, narrow) + recv(1, narrow)
    for _ in range(4):
        scratch += [split(1, wide)] + recv(1, wide)
    copies = (
        15 * (parts - 1)
        + 5 * (groups - 1)
        + 6 * (parts - 1) * (1 + levels)
        + (3 * parts + 4) * levels
        + 3 * (parts - 1)
    )
    scratch += [
        pltpu.SemaphoreType.DMA((copies,)),
        pltpu.SemaphoreType.DMA((copies,)),
        pltpu.SemaphoreType.DMA((9,)),
        pltpu.SemaphoreType.DMA((2,)),
        pltpu.SemaphoreType.DMA((1 + slots,)),
    ]
    vm = pl.BlockSpec(memory_space=pltpu.VMEM)
    hbm = pl.BlockSpec(memory_space=pltpu.MemorySpace.HBM)
    return pl.pallas_call(
        functools.partial(layer_kernel, groups, parts),
        in_specs=[vm] * 8 + [hbm] * 9,
        out_specs=[vm] * 10 + [hbm] * 3,
        out_shape=[
            S((nres, part), BF),
            S((nres, part), F32),
            S((wide, units), F32),
            S((wide, units), F32),
            S((narrow, units), F32),
            S((wide, units), F32),
            S((narrow, units), F32),
            S((wide, units), F32),
            S((wide, units), F32),
            S((1, total), F32),
            S(edges.shape, BF),
            S(edges.shape, F32),
            S((parts, units, rows), BF),
        ],
        scratch_shapes=scratch,
        compiler_params=pltpu.CompilerParams(
            collective_id=0, has_side_effects=True, vmem_limit_bytes=62 << 20
        ),
        name="layer",
    )(node, ncot, req, nbr, egain, counts, ngain, fgain, edges, ecot, *weights)


def pieces(shape):
    return 4 if len(shape) == 3 else 1


def publish_kernel(groups, sizes, *refs):
    count = (len(refs) - 7) // 3
    ins, vec_ref = refs[:count], refs[count]
    outs, gains = refs[count + 1 : 2 * count + 1], refs[2 * count + 1 : 2 * count + 4]
    stage, (table, sems, out_sems) = refs[2 * count + 4 : 3 * count + 4], refs[3 * count + 4 :]
    loads, saves = [], []
    for k in sorted(range(count), key=lambda k: -len(ins[k].shape)):
        step = ins[k].shape[0] // pieces(ins[k].shape)
        for first in range(0, ins[k].shape[0], step):
            at, n = pl.ds(first, step), len(loads)
            loads.append(pltpu.make_async_copy(ins[k].at[at], stage[k].at[at], sems.at[n]))
            saves.append(pltpu.make_async_copy(stage[k].at[at], outs[k].at[at], out_sems.at[n]))
    start(loads)
    begin = 0
    for size, out in zip(sizes, gains):
        each = size // groups
        for q in range(groups):
            table[q : q + 1, :each] = vec_ref[:, begin + q * each : begin + (q + 1) * each]
        begin += size
        out[...] = table[pl.ds(lax.axis_index("res"), 1), :each]
    for load, save in zip(loads, saves):
        load.wait()
        save.start()
    for save in saves:
        save.wait()


def publish(groups, sizes, arrays, vec):
    S = jax.ShapeDtypeStruct
    vm = pl.BlockSpec(memory_space=pltpu.VMEM)
    hbm = pl.BlockSpec(memory_space=pltpu.MemorySpace.HBM)
    return pl.pallas_call(
        functools.partial(publish_kernel, groups, sizes),
        in_specs=[hbm] * len(arrays) + [vm],
        out_specs=[hbm] * len(arrays) + [vm] * len(sizes),
        out_shape=[S(a.shape, a.dtype) for a in arrays]
        + [S((1, size // groups), F32) for size in sizes],
        scratch_shapes=[pltpu.VMEM(a.shape, a.dtype) for a in arrays]
        + [
            pltpu.VMEM((groups, 128), F32),
            pltpu.SemaphoreType.DMA((sum(pieces(a.shape) for a in arrays),)),
            pltpu.SemaphoreType.DMA((sum(pieces(a.shape) for a in arrays),)),
        ],
        compiler_params=pltpu.CompilerParams(vmem_limit_bytes=60 << 20),
        name="publish",
    )(*arrays, vec)


def per_device(
    node_state,
    edge_state,
    node_gain,
    edge_gain,
    ffn_gain,
    w_self,
    w_neigh,
    w_edge,
    w_message,
    w_update,
    w_expand,
    w_contract,
    neighbours,
    requests,
    counts,
    node_cotangent,
    edge_cotangent,
):
    groups, parts = lax.axis_size("res"), lax.axis_size("hid")
    nres, slot_part, cw = edge_state.shape
    ngain, egain, fgain = node_gain[None], edge_gain[None], ffn_gain[None]
    edges = edge_state.transpose(1, 2, 0)
    cot = edge_cotangent.transpose(1, 2, 0)
    node_two, gnode, gws, gwn, gwe, gwm, gwu, gwx, gwc, vec, e2, ge, _slopes = layer(
        groups,
        parts,
        node_state,
        node_cotangent,
        requests[0][:, None, :],
        neighbours.T,
        egain,
        counts[None],
        ngain,
        fgain,
        edges,
        cot,
        [w_neigh, w_self, w_edge, w_update.T, w_message, w_expand, w_contract],
    )
    dn = ngain.shape[1]
    node_two, gnode, gws, gwn, gwe, gwm, gwu, gwx, gwc, e2, ge, gng, gfg, geg = publish(
        groups, (dn, dn, cw), (node_two, gnode, gws, gwn, gwe, gwm, gwu, gwx, gwc, e2, ge), vec
    )
    return (
        node_two,
        e2.transpose(2, 0, 1),
        gnode,
        ge.transpose(2, 0, 1),
        gng[0],
        geg[0],
        gfg[0],
        gws,
        gwn,
        gwe,
        gwm.T,
        gwu.T,
        gwx,
        gwc.T,
    )


def solution(mesh):
    return jax.shard_map(
        per_device,
        mesh=mesh,
        in_specs=(
            P("res", "hid"),
            P("res", "hid", None),
            P(),
            P(),
            P(),
            P(None, "hid"),
            P(None, "hid"),
            P(None, "hid"),
            P("hid", None),
            P("hid", None),
            P(None, "hid"),
            P("hid", None),
            P("res", None),
            P("res", None, None),
            P("res"),
            P("res", "hid"),
            P("res", "hid", None),
        ),
        out_specs=(
            P("res", "hid"),
            P("res", "hid", None),
            P("res", "hid"),
            P("res", "hid", None),
            P("res"),
            P("res"),
            P("res"),
            P("res", "hid"),
            P("res", "hid"),
            P("res", "hid"),
            P("hid", "res"),
            P("hid", "res"),
            P("res", "hid"),
            P("hid", "res"),
        ),
        check_vma=False,
    )
```
